32 devices in a mesh: gx: 4 (over z), gy: 4 (over y, core), ma: 2 (over x).
Axes of the slice: x: 2, y: 2, z: 4, core: 2. Of those that a mesh axis runs over, the one named last changes fastest.
Arguments:
- mode_fields: bfloat16 [3, 128, 64, 512], P(None, 'ma', 'gx', 'gy'), may hold values from -6 to 6
- cell_volumes: float32 [64, 512], P('gx', 'gy'), may hold values from 0.25 to 4
Outputs:
- convection: float32 [128, 128, 128], P(('gx', 'gy'), 'ma')
The draws below stay inside these ranges and needn't reach their ends.
All inputs are finite; a program needn't handle non-finite values.
Results may differ from the reference program's by a relative error of at most 0.0051.
Values may be sent and summed in bfloat16 or wider, within the bound.
No kernel may reach another device: no remote copies, remote signals or barrier semaphores. Data moves between devices by JAX's collectives and lax.ppermute only.
A program may use at most 128 MiB of HBM per device.

```python
import math
import jax
import jax.numpy as jnp
from jax import lax

M = 128
NX = 64
NY = 512


def with_spikes(array, stream_key, source, target, shards_of, factor):
    def block_of(position):
        return (jnp.arange(array.shape[position]) // (array.shape[position] // shards_of)).reshape((-1,) + (1,) * (array.ndim - 1 - position))

    one_side = jax.random.permutation(stream_key, shards_of)[block_of(target)]
    other_side = (block_of(target) + shards_of // 2) % shards_of
    return jnp.where((block_of(source) == one_side) | (block_of(source) == other_side), factor * array, array)


def shard_levels(own_key, dims, cuts, smallest, largest):
    def one(axis_at, blocks):
        heights = jax.random.uniform(jax.random.fold_in(jax.random.fold_in(own_key, 6), axis_at), (blocks,), jnp.float32, smallest / len(cuts), largest / len(cuts))
        return jnp.repeat(jnp.exp(heights), dims[axis_at] // blocks).reshape((-1,) + (1,) * (len(dims) - axis_at - 1))

    gain = one(*cuts[0])
    for cut in cuts[1:]:
        gain = gain * one(*cut)
    return gain


def gaussian_with(stream_key, extent, spread, most, pieces, heavy, held_as=jnp.bfloat16):
    result = spread * jax.random.normal(stream_key, extent, jnp.float32)
    if pieces:
        result = result * shard_levels(stream_key, extent, pieces, -0.22, 0.18)
    return jnp.clip(with_spikes(result, jax.random.fold_in(stream_key, 3), *heavy), -most, most).astype(held_as)


def setup_inputs(seed: int = 0) -> dict:
    key_list = jax.random.split(jax.random.key(seed), 3)
    mode_fields = gaussian_with(key_list[0], (3, M, NX, NY), 1.0, 6.0, ((1, 2), (2, 4), (3, 4)), (2, 1, 4, 2.0))
    cell_volumes = jnp.clip(jnp.exp(math.log(4.0) - 2.7725887 * jax.random.uniform(key_list[1], (NX, NY), jnp.float32) ** shard_levels(key_list[1], (NX, NY), ((0, 4), (1, 4)), -0.2, 0.2)), 0.25, 4.0)
    return {"mode_fields": mode_fields, "cell_volumes": cell_volumes}


def central_slopes(mode_fields):
    widened = jnp.pad(mode_fields.astype(jnp.float32), ((0, 0), (0, 0), (1, 1), (1, 1)))
    along_first = (widened[:, :, 2:, 1:-1] - widened[:, :, :-2, 1:-1]) * 0.5
    along_second = (widened[:, :, 1:-1, 2:] - widened[:, :, 1:-1, :-2]) * 0.5
    return jnp.concatenate([along_first, along_second], 0).astype(jnp.bfloat16)

def rows_tensor(values, own_modes, slopes, weights):
    mode_count = values.shape[1]
    pair_width = own_modes.shape[1]
    cell_count = values.shape[3]
    weighted = (weights[None, None] * values.astype(jnp.float32)).astype(jnp.bfloat16)
    left_rows = jnp.transpose(weighted, (2, 1, 0, 3))
    own_rows = jnp.transpose(own_modes, (2, 0, 1, 3))
    slope_rows = jnp.transpose(slopes.reshape(2, 3, mode_count, slopes.shape[2], cell_count), (3, 0, 2, 1, 4))
    block_size = min(32, pair_width)

    def advance(running, row_data):
        left_row, own_row, slope_row = row_data
        flattened = left_row.reshape(mode_count, 3 * cell_count)
        slope_float = slope_row.astype(jnp.float32)
        results = []
        for offset in range(0, pair_width, block_size):
            selected = own_row[:, offset:offset + block_size].astype(jnp.float32)
            pairing = (selected[0][:, None, None, :] * slope_float[0][None] + selected[1][:, None, None, :] * slope_float[1][None]).astype(jnp.bfloat16)
            products = lax.dot_general(flattened, pairing.reshape(block_size * mode_count, 3 * cell_count), (((1,), (1,)), ((), ())), preferred_element_type=jnp.float32)
            results.append(products.reshape(mode_count, block_size, mode_count))
        return (running + jnp.concatenate(results, 1), None)
    zero_start = jnp.zeros((mode_count, pair_width, mode_count), jnp.float32)
    running, _ = lax.scan(advance, zero_start, (left_rows, own_rows, slope_rows))
    return running

def reference(mode_fields, cell_volumes):
    slopes = central_slopes(mode_fields)
    weights = cell_volumes * (1.0 / math.sqrt(NX * NY))
    return rows_tensor(mode_fields, mode_fields[0:2], slopes, weights)
```

```python
import functools
import math

import jax
import jax.numpy as jnp
from jax import lax
from jax.experimental import pallas as pl
from jax.experimental.pallas import tpu as pltpu
from jax.sharding import PartitionSpec as P

BF16 = jnp.bfloat16
F32 = jnp.float32


def bits_of(count):
    return count.bit_length() - 1


def send_order(mesh_sizes):
    order = []
    for axis in ("gy", "gx"):
        order += [(axis, bit) for bit in range(bits_of(mesh_sizes[axis]))]
    return order


def source_bits(mesh_sizes, rows_each):
    row_bits = bits_of(rows_each)
    base = {"gy": row_bits, "gx": row_bits + bits_of(mesh_sizes["gy"])}
    found = list(range(row_bits))
    for axis, bit in reversed(send_order(mesh_sizes)):
        found.append(base[axis] + bit)
    return found


def tensor_kernel(own_ref, other_ref, slope_ref, weight_ref, out_ref, left, right, *, bits, block, rows_each):
    row_count, _, share, cells = own_ref.shape
    step = pl.program_id(0)
    gy_count = lax.axis_size("gy")
    top = bits_of(2 * share) - 1

    @pl.when(step == 0)
    def _():
        for x in range(row_count):
            weight = weight_ref[pl.ds(x, 1), :]
            for half, ref in enumerate((own_ref, other_ref)):
                for a in range(3):
                    value = (weight * ref[x, a].astype(F32)).astype(BF16)
                    left[x, a, half * share : (half + 1) * share, :] = value.astype(F32)
            for b in range(2):
                both = jnp.concatenate([own_ref[x, b], other_ref[x, b]], 0)
                right[(2 * x + b) * cells : (2 * x + b + 1) * cells, :] = both.T

    here = (lax.axis_index("gx") * gy_count + lax.axis_index("gy")) * rows_each
    here = here ^ (lax.axis_index("ma") << top)
    start = here
    position = step * block
    for place, bit in enumerate(bits):
        start = start ^ (((position >> place) & 1) << bit)
    columns = []
    for x in range(row_count):
        slopes = [slope_ref[x, n] for n in range(6)]
        sums = [[], []]
        for row in range(block):
            offset = 0
            for place, bit in enumerate(bits):
                offset |= ((row >> place) & 1) << bit
            test = [
                jnp.concatenate(
                    [left[x, a, pl.ds(start ^ offset, 16, stride=0), :].astype(BF16)] * (share // 16), 0
                )
                for a in range(3)
            ]
            for b in range(2):
                sums[b].append(
                    test[0] * slopes[3 * b] + test[1] * slopes[3 * b + 1] + test[2] * slopes[3 * b + 2]
                )
        columns += [jnp.concatenate(sums[0], 0), jnp.concatenate(sums[1], 0)]
    sums = jnp.concatenate(columns, 1)
    out_ref[...] = jnp.dot(sums, right[...], preferred_element_type=F32).reshape(out_ref.shape)


def partial_tensor(own, other, slopes, weights, mesh_sizes, rows_each):
    row_count, _, share, cells = own.shape
    block = 8
    body = functools.partial(
        tensor_kernel, bits=source_bits(mesh_sizes, rows_each), block=block, rows_each=rows_each
    )
    whole = lambda array: pl.BlockSpec(array.shape, lambda g: (0,) * array.ndim, pipeline_mode=pl.Buffered(1))
    modes = 2 * share
    return pl.pallas_call(
        body,
        grid=(modes // block,),
        out_shape=jax.ShapeDtypeStruct((modes, share, modes), F32),
        in_specs=[whole(own), whole(other), whole(slopes), whole(weights)],
        out_specs=pl.BlockSpec((block, share, modes), lambda g: (g, 0, 0)),
        scratch_shapes=[
            pltpu.VMEM((row_count, 3, modes, cells), F32),
            pltpu.VMEM((row_count * 2 * cells, modes), BF16),
        ],
        compiler_params=pltpu.CompilerParams(vmem_limit_bytes=58 << 20),
        cost_estimate=pl.CostEstimate(
            flops=4 * modes * share * modes * row_count * cells, bytes_accessed=8 << 20, transcendentals=0
        ),
    )(own, other, slopes, weights)


def neighbours(axis):
    count = lax.axis_size(axis)
    forward = [(i, i + 1) for i in range(count - 1)]
    return forward, [(target, source) for source, target in forward]


def shards(mode_fields, cell_volumes, mesh_sizes):
    total_cells = (
        cell_volumes.shape[0] * mesh_sizes["gx"] * cell_volumes.shape[1] * mesh_sizes["gy"]
    )
    weights = cell_volumes * (1.0 / math.sqrt(total_cells))
    own = jnp.transpose(mode_fields, (2, 0, 1, 3))
    swap = [(0, 1), (1, 0)]
    share = own.shape[2]
    rows_each = 2 * share // (mesh_sizes["gx"] * mesh_sizes["gy"])

    forward, backward = neighbours("gx")
    above = lax.ppermute(own[-1:], "gx", forward)
    below = lax.ppermute(own[:1], "gx", backward)
    forward, backward = neighbours("gy")
    before = lax.ppermute(own[:, :, :, -1], "gy", forward)
    after = lax.ppermute(own[:, :, :, 0], "gy", backward)
    other = lax.ppermute(own, "ma", swap)

    tall = jnp.concatenate([above, own, below], 0).astype(F32)
    along_first = (tall[2:] - tall[:-2]) * 0.5
    wide = jnp.concatenate([before[..., None], own, after[..., None]], 3).astype(F32)
    along_second = (wide[..., 2:] - wide[..., :-2]) * 0.5
    slopes = jnp.concatenate([along_first, along_second], 1).astype(BF16)

    partial = partial_tensor(own, other, slopes, weights, mesh_sizes, rows_each)
    for axis, bit in send_order(mesh_sizes):
        pairs = [(i, i ^ (1 << bit)) for i in range(mesh_sizes[axis])]
        half = partial.shape[0] // 2
        arrived = lax.ppermute(partial[half:].astype(BF16), axis, pairs)
        partial = partial[:half] + arrived.astype(F32)
    partial = jnp.transpose(partial, (0, 2, 1))
    arrived = lax.ppermute(partial[:, share:], "ma", swap)
    kept = partial[:, :share]
    first = lax.axis_index("ma") == 0
    return jnp.concatenate([jnp.where(first, kept, arrived), jnp.where(first, arrived, kept)], 2)


def solution(mesh):
    in_specs = (P(None, "ma", "gx", "gy"), P("gx", "gy"))
    out_specs = P(("gx", "gy"), "ma", None)
    body = functools.partial(shards, mesh_sizes=dict(mesh.shape))
    return jax.shard_map(body, mesh=mesh, in_specs=in_specs, out_specs=out_specs, check_vma=False)
```

```python
import functools
import math

import jax
import jax.numpy as jnp
from jax import lax
from jax.experimental import pallas as pl
from jax.experimental.pallas import tpu as pltpu
from jax.sharding import PartitionSpec as P

BF16 = jnp.bfloat16
F32 = jnp.float32


def bits_of(count):
    return count.bit_length() - 1


def send_order(mesh_sizes):
    order = []
    for axis in ("gy", "gx"):
        order += [(axis, bit) for bit in range(bits_of(mesh_sizes[axis]))]
    return order


def source_bits(mesh_sizes, rows_each, chunks):
    row_bits = bits_of(rows_each)
    base = {"gy": row_bits, "gx": row_bits + bits_of(mesh_sizes["gy"])}
    inner = row_bits - bits_of(chunks)
    found = list(range(inner))
    for axis, bit in reversed(send_order(mesh_sizes)):
        found.append(base[axis] + bit)
    return found + list(range(inner, row_bits))


def tensor_kernel(*refs, bits, block, rows_each, first_step, split):
    own_ref, other_ref, slope_ref, weight_ref = refs[:4]
    refs = refs[4:]
    before_ref = None
    if first_step is not None:
        before_ref, refs = refs[0], refs[1:]
    if split:
        keep_ref, send_ref, left, right = refs
    else:
        keep_ref, left, right = refs
    row_count, _, share, cells = own_ref.shape
    step = pl.program_id(0)
    top = bits_of(2 * share) - 1

    @pl.when(step == 0)
    def _():
        for x in range(row_count):
            weight = weight_ref[pl.ds(x, 1), :]
            for half, ref in enumerate((own_ref, other_ref)):
                for a in range(3):
                    value = (weight * ref[x, a].astype(F32)).astype(BF16)
                    left[x, a, half * share : (half + 1) * share, :] = value.astype(F32)
                for b in range(2):
                    right[
                        half * share : (half + 1) * share, (2 * x + b) * cells : (2 * x + b + 1) * cells
                    ] = ref[x, b]

    here = (lax.axis_index("gx") * lax.axis_size("gy") + lax.axis_index("gy")) * rows_each
    start = here ^ (lax.axis_index("ma") << top)
    if split:
        steps = pl.num_programs(0)
        position = (first_step + lax.rem(step + steps // 2, steps)) * block
    else:
        position = step * block
    for place, bit in enumerate(bits):
        start = start ^ (((position >> place) & 1) << bit)
    columns = []
    for x in range(row_count):
        slopes = [slope_ref[x, n] for n in range(6)]
        sums = [[], []]
        for row in range(block):
            offset = 0
            for place, bit in enumerate(bits):
                offset |= ((row >> place) & 1) << bit
            test = [
                jnp.concatenate(
                    [left[x, a, pl.ds(start ^ offset, 16, stride=0), :].astype(BF16)] * (share // 16), 0
                )
                for a in range(3)
            ]
            for b in range(2):
                sums[b].append(
                    test[0] * slopes[3 * b] + test[1] * slopes[3 * b + 1] + test[2] * slopes[3 * b + 2]
                )
        columns += [jnp.concatenate(sums[0], 0), jnp.concatenate(sums[1], 0)]
    sums = jnp.concatenate(columns, 1)
    product = lax.dot_general(sums, right[...], (((1,), (1,)), ((), ())), preferred_element_type=F32)
    product = product.reshape(block, share, 2 * share)
    if before_ref is not None:
        product = product + before_ref[...]
    if not split:
        keep_ref[...] = product
    else:
        half = pl.num_programs(0) // 2

        @pl.when(step < half)
        def _():
            send_ref[...] = product.astype(BF16)

        @pl.when(step >= half)
        def _():
            keep_ref[...] = product


def partial_tensor(own, other, slopes, weights, mesh_sizes, rows_each, chunks, chunk=None, before=None):
    row_count, _, share, cells = own.shape
    modes = 2 * share
    block = 16
    split = chunk is not None
    count = modes // chunks if split else modes
    steps = count // block
    half = steps // 2
    first_step = chunk * steps if split else None
    body = functools.partial(
        tensor_kernel,
        bits=source_bits(mesh_sizes, rows_each, chunks),
        block=block,
        rows_each=rows_each,
        first_step=first_step,
        split=split,
    )
    whole = lambda array: pl.BlockSpec(array.shape, lambda g: (0,) * array.ndim, pipeline_mode=pl.Buffered(1))
    shape = (block, share, modes)
    place = lambda g: (g + half) % steps
    operands = [own, other, slopes, weights]
    in_specs = [whole(array) for array in operands]
    if split:
        operands.append(before)
        in_specs.append(pl.BlockSpec(shape, lambda g: (first_step + place(g), 0, 0)))
        out_shape = (
            jax.ShapeDtypeStruct((count // 2, share, modes), F32),
            jax.ShapeDtypeStruct((count // 2, share, modes), BF16),
        )
        out_specs = (
            pl.BlockSpec(shape, lambda g: (jnp.maximum(g - half, 0), 0, 0)),
            pl.BlockSpec(shape, lambda g: (jnp.minimum(g, half - 1), 0, 0)),
        )
    else:
        out_shape = jax.ShapeDtypeStruct((count, share, modes), F32)
        out_specs = pl.BlockSpec(shape, lambda g: (g, 0, 0))
    return pl.pallas_call(
        body,
        grid=(steps,),
        out_shape=out_shape,
        in_specs=in_specs,
        out_specs=out_specs,
        scratch_shapes=[
            pltpu.VMEM((row_count, 3, modes, cells), F32),
            pltpu.VMEM((modes, row_count * 2 * cells), BF16),
        ],
        compiler_params=pltpu.CompilerParams(vmem_limit_bytes=40 << 20),
        cost_estimate=pl.CostEstimate(
            flops=8 * count * share * modes * row_count * cells, bytes_accessed=8 << 20, transcendentals=0
        ),
    )(*operands)


def neighbours(axis):
    count = lax.axis_size(axis)
    forward = [(i, i + 1) for i in range(count - 1)]
    return forward, [(target, source) for source, target in forward]


def halve(kept, sent, mesh_sizes):
    for axis, bit in send_order(mesh_sizes):
        pairs = [(i, i ^ (1 << bit)) for i in range(mesh_sizes[axis])]
        arrived = lax.ppermute(sent, axis, pairs)
        half = kept.shape[0] // 2
        if (axis, bit) != send_order(mesh_sizes)[-1]:
            sent = (kept[half:] + arrived[half:].astype(F32)).astype(BF16)
            kept = kept[:half] + arrived[:half].astype(F32)
        else:
            kept = kept + arrived.astype(F32)
    return kept


def shards(mode_fields, cell_volumes, mesh_sizes):
    total_cells = (
        cell_volumes.shape[0] * mesh_sizes["gx"] * cell_volumes.shape[1] * mesh_sizes["gy"]
    )
    weights = cell_volumes * (1.0 / math.sqrt(total_cells))
    own = jnp.transpose(mode_fields, (2, 0, 1, 3))
    swap = [(0, 1), (1, 0)]
    row_count, _, share, _ = own.shape
    rows_each = 2 * share // (mesh_sizes["gx"] * mesh_sizes["gy"])
    chunks = 2 if rows_each > 1 else 1
    quarter = row_count // 4

    def inner_rows(array):
        return array[quarter : 3 * quarter]

    def outer_rows(array):
        return jnp.concatenate([array[:quarter], array[3 * quarter :]], 0)

    own_inner, own_outer = inner_rows(own), outer_rows(own)
    other_inner = lax.ppermute(own_inner, "ma", swap)
    forward, backward = neighbours("gy")
    before = lax.ppermute(own[:, :, :, -1], "gy", forward)
    after = lax.ppermute(own[:, :, :, 0], "gy", backward)
    forward, backward = neighbours("gx")
    above = lax.ppermute(own[-1:], "gx", forward)
    below = lax.ppermute(own[:1], "gx", backward)
    own_outer_held, other_inner = lax.optimization_barrier((own_outer, other_inner))
    other_outer = lax.ppermute(own_outer_held, "ma", swap)

    def along_second(rows):
        wide = jnp.concatenate([rows(before)[..., None], rows(own), rows(after)[..., None]], 3).astype(F32)
        return (wide[..., 2:] - wide[..., :-2]) * 0.5

    tall = own[quarter - 1 : 3 * quarter + 1].astype(F32)
    slopes_inner = jnp.concatenate([(tall[2:] - tall[:-2]) * 0.5, along_second(inner_rows)], 1).astype(BF16)
    upper = jnp.concatenate([above, own[: quarter + 1]], 0).astype(F32)
    lower = jnp.concatenate([own[3 * quarter - 1 :], below], 0).astype(F32)
    tall = jnp.concatenate([upper[2:] - upper[:-2], lower[2:] - lower[:-2]], 0) * 0.5
    slopes_outer = jnp.concatenate([tall, along_second(outer_rows)], 1).astype(BF16)

    inner = partial_tensor(
        own_inner, other_inner, slopes_inner, inner_rows(weights), mesh_sizes, rows_each, chunks
    )
    results = []
    first = lax.axis_index("ma") == 0
    for chunk in range(chunks):
        kept, sent = partial_tensor(
            own_outer, other_outer, slopes_outer, outer_rows(weights), mesh_sizes, rows_each, chunks, chunk, inner
        )
        summed = halve(kept, sent, mesh_sizes)
        summed = jnp.transpose(summed, (0, 2, 1))
        arrived = lax.ppermute(summed[:, share:], "ma", swap)
        kept = summed[:, :share]
        results.append(jnp.concatenate([jnp.where(first, kept, arrived), jnp.where(first, arrived, kept)], 2))
    return jnp.concatenate(results, 0)


def solution(mesh):
    in_specs = (P(None, "ma", "gx", "gy"), P("gx", "gy"))
    out_specs = P(("gx", "gy"), "ma", None)
    body = functools.partial(shards, mesh_sizes=dict(mesh.shape))
    return jax.shard_map(body, mesh=mesh, in_specs=in_specs, out_specs=out_specs, check_vma=False)
```

```python
import functools
import math

import jax
import jax.numpy as jnp
from jax import lax
from jax.experimental import pallas as pl
from jax.experimental.pallas import tpu as pltpu
from jax.sharding import PartitionSpec as P

BF16 = jnp.bfloat16
F32 = jnp.float32


def bits_of(count):
    return count.bit_length() - 1


def send_order(sizes):
    order = []
    for axis in ("gy", "gx"):
        order += [(axis, bit) for bit in range(bits_of(sizes[axis]))]
    return order


def source_bits(sizes, rows_each, chunks):
    row_bits = bits_of(rows_each)
    base = {"gy": row_bits, "gx": row_bits + bits_of(sizes["gy"])}
    inner = row_bits - bits_of(chunks)
    found = list(range(inner))
    for axis, bit in reversed(send_order(sizes)):
        found.append(base[axis] + bit)
    return found + list(range(inner, row_bits))


def slopes_kernel(own_ref, before_ref, after_ref, *refs, rows):
    out_ref = refs[-1]
    last = own_ref.shape[0] - 1
    before = before_ref[...].astype(F32).T
    after = after_ref[...].astype(F32).T
    cells = own_ref.shape[3]
    lane = lax.broadcasted_iota(jnp.int32, own_ref.shape[2:], 1)
    for place, x in enumerate(rows):
        for a in range(3):
            down = (refs[0][0, a] if x == 0 else own_ref[x - 1, a]).astype(F32)
            up = (refs[1][0, a] if x == last else own_ref[x + 1, a]).astype(F32)
            out_ref[place, a] = ((up - down) * 0.5).astype(BF16)
            value = own_ref[x, a].astype(F32)
            column = 3 * x + a
            down = jnp.where(lane == 0, before[:, column : column + 1], pltpu.roll(value, 1, 1))
            up = jnp.where(lane == cells - 1, after[:, column : column + 1], pltpu.roll(value, cells - 1, 1))
            out_ref[place, 3 + a] = ((up - down) * 0.5).astype(BF16)


def slopes_of(own, before, after, rows, token, edges):
    row_count, _, share, cells = own.shape
    return pl.pallas_call(
        functools.partial(slopes_kernel, rows=rows),
        out_shape=jax.ShapeDtypeStruct((len(rows), 6, share, cells), BF16),
        in_specs=[pl.BlockSpec(memory_space=pltpu.VMEM)] * (4 + len(edges)),
        out_specs=pl.BlockSpec(memory_space=pltpu.VMEM),
        compiler_params=pltpu.CompilerParams(vmem_limit_bytes=16 << 20),
        cost_estimate=pl.CostEstimate(flops=1, bytes_accessed=1024, transcendentals=0),
    )(own, before.reshape(3 * row_count, share), after.reshape(3 * row_count, share), *edges, token)


def chunks_of(rows_each):
    return 2 if rows_each > 1 else 1


def tensor_kernel(*refs, bits, block, rows_each, first_step):
    own_ref, other_ref, slope_ref, weight_ref = refs[:4]
    before_ref = refs[4] if len(refs) == 8 else None
    out_ref, left, right = refs[-3:]
    row_count, _, share, cells = own_ref.shape
    step = pl.program_id(0)
    top = bits_of(2 * share) - 1

    @pl.when(step == 0)
    def _():
        for x in range(row_count):
            weight = weight_ref[pl.ds(x, 1), :]
            for half, ref in enumerate((own_ref, other_ref)):
                for a in range(3):
                    value = (weight * ref[x, a].astype(F32)).astype(BF16)
                    left[x, a, half * share : (half + 1) * share, :] = value.astype(F32)
                for b in range(2):
                    right[
                        half * share : (half + 1) * share, (2 * x + b) * cells : (2 * x + b + 1) * cells
                    ] = ref[x, b]

    here = (lax.axis_index("gx") * lax.axis_size("gy") + lax.axis_index("gy")) * rows_each
    start = here ^ (lax.axis_index("ma") << top)
    position = (first_step + step) * block
    for place, bit in enumerate(bits):
        start = start ^ (((position >> place) & 1) << bit)
    columns = []
    for x in range(row_count):
        slopes = [slope_ref[x, n] for n in range(6)]
        sums = [[], []]
        for row in range(block):
            offset = 0
            for place, bit in enumerate(bits):
                offset |= ((row >> place) & 1) << bit
            test = [
                jnp.concatenate(
                    [left[x, a, pl.ds(start ^ offset, 16, stride=0), :].astype(BF16)] * (share // 16), 0
                )
                for a in range(3)
            ]
            for b in range(2):
                sums[b].append(
                    test[0] * slopes[3 * b] + test[1] * slopes[3 * b + 1] + test[2] * slopes[3 * b + 2]
                )
        columns += [jnp.concatenate(sums[0], 0), jnp.concatenate(sums[1], 0)]
    sums = jnp.concatenate(columns, 1)
    product = lax.dot_general(sums, right[...], (((1,), (1,)), ((), ())), preferred_element_type=F32)
    product = product.reshape(block, share, 2 * share)
    if before_ref is not None:
        product = product + before_ref[...]
    out_ref[...] = product.astype(out_ref.dtype)


def partial_tensor(own, other, slopes, weights, sizes, positions, before=None, dtype=F32):
    row_count, _, share, cells = own.shape
    modes = 2 * share
    low, high = positions
    block = min(16, high - low)
    first_step = low // block
    rows_each = modes // (sizes["gx"] * sizes["gy"])
    body = functools.partial(
        tensor_kernel,
        bits=source_bits(sizes, rows_each, chunks_of(rows_each)),
        block=block,
        rows_each=rows_each,
        first_step=first_step,
    )
    whole = lambda array: pl.BlockSpec(array.shape, lambda g: (0,) * array.ndim, pipeline_mode=pl.Buffered(1))
    shape = (block, share, modes)
    operands = [own, other, slopes, weights]
    in_specs = [whole(array) for array in operands]
    if before is not None:
        operands.append(before)
        in_specs.append(pl.BlockSpec(shape, lambda g: (first_step + g, 0, 0)))
    return pl.pallas_call(
        body,
        grid=((high - low) // block,),
        out_shape=jax.ShapeDtypeStruct((high - low, share, modes), dtype),
        in_specs=in_specs,
        out_specs=pl.BlockSpec(shape, lambda g: (g, 0, 0)),
        scratch_shapes=[
            pltpu.VMEM((row_count, 3, modes, cells), F32),
            pltpu.VMEM((modes, row_count * 2 * cells), BF16),
        ],
        compiler_params=pltpu.CompilerParams(vmem_limit_bytes=20 << 20),
        cost_estimate=pl.CostEstimate(
            flops=8 * (high - low) * share * modes * row_count * cells, bytes_accessed=4 << 20, transcendentals=0
        ),
    )(*operands)


def neighbours(axis):
    count = lax.axis_size(axis)
    forward = [(i, i + 1) for i in range(count - 1)]
    return forward, [(target, source) for source, target in forward]


def flip(array, flips, sizes):
    axes = tuple(sorted({axis for axis, _ in flips}, key=("gx", "gy", "ma").index))
    strides = {}
    count = 1
    for axis in reversed(axes):
        strides[axis] = count
        count *= sizes[axis]
    change = 0
    for axis, bit in flips:
        change |= strides[axis] << bit
    return lax.ppermute(array, axes, [(i, i ^ change) for i in range(count)])


def subsets(stage):
    for code in range(1, 1 << len(stage)):
        yield code, [stage[n] for n in range(len(stage)) if (code >> (len(stage) - 1 - n)) & 1]


def stages_of(sizes, last):
    order = send_order(sizes)
    stages = [[order[0]]]
    rest = order[1:]
    if last:
        stages.append(rest[:2])
        rest = rest[2:]
    stages += [[entry] for entry in rest]
    return stages


def pieces_sum(kept, arrived, low, high):
    total = kept[low:high].astype(F32)
    for array in arrived:
        total = total + array[low:high].astype(F32)
    return total


def halve_stages(kept, arrived, stages, sizes):
    for stage in stages[:-1]:
        parts = 1 << len(stage)
        length = kept.shape[0] // parts
        received = []
        for code, flips in reversed(list(subsets(stage))):
            sent = pieces_sum(kept, arrived, code * length, (code + 1) * length).astype(BF16)
            received.append(flip(sent, flips, sizes))
        kept, arrived = pieces_sum(kept, arrived, 0, length), received
    return kept, arrived


def finish(kept, arrived, stage, sizes, share):
    total = pieces_sum(kept, arrived, 0, kept.shape[0])
    count = total.shape[0]
    pair = 2 if count % 4 == 0 else 1
    total = jnp.transpose(total.reshape(count // pair, pair * share, 2 * share), (0, 2, 1))
    length = count // pair // 2
    pieces = {}
    stage = stage + [("ma", 0)]
    for code, flips in reversed(list(subsets(stage))):
        above, swapped = code >> 1, code & 1
        sent = total[above * length : (above + 1) * length, swapped * share : (swapped + 1) * share]
        pieces[code] = flip(sent.astype(BF16), flips, sizes).astype(F32)
    mine = total[:length, :share] + pieces[2]
    theirs = pieces[1] + pieces[3]
    first = lax.axis_index("ma") == 0
    rows = []
    for part in range(pair):
        lanes = slice(part * share, (part + 1) * share)
        one, two = mine[:, :, lanes], theirs[:, :, lanes]
        rows.append(jnp.concatenate([jnp.where(first, one, two), jnp.where(first, two, one)], 2))
    return jnp.stack(rows, 1).reshape(count // 2, share, 2 * share)


def shards(mode_fields, cell_volumes, sizes):
    total_cells = cell_volumes.shape[0] * sizes["gx"] * cell_volumes.shape[1] * sizes["gy"]
    weights = cell_volumes * (1.0 / math.sqrt(total_cells))
    barrier = lax.optimization_barrier
    own = jnp.transpose(mode_fields, (2, 0, 1, 3))
    row_count, _, share, _ = own.shape
    modes = 2 * share
    quarter = row_count // 4

    def inner_rows(array):
        return array[quarter : 3 * quarter]

    def outer_rows(array):
        return jnp.concatenate([array[:quarter], array[3 * quarter :]], 0)

    own_inner, own_outer = inner_rows(own), outer_rows(own)
    other_inner = flip(own_inner, [("ma", 0)], sizes)
    forward, backward = neighbours("gy")
    before = lax.ppermute(own[:, :, :, -1], "gy", forward)
    after = lax.ppermute(own[:, :, :, 0], "gy", backward)
    forward, backward = neighbours("gx")
    held, before, after = barrier((own, before, after))
    above = lax.ppermute(held[-1:], "gx", forward)
    below = lax.ppermute(held[:1], "gx", backward)
    token = other_inner[:1, 0, :8] + other_inner[1:2, 0, :8]
    own_outer_held, above, below = barrier((own_outer, above, below))
    other_outer = flip(own_outer_held, [("ma", 0)], sizes)
    all_rows = tuple(range(row_count))
    slopes_inner = slopes_of(own, before, after, all_rows[quarter : 3 * quarter], token, [])
    slopes_outer = slopes_of(
        own, before, after, all_rows[:quarter] + all_rows[3 * quarter :], token, [above, below]
    )

    inner = partial_tensor(own_inner, other_inner, slopes_inner, inner_rows(weights), sizes, (0, modes))
    outer_weights = outer_rows(weights)
    chunks = chunks_of(modes // (sizes["gx"] * sizes["gy"]))
    length = modes // chunks
    results = []
    for chunk in range(chunks):
        low, middle, high = chunk * length, chunk * length + length // 2, (chunk + 1) * length
        outer = functools.partial(partial_tensor, own_outer, other_outer, slopes_outer, sizes=sizes, before=inner)
        stages = stages_of(sizes, chunk == chunks - 1)
        sent = outer(weights=outer_weights, positions=(middle, high), dtype=BF16)
        outer_weights, sent = barrier((outer_weights, sent))
        arrived = [flip(sent, stages[0], sizes)]
        kept = outer(weights=outer_weights, positions=(low, middle))
        if chunk < chunks - 1:
            outer_weights, kept, arrived = barrier((outer_weights, kept, arrived))
        results.append((kept, arrived, stages))
    finished = []
    for kept, arrived, stages in results:
        kept, arrived = halve_stages(kept, arrived, stages[1:], sizes)
        finished.append(finish(kept, arrived, stages[-1], sizes, share))
    return jnp.concatenate(finished, 0)


def solution(mesh):
    in_specs = (P(None, "ma", "gx", "gy"), P("gx", "gy"))
    out_specs = P(("gx", "gy"), "ma", None)
    body = functools.partial(shards, sizes=dict(mesh.shape))
    return jax.shard_map(body, mesh=mesh, in_specs=in_specs, out_specs=out_specs, check_vma=False)
```

```python
import functools
import math

import jax
import jax.numpy as jnp
from jax import lax
from jax.experimental import pallas as pl
from jax.experimental.pallas import tpu as pltpu
from jax.sharding import PartitionSpec as P

BF16 = jnp.bfloat16
F32 = jnp.float32


def bits_of(count):
    return count.bit_length() - 1


def send_order(sizes):
    order = []
    for axis in ("gy", "gx"):
        order += [(axis, bit) for bit in range(bits_of(sizes[axis]))]
    return order


def source_bits(sizes, rows_each, chunks):
    row_bits = bits_of(rows_each)
    base = {"gy": row_bits, "gx": row_bits + bits_of(sizes["gy"])}
    inner = row_bits - bits_of(chunks)
    found = list(range(inner))
    for axis, bit in reversed(send_order(sizes)):
        found.append(base[axis] + bit)
    return found + list(range(inner, row_bits))


def slopes_kernel(own_ref, before_ref, after_ref, *refs, rows):
    out_ref = refs[-1]
    last = own_ref.shape[0] - 1
    before = before_ref[...].astype(F32).T
    after = after_ref[...].astype(F32).T
    cells = own_ref.shape[3]
    lane = lax.broadcasted_iota(jnp.int32, own_ref.shape[2:], 1)
    for place, x in enumerate(rows):
        for a in range(3):
            down = (refs[0][0, a] if x == 0 else own_ref[x - 1, a]).astype(F32)
            up = (refs[1][0, a] if x == last else own_ref[x + 1, a]).astype(F32)
            out_ref[place, a] = ((up - down) * 0.5).astype(BF16)
            value = own_ref[x, a].astype(F32)
            column = 3 * x + a
            down = jnp.where(lane == 0, before[:, column : column + 1], pltpu.roll(value, 1, 1))
            up = jnp.where(lane == cells - 1, after[:, column : column + 1], pltpu.roll(value, cells - 1, 1))
            out_ref[place, 3 + a] = ((up - down) * 0.5).astype(BF16)


def slopes_of(own, before, after, rows, token, edges):
    row_count, _, share, cells = own.shape
    return pl.pallas_call(
        functools.partial(slopes_kernel, rows=rows),
        out_shape=jax.ShapeDtypeStruct((len(rows), 6, share, cells), BF16),
        in_specs=[pl.BlockSpec(memory_space=pltpu.VMEM)] * (4 + len(edges)),
        out_specs=pl.BlockSpec(memory_space=pltpu.VMEM),
        compiler_params=pltpu.CompilerParams(vmem_limit_bytes=16 << 20),
        cost_estimate=pl.CostEstimate(flops=1, bytes_accessed=1024, transcendentals=0),
    )(own, before.reshape(3 * row_count, share), after.reshape(3 * row_count, share), *edges, token)


def chunks_of(rows_each):
    return 2 if rows_each > 1 else 1


def tensor_kernel(*refs, bits, block, rows_each, first_step):
    own_ref, other_ref, slope_ref, weight_ref = refs[:4]
    before_ref = refs[4] if len(refs) == 8 else None
    out_ref, left, right = refs[-3:]
    row_count, _, share, cells = own_ref.shape
    step = pl.program_id(0)
    top = bits_of(2 * share) - 1

    @pl.when(step == 0)
    def _():
        for x in range(row_count):
            weight = weight_ref[pl.ds(x, 1), :]
            for half, ref in enumerate((own_ref, other_ref)):
                for a in range(3):
                    value = (weight * ref[x, a].astype(F32)).astype(BF16)
                    left[x, a, half * share : (half + 1) * share, :] = value.astype(F32)
                for b in range(2):
                    right[
                        half * share : (half + 1) * share, (2 * x + b) * cells : (2 * x + b + 1) * cells
                    ] = ref[x, b]

    here = (lax.axis_index("gx") * lax.axis_size("gy") + lax.axis_index("gy")) * rows_each
    start = here ^ (lax.axis_index("ma") << top)
    position = (first_step + step) * block
    for place, bit in enumerate(bits):
        start = start ^ (((position >> place) & 1) << bit)
    columns = []
    for x in range(row_count):
        slopes = [slope_ref[x, n] for n in range(6)]
        sums = [[], []]
        for row in range(block):
            offset = 0
            for place, bit in enumerate(bits):
                offset |= ((row >> place) & 1) << bit
            test = [
                jnp.concatenate(
                    [left[x, a, pl.ds(start ^ offset, 16, stride=0), :].astype(BF16)] * (share // 16), 0
                )
                for a in range(3)
            ]
            for b in range(2):
                sums[b].append(
                    test[0] * slopes[3 * b] + test[1] * slopes[3 * b + 1] + test[2] * slopes[3 * b + 2]
                )
        columns += [jnp.concatenate(sums[0], 0), jnp.concatenate(sums[1], 0)]
    sums = jnp.concatenate(columns, 1)
    product = lax.dot_general(sums, right[...], (((1,), (1,)), ((), ())), preferred_element_type=F32)
    product = product.reshape(block, share, 2 * share)
    if before_ref is not None:
        product = product + before_ref[...]
    out_ref[...] = product.astype(out_ref.dtype)


def partial_tensor(own, other, slopes, weights, sizes, positions, before=None, dtype=F32):
    row_count, _, share, cells = own.shape
    modes = 2 * share
    low, high = positions
    block = min(16, high - low)
    first_step = low // block
    rows_each = modes // (sizes["gx"] * sizes["gy"])
    body = functools.partial(
        tensor_kernel,
        bits=source_bits(sizes, rows_each, chunks_of(rows_each)),
        block=block,
        rows_each=rows_each,
        first_step=first_step,
    )
    whole = lambda array: pl.BlockSpec(array.shape, lambda g: (0,) * array.ndim, pipeline_mode=pl.Buffered(1))
    shape = (block, share, modes)
    operands = [own, other, slopes, weights]
    in_specs = [whole(array) for array in operands]
    if before is not None:
        operands.append(before)
        in_specs.append(pl.BlockSpec(shape, lambda g: (first_step + g, 0, 0)))
    return pl.pallas_call(
        body,
        grid=((high - low) // block,),
        out_shape=jax.ShapeDtypeStruct((high - low, share, modes), dtype) if before is not None
        else pltpu.VMEM((high - low, share, modes), dtype),
        in_specs=in_specs,
        out_specs=pl.BlockSpec(shape, lambda g: (g, 0, 0)),
        scratch_shapes=[
            pltpu.VMEM((row_count, 3, modes, cells), F32),
            pltpu.VMEM((modes, row_count * 2 * cells), BF16),
        ],
        compiler_params=pltpu.CompilerParams(vmem_limit_bytes=20 << 20),
        cost_estimate=pl.CostEstimate(
            flops=8 * (high - low) * share * modes * row_count * cells, bytes_accessed=4 << 20, transcendentals=0
        ),
    )(*operands)


def neighbours(axis):
    count = lax.axis_size(axis)
    forward = [(i, i + 1) for i in range(count - 1)]
    return forward, [(target, source) for source, target in forward]


def flip(array, flips, sizes):
    axes = tuple(sorted({axis for axis, _ in flips}, key=("gx", "gy", "ma").index))
    strides = {}
    count = 1
    for axis in reversed(axes):
        strides[axis] = count
        count *= sizes[axis]
    change = 0
    for axis, bit in flips:
        change |= strides[axis] << bit
    return lax.ppermute(array, axes, [(i, i ^ change) for i in range(count)])


def subsets(stage):
    for code in range(1, 1 << len(stage)):
        yield code, [stage[n] for n in range(len(stage)) if (code >> (len(stage) - 1 - n)) & 1]


def stages_of(sizes):
    order = send_order(sizes)
    return [[order[0]], order[1:3]] + [[entry] for entry in order[3:]]


def term_sum(terms, low, high):
    total = terms[0][low:high].astype(F32)
    for array in terms[1:]:
        total = total + array[low:high].astype(F32)
    return total


def sends(terms, count, stage):
    length = count >> len(stage)
    return [
        term_sum(terms, code * length, (code + 1) * length).astype(BF16)
        for code, _ in reversed(list(subsets(stage)))
    ]


def exchange(terms, stage, sent, sizes):
    received = [flip(array, flips, sizes) for array, (_, flips) in zip(sent, reversed(list(subsets(stage))))]
    return terms + received


def combine_kernel(*refs, chunks, terms, pair):
    outs = refs[chunks * terms :]
    count, share, modes = refs[0].shape
    each = count // 2 // pair
    for above in range(2):
        for chunk in range(chunks):
            for place in range(each):
                rows = pl.ds(above * (count // 2) + place * pair, pair)
                total = refs[chunk * terms][rows].astype(F32)
                for ref in refs[chunk * terms + 1 : (chunk + 1) * terms]:
                    total = total + ref[rows].astype(F32)
                total = total.reshape(pair * share, modes).T
                for swapped in range(2):
                    out = outs[2 * above + swapped]
                    out[chunk * each + place] = total[swapped * share : (swapped + 1) * share].astype(out.dtype)


def assemble_kernel(own_ref, swapped_ref, above_ref, both_ref, out_ref, *, pair):
    count, share, width = own_ref.shape
    first = lax.axis_index("ma") == 0
    for place in range(count):
        mine = own_ref[place] + above_ref[place].astype(F32)
        theirs = swapped_ref[place].astype(F32) + both_ref[place].astype(F32)
        low = jnp.where(first, mine, theirs)
        high = jnp.where(first, theirs, mine)
        for part in range(pair):
            lanes = slice(part * (width // pair), (part + 1) * (width // pair))
            out_ref[place * pair + part] = jnp.concatenate([low[:, lanes], high[:, lanes]], 1)


def finish(chunk_terms, count, stage, sizes):
    chunks, terms = len(chunk_terms), len(chunk_terms[0])
    _, share, modes = chunk_terms[0][0].shape
    pair = 2 if count % 4 == 0 else 1
    places = chunks * count // 2 // pair
    shape = (places, share, pair * share)
    whole = lambda shape: pl.BlockSpec(shape, lambda g: (0,) * len(shape))
    parts = pl.pallas_call(
        functools.partial(combine_kernel, chunks=chunks, terms=terms, pair=pair),
        grid=(1,),
        out_shape=[jax.ShapeDtypeStruct(shape, dtype) for dtype in (F32, BF16, BF16, BF16)],
        in_specs=[whole((count, share, modes))] * (chunks * terms),
        out_specs=[whole(shape)] * 4,
        compiler_params=pltpu.CompilerParams(vmem_limit_bytes=16 << 20),
        cost_estimate=pl.CostEstimate(flops=1, bytes_accessed=1024, transcendentals=0),
    )(*[array for terms in chunk_terms for array in terms])
    stage = stage + [("ma", 0)]
    arrived = {code: flip(parts[code], flips, sizes) for code, flips in reversed(list(subsets(stage)))}
    return pl.pallas_call(
        functools.partial(assemble_kernel, pair=pair),
        out_shape=jax.ShapeDtypeStruct((places * pair, share, modes), F32),
        in_specs=[pl.BlockSpec(memory_space=pltpu.VMEM)] * 4,
        out_specs=pl.BlockSpec(memory_space=pltpu.VMEM),
        compiler_params=pltpu.CompilerParams(vmem_limit_bytes=16 << 20),
        cost_estimate=pl.CostEstimate(flops=1, bytes_accessed=1024, transcendentals=0),
    )(parts[0], arrived[1], arrived[2], arrived[3])


def shards(mode_fields, cell_volumes, sizes):
    total_cells = cell_volumes.shape[0] * sizes["gx"] * cell_volumes.shape[1] * sizes["gy"]
    weights = cell_volumes * (1.0 / math.sqrt(total_cells))
    barrier = lax.optimization_barrier
    own = jnp.transpose(mode_fields, (2, 0, 1, 3))
    row_count, _, share, _ = own.shape
    modes = 2 * share
    quarter = row_count // 4

    def inner_rows(array):
        return array[quarter : 3 * quarter]

    def outer_rows(array):
        return jnp.concatenate([array[:quarter], array[3 * quarter :]], 0)

    own_inner, own_outer = inner_rows(own), outer_rows(own)
    other_inner = flip(own_inner, [("ma", 0)], sizes)
    token = flip(own[quarter, 0, :16], [("ma", 0)], sizes)
    held, token = barrier((own, token))
    forward, backward = neighbours("gy")
    before = lax.ppermute(held[:, :, :, -1], "gy", forward)
    after = lax.ppermute(held[:, :, :, 0], "gy", backward)
    forward, backward = neighbours("gx")
    held, before, after = barrier((own, before, after))
    above = lax.ppermute(held[-1:], "gx", forward)
    below = lax.ppermute(held[:1], "gx", backward)
    own_outer_held, above, below = barrier((own_outer, above, below))
    other_outer = flip(own_outer_held, [("ma", 0)], sizes)
    all_rows = tuple(range(row_count))
    slopes_inner = slopes_of(own, before, after, all_rows[quarter : 3 * quarter], token, [])
    slopes_outer = slopes_of(
        own, before, after, all_rows[:quarter] + all_rows[3 * quarter :], token, [above, below]
    )

    inner = partial_tensor(own_inner, other_inner, slopes_inner, inner_rows(weights), sizes, (0, modes))
    outer_weights = outer_rows(weights)
    chunks = chunks_of(modes // (sizes["gx"] * sizes["gy"]))
    length = modes // chunks
    stages = stages_of(sizes)
    results = []
    for chunk in range(chunks):
        low, middle, high = chunk * length, chunk * length + length // 2, (chunk + 1) * length
        outer = functools.partial(partial_tensor, own_outer, other_outer, slopes_outer, sizes=sizes, before=inner)
        sent = outer(weights=outer_weights, positions=(middle, high), dtype=BF16)
        outer_weights, sent = barrier((outer_weights, sent))
        arrived = flip(sent, stages[0], sizes)
        terms = [outer(weights=outer_weights, positions=(low, middle)), arrived]
        sent = sends(terms, length // 2, stages[1])
        if chunk < chunks - 1:
            outer_weights, sent = barrier((outer_weights, sent))
        results.append(exchange(terms, stages[1], sent, sizes))
    count = (length // 2) >> len(stages[1])
    for stage in stages[2:-1]:
        results = [exchange(terms, stage, sends(terms, count, stage), sizes) for terms in results]
        count = count >> len(stage)
    return finish(results, count, stages[-1], sizes)


def solution(mesh):
    in_specs = (P(None, "ma", "gx", "gy"), P("gx", "gy"))
    out_specs = P(("gx", "gy"), "ma", None)
    body = functools.partial(shards, sizes=dict(mesh.shape))
    return jax.shard_map(body, mesh=mesh, in_specs=in_specs, out_specs=out_specs, check_vma=False)
```

```python
import functools
import math

import jax
import jax.numpy as jnp
from jax import lax
from jax.experimental import pallas as pl
from jax.experimental.pallas import tpu as pltpu
from jax.sharding import PartitionSpec as P

BF16 = jnp.bfloat16
F32 = jnp.float32


def bits_of(count):
    return count.bit_length() - 1


def send_order(sizes):
    order = []
    for axis in ("gy", "gx"):
        order += [(axis, bit) for bit in range(bits_of(sizes[axis]))]
    return order


def source_bits(sizes, rows_each):
    row_bits = bits_of(rows_each)
    base = {"gy": row_bits, "gx": row_bits + bits_of(sizes["gy"])}
    found = list(range(row_bits))
    for axis, bit in reversed(send_order(sizes)):
        found.append(base[axis] + bit)
    return found


def slopes_kernel(own_ref, before_ref, after_ref, *refs, rows):
    out_ref = refs[-1]
    last = own_ref.shape[0] - 1
    before = before_ref[...].astype(F32).T
    after = after_ref[...].astype(F32).T
    cells = own_ref.shape[3]
    lane = lax.broadcasted_iota(jnp.int32, own_ref.shape[2:], 1)
    for place, x in enumerate(rows):
        for a in range(3):
            down = (refs[0][0, a] if x == 0 else own_ref[x - 1, a]).astype(F32)
            up = (refs[1][0, a] if x == last else own_ref[x + 1, a]).astype(F32)
            out_ref[place, a] = ((up - down) * 0.5).astype(BF16)
            value = own_ref[x, a].astype(F32)
            column = 3 * x + a
            down = jnp.where(lane == 0, before[:, column : column + 1], pltpu.roll(value, 1, 1))
            up = jnp.where(lane == cells - 1, after[:, column : column + 1], pltpu.roll(value, cells - 1, 1))
            out_ref[place, 3 + a] = ((up - down) * 0.5).astype(BF16)


def slopes_of(own, before, after, rows, token, edges):
    row_count, _, share, cells = own.shape
    return pl.pallas_call(
        functools.partial(slopes_kernel, rows=rows),
        out_shape=jax.ShapeDtypeStruct((len(rows), 6, share, cells), BF16),
        in_specs=[pl.BlockSpec(memory_space=pltpu.VMEM)] * (4 + len(edges)),
        out_specs=pl.BlockSpec(memory_space=pltpu.VMEM),
        compiler_params=pltpu.CompilerParams(vmem_limit_bytes=16 << 20),
        cost_estimate=pl.CostEstimate(flops=1, bytes_accessed=1024, transcendentals=0),
    )(own, before.reshape(3 * row_count, share), after.reshape(3 * row_count, share), *edges, token)


def tensor_kernel(*refs, bits, block, rows_each, first_step, rows, scale):
    own_ref, other_ref, slope_ref, volume_ref = refs[:4]
    before_ref = refs[4] if len(refs) == 8 else None
    out_ref, left, right = refs[-3:]
    row_count, _, share, cells = own_ref.shape
    step = pl.program_id(0)
    top = bits_of(2 * share) - 1

    @pl.when(step == 0)
    def _():
        for x in range(row_count):
            weight = volume_ref[pl.ds(rows[x], 1), :] * scale
            for half, ref in enumerate((own_ref, other_ref)):
                for a in range(3):
                    value = (weight * ref[x, a].astype(F32)).astype(BF16)
                    left[x, a, half * share : (half + 1) * share, :] = value.astype(F32)
                for b in range(2):
                    right[
                        half * share : (half + 1) * share, (2 * x + b) * cells : (2 * x + b + 1) * cells
                    ] = ref[x, b]

    here = (lax.axis_index("gx") * lax.axis_size("gy") + lax.axis_index("gy")) * rows_each
    start = here ^ (lax.axis_index("ma") << top)
    position = (first_step + step) * block
    for place, bit in enumerate(bits):
        start = start ^ (((position >> place) & 1) << bit)
    columns = []
    for x in range(row_count):
        slopes = [slope_ref[x, n] for n in range(6)]
        sums = [[], []]
        for row in range(block):
            offset = 0
            for place, bit in enumerate(bits):
                offset |= ((row >> place) & 1) << bit
            test = [
                jnp.concatenate(
                    [left[x, a, pl.ds(start ^ offset, 16, stride=0), :].astype(BF16)] * (share // 16), 0
                )
                for a in range(3)
            ]
            for b in range(2):
                sums[b].append(
                    test[0] * slopes[3 * b] + test[1] * slopes[3 * b + 1] + test[2] * slopes[3 * b + 2]
                )
        columns += [jnp.concatenate(sums[0], 0), jnp.concatenate(sums[1], 0)]
    sums = jnp.concatenate(columns, 1)
    product = lax.dot_general(sums, right[...], (((1,), (1,)), ((), ())), preferred_element_type=F32)
    product = product.reshape(block, share, 2 * share)
    if before_ref is not None:
        product = product + before_ref[...]
    out_ref[...] = product.astype(out_ref.dtype)


def partial_tensor(own, other, slopes, volumes, rows, sizes, positions, before=None, dtype=F32):
    row_count, _, share, cells = own.shape
    modes = 2 * share
    low, high = positions
    block = min(16, high - low)
    first_step = low // block
    devices = sizes["gx"] * sizes["gy"]
    rows_each = modes // devices
    body = functools.partial(
        tensor_kernel,
        bits=source_bits(sizes, rows_each),
        block=block,
        rows_each=rows_each,
        first_step=first_step,
        rows=rows,
        scale=1.0 / math.sqrt(volumes.shape[0] * volumes.shape[1] * devices),
    )
    whole = lambda array: pl.BlockSpec(array.shape, lambda g: (0,) * array.ndim, pipeline_mode=pl.Buffered(1))
    shape = (block, share, modes)
    operands = [own, other, slopes, volumes]
    in_specs = [whole(array) for array in operands]
    if before is not None:
        operands.append(before)
        in_specs.append(pl.BlockSpec(shape, lambda g: (first_step + g, 0, 0)))
    return pl.pallas_call(
        body,
        grid=((high - low) // block,),
        out_shape=jax.ShapeDtypeStruct((high - low, share, modes), dtype) if before is not None
        else pltpu.VMEM((high - low, share, modes), dtype),
        in_specs=in_specs,
        out_specs=pl.BlockSpec(shape, lambda g: (g, 0, 0)),
        scratch_shapes=[
            pltpu.VMEM((row_count, 3, modes, cells), F32),
            pltpu.VMEM((modes, row_count * 2 * cells), BF16),
        ],
        compiler_params=pltpu.CompilerParams(vmem_limit_bytes=20 << 20),
        cost_estimate=pl.CostEstimate(
            flops=8 * (high - low) * share * modes * row_count * cells, bytes_accessed=4 << 20, transcendentals=0
        ),
    )(*operands)


def neighbours(axis):
    count = lax.axis_size(axis)
    forward = [(i, i + 1) for i in range(count - 1)]
    return forward, [(target, source) for source, target in forward]


def flip(array, flips, sizes):
    axes = tuple(sorted({axis for axis, _ in flips}, key=("gx", "gy", "ma").index))
    strides = {}
    count = 1
    for axis in reversed(axes):
        strides[axis] = count
        count *= sizes[axis]
    change = 0
    for axis, bit in flips:
        change |= strides[axis] << bit
    return lax.ppermute(array, axes, [(i, i ^ change) for i in range(count)])


def subsets(stage):
    for code in range(1, 1 << len(stage)):
        yield code, [stage[n] for n in range(len(stage)) if (code >> (len(stage) - 1 - n)) & 1]


def stages_of(sizes):
    order = send_order(sizes)
    return [[order[0]], order[1:3]] + [[entry] for entry in order[3:]]


def term_sum(terms, low, high):
    total = terms[0][low:high].astype(F32)
    for array in terms[1:]:
        total = total + array[low:high].astype(F32)
    return total


def sends(terms, count, stage):
    length = count >> len(stage)
    return [
        term_sum(terms, code * length, (code + 1) * length).astype(BF16) for code, _ in subsets(stage)
    ]


def exchange(stage, sent, sizes):
    return [flip(array, flips, sizes) for array, (_, flips) in zip(sent, subsets(stage))]


def combine_kernel(*refs, terms, pair):
    outs = refs[terms:]
    count, share, modes = refs[0].shape
    each = count // 2 // pair
    for above in range(2):
        for place in range(each):
            rows = pl.ds(above * (count // 2) + place * pair, pair)
            total = refs[0][rows].astype(F32)
            for ref in refs[1:terms]:
                total = total + ref[rows].astype(F32)
            total = total.reshape(pair * share, modes).T
            for swapped in range(2):
                out = outs[2 * above + swapped]
                out[place] = total[swapped * share : (swapped + 1) * share].astype(out.dtype)


def assemble_kernel(own_ref, swapped_ref, above_ref, both_ref, out_ref, *, pair):
    count, share, width = own_ref.shape
    first = lax.axis_index("ma") == 0
    for place in range(count):
        mine = own_ref[place] + above_ref[place].astype(F32)
        theirs = swapped_ref[place].astype(F32) + both_ref[place].astype(F32)
        low = jnp.where(first, mine, theirs)
        high = jnp.where(first, theirs, mine)
        for part in range(pair):
            lanes = slice(part * (width // pair), (part + 1) * (width // pair))
            out_ref[place * pair + part] = jnp.concatenate([low[:, lanes], high[:, lanes]], 1)


def sum_kernel(*refs):
    total = refs[0][...].astype(F32)
    for ref in refs[1:-1]:
        total = total + ref[...].astype(F32)
    refs[-1][...] = total


def summed(terms, count, cost):
    shape = (count, *terms[0].shape[1:])
    whole = pl.BlockSpec(shape, lambda g: (0,) * len(shape))
    return pl.pallas_call(
        sum_kernel,
        grid=(1,),
        out_shape=jax.ShapeDtypeStruct(shape, F32),
        in_specs=[whole] * len(terms),
        out_specs=whole,
        compiler_params=pltpu.CompilerParams(vmem_limit_bytes=16 << 20),
        cost_estimate=pl.CostEstimate(flops=cost, bytes_accessed=1024, transcendentals=0),
    )(*terms)


def finish(terms, count, stage, sizes):
    _, share, modes = terms[0].shape
    pair = 2 if count % 4 == 0 else 1
    places = count // 2 // pair
    shape = (places, share, pair * share)
    whole = lambda shape: pl.BlockSpec(shape, lambda g: (0,) * len(shape))
    parts = pl.pallas_call(
        functools.partial(combine_kernel, terms=len(terms), pair=pair),
        grid=(1,),
        out_shape=[jax.ShapeDtypeStruct(shape, dtype) for dtype in (F32, BF16, BF16, BF16)],
        in_specs=[whole((count, share, modes))] * len(terms),
        out_specs=[whole(shape)] * 4,
        compiler_params=pltpu.CompilerParams(vmem_limit_bytes=16 << 20),
        cost_estimate=pl.CostEstimate(flops=1, bytes_accessed=1024, transcendentals=0),
    )(*terms)
    stage = stage + [("ma", 0)]
    arrived = {code: flip(parts[code], flips, sizes) for code, flips in reversed(list(subsets(stage)))}
    return pl.pallas_call(
        functools.partial(assemble_kernel, pair=pair),
        out_shape=jax.ShapeDtypeStruct((places * pair, share, modes), F32),
        in_specs=[pl.BlockSpec(memory_space=pltpu.VMEM)] * 4,
        out_specs=pl.BlockSpec(memory_space=pltpu.VMEM),
        compiler_params=pltpu.CompilerParams(vmem_limit_bytes=16 << 20),
        cost_estimate=pl.CostEstimate(flops=1, bytes_accessed=1024, transcendentals=0),
    )(parts[0], arrived[1], arrived[2], arrived[3])


def shards(mode_fields, cell_volumes, sizes):
    barrier = lax.optimization_barrier
    own = jnp.transpose(mode_fields, (2, 0, 1, 3))
    row_count, _, share, _ = own.shape
    modes = 2 * share
    quarter = row_count // 4
    all_rows = tuple(range(row_count))
    inner_rows = all_rows[quarter : 3 * quarter]
    outer_rows = all_rows[:quarter] + all_rows[3 * quarter :]
    own_inner = own[quarter : 3 * quarter]
    own_outer = jnp.concatenate([own[:quarter], own[3 * quarter :]], 0)

    other_inner = flip(own_inner, [("ma", 0)], sizes)
    token = flip(own[quarter, 0, :16], [("ma", 0)], sizes)
    edges = own[:, :, :, -1], own[:, :, :, 0], own[-1:], own[:1]
    edges, token = barrier((edges, token))
    forward, backward = neighbours("gy")
    before = lax.ppermute(edges[0], "gy", forward)
    after = lax.ppermute(edges[1], "gy", backward)
    forward, backward = neighbours("gx")
    above = lax.ppermute(edges[2], "gx", forward)
    below = lax.ppermute(edges[3], "gx", backward)
    own_outer_held, before, after = barrier((own_outer, before, after))
    other_outer = flip(own_outer_held, [("ma", 0)], sizes)
    slopes_inner = slopes_of(own, before, after, inner_rows, token, [])
    slopes_outer = slopes_of(own, before, after, outer_rows, token, [above, below])

    inner = partial_tensor(own_inner, other_inner, slopes_inner, cell_volumes, inner_rows, sizes, (0, modes))
    outer = functools.partial(
        partial_tensor, own_outer, other_outer, slopes_outer, rows=outer_rows, sizes=sizes, before=inner
    )
    stages = stages_of(sizes)
    half, quarter = modes // 2, modes // 4
    cell_count = mode_fields.shape[2] * mode_fields.shape[3]
    sent = outer(cell_volumes, positions=(half, modes), dtype=BF16)
    cell_volumes, sent = barrier((cell_volumes, sent))
    arrived = flip(sent, stages[0], sizes)
    upper = outer(cell_volumes, positions=(quarter, half))
    eighth = quarter // 2
    sent = [
        (upper[at : at + eighth] + arrived[quarter + at : quarter + at + eighth].astype(F32)).astype(BF16)
        for at in (0, eighth)
    ]
    cell_volumes, sent = barrier((cell_volumes, sent))
    lower = outer(cell_volumes, positions=(0, quarter))
    sent = [(lower[eighth:] + arrived[eighth:quarter].astype(F32)).astype(BF16)] + sent
    received = exchange(stages[1], sent, sizes)
    count = eighth
    terms = [summed([lower, arrived] + received[1:], count, 2 * quarter * modes * share * cell_count), received[0]]
    for stage in stages[2:-1]:
        terms = terms + exchange(stage, sends(terms, count, stage), sizes)
        count = count >> len(stage)
    return finish(terms, count, stages[-1], sizes)


def solution(mesh):
    in_specs = (P(None, "ma", "gx", "gy"), P("gx", "gy"))
    out_specs = P(("gx", "gy"), "ma", None)
    body = functools.partial(shards, sizes=dict(mesh.shape))
    return jax.shard_map(body, mesh=mesh, in_specs=in_specs, out_specs=out_specs, check_vma=False)
```

```python
import functools
import math

import jax
import jax.numpy as jnp
from jax import lax
from jax.experimental import pallas as pl
from jax.experimental.pallas import tpu as pltpu
from jax.sharding import PartitionSpec as P

BF16 = jnp.bfloat16
F32 = jnp.float32
BLOCKS = 8


def bits_of(count):
    return count.bit_length() - 1


def send_order(sizes):
    order = []
    for axis in ("gy", "gx"):
        order += [(axis, bit) for bit in range(bits_of(sizes[axis]))]
    return order


def source_bits(sizes, rows_each):
    row_bits = bits_of(rows_each)
    base = {"gy": row_bits, "gx": row_bits + bits_of(sizes["gy"])}
    found = list(range(row_bits))
    for axis, bit in reversed(send_order(sizes)):
        found.append(base[axis] + bit)
    return found


def slopes_kernel(own_ref, *refs, rows, parts):
    out_ref = refs[-1]
    last = own_ref.shape[0] - 1
    cells = own_ref.shape[3]
    if 1 in parts:
        before = refs[0][...].astype(F32).T
        after = refs[1][...].astype(F32).T
        lane = lax.broadcasted_iota(jnp.int32, own_ref.shape[2:], 1)
    for place, x in enumerate(rows):
        for a in range(3):
            if 0 in parts:
                down = (refs[2][0, a] if x == 0 else own_ref[x - 1, a]).astype(F32)
                up = (refs[3][0, a] if x == last else own_ref[x + 1, a]).astype(F32)
                out_ref[place, a] = ((up - down) * 0.5).astype(BF16)
            if 1 in parts:
                value = own_ref[x, a].astype(F32)
                column = 3 * x + a
                down = jnp.where(lane == 0, before[:, column : column + 1], pltpu.roll(value, 1, 1))
                up = jnp.where(lane == cells - 1, after[:, column : column + 1], pltpu.roll(value, cells - 1, 1))
                out_ref[place, 3 * parts.index(1) + a] = ((up - down) * 0.5).astype(BF16)


def slopes_of(own, rows, parts, *others):
    _, _, share, cells = own.shape
    return pl.pallas_call(
        functools.partial(slopes_kernel, rows=rows, parts=parts),
        out_shape=jax.ShapeDtypeStruct((len(rows), 3 * len(parts), share, cells), BF16),
        in_specs=[pl.BlockSpec(memory_space=pltpu.VMEM)] * (1 + len(others)),
        out_specs=pl.BlockSpec(memory_space=pltpu.VMEM),
        compiler_params=pltpu.CompilerParams(vmem_limit_bytes=16 << 20),
        cost_estimate=pl.CostEstimate(flops=1, bytes_accessed=1024, transcendentals=0),
    )(own, *others)


def sum_of(left, right):
    return left[0] * right[0] + left[1] * right[1] + left[2] * right[2]


def tensor_kernel(*refs, bits, block, rows_each, first_block, stride, rows, scale, parts, outputs):
    own_ref, other_ref, slope_ref, volume_ref = refs[:4]
    left, right = refs[-2:]
    out_refs = refs[-2 - outputs : -2]
    before_ref = refs[4] if len(refs) == 7 + outputs else None
    row_count, _, share, cells = own_ref.shape
    step = pl.program_id(0)
    top = bits_of(2 * share) - 1

    @pl.when(step == 0)
    def _():
        for x in range(row_count):
            weight = volume_ref[pl.ds(rows[x], 1), :] * scale
            for half, ref in enumerate((own_ref, other_ref)):
                for a in range(3):
                    value = (weight * ref[x, a].astype(F32)).astype(BF16)
                    left[x, a, half * share : (half + 1) * share, :] = value.astype(F32)
                for place, b in enumerate(parts):
                    lanes = len(parts) * x + place
                    right[half * share : (half + 1) * share, lanes * cells : (lanes + 1) * cells] = ref[x, b]

    here = (lax.axis_index("gx") * lax.axis_size("gy") + lax.axis_index("gy")) * rows_each
    start = here ^ (lax.axis_index("ma") << top)
    position = (first_block + stride * step) * block
    for place, bit in enumerate(bits):
        start = start ^ (((position >> place) & 1) << bit)
    columns = []
    for x in range(row_count):
        slopes = [slope_ref[x, n] for n in range(3 * len(parts))]
        sums = [[] for _ in parts]
        for row in range(block):
            offset = 0
            for place, bit in enumerate(bits):
                offset |= ((row >> place) & 1) << bit
            test = [
                jnp.concatenate(
                    [left[x, a, pl.ds(start ^ offset, 16, stride=0), :].astype(BF16)] * (share // 16), 0
                )
                for a in range(3)
            ]
            for place, found in enumerate(sums):
                found.append(sum_of(test, slopes[3 * place : 3 * place + 3]))
        columns += [jnp.concatenate(found, 0) for found in sums]
    sums = jnp.concatenate(columns, 1)
    product = lax.dot_general(sums, right[...], (((1,), (1,)), ((), ())), preferred_element_type=F32)
    product = product.reshape(block, share, 2 * share)
    if before_ref is not None:
        product = product + before_ref[...]
    if outputs == 1:
        out_refs[0][...] = product.astype(out_refs[0].dtype)
    else:
        for place, out_ref in enumerate(out_refs):

            @pl.when(step == place)
            def _(out_ref=out_ref):
                out_ref[...] = product.astype(out_ref.dtype)


def partial_tensor(own, other, slopes, volumes, rows, sizes, blocks, before=None, dtypes=(F32,), parts=(0, 1)):
    row_count, _, share, cells = own.shape
    modes = 2 * share
    block = modes // BLOCKS
    stride = blocks[1] - blocks[0] if len(blocks) > 1 else 1
    outputs = len(dtypes)
    devices = sizes["gx"] * sizes["gy"]
    rows_each = modes // devices
    body = functools.partial(
        tensor_kernel,
        bits=source_bits(sizes, rows_each),
        block=block,
        rows_each=rows_each,
        first_block=blocks[0],
        stride=stride,
        outputs=outputs,
        rows=rows,
        parts=parts,
        scale=1.0 / math.sqrt(volumes.shape[0] * volumes.shape[1] * devices),
    )
    whole = lambda array: pl.BlockSpec(array.shape, lambda g: (0,) * array.ndim, pipeline_mode=pl.Buffered(1))
    shape = (block, share, modes)
    operands = [own, other, slopes, volumes]
    in_specs = [whole(array) for array in operands]
    if before is not None:
        operands.append(before)
        in_specs.append(pl.BlockSpec(shape, lambda g: (blocks[0] + stride * g, 0, 0)))
    if outputs > 1:
        out_shape = [jax.ShapeDtypeStruct(shape, dtype) for dtype in dtypes]
        out_specs = [pl.BlockSpec(shape, lambda g: (0, 0, 0))] * outputs
    else:
        out_shape = (pltpu.VMEM if len(blocks) == BLOCKS else jax.ShapeDtypeStruct)(
            (len(blocks) * block, share, modes), dtypes[0]
        )
        out_specs = pl.BlockSpec(shape, lambda g: (g, 0, 0))
    return pl.pallas_call(
        body,
        grid=(len(blocks),),
        out_shape=out_shape,
        in_specs=in_specs,
        out_specs=out_specs,
        scratch_shapes=[
            pltpu.VMEM((row_count, 3, modes, cells), F32),
            pltpu.VMEM((modes, row_count * len(parts) * cells), BF16),
        ],
        compiler_params=pltpu.CompilerParams(vmem_limit_bytes=20 << 20),
        cost_estimate=pl.CostEstimate(
            flops=4 * len(parts) * len(blocks) * block * share * modes * row_count * cells, bytes_accessed=4 << 20, transcendentals=0
        ),
    )(*operands)


def neighbours(axis):
    count = lax.axis_size(axis)
    forward = [(i, i + 1) for i in range(count - 1)]
    return forward, [(target, source) for source, target in forward]


def flip(array, flips, sizes):
    axes = tuple(sorted({axis for axis, _ in flips}, key=("gx", "gy", "ma").index))
    strides = {}
    count = 1
    for axis in reversed(axes):
        strides[axis] = count
        count *= sizes[axis]
    change = 0
    for axis, bit in flips:
        change |= strides[axis] << bit
    return lax.ppermute(array, axes, [(i, i ^ change) for i in range(count)])


def subsets(stage):
    for code in range(1, 1 << len(stage)):
        yield code, [stage[n] for n in range(len(stage)) if (code >> (len(stage) - 1 - n)) & 1]


def stages_of(sizes):
    order = send_order(sizes)
    return [[order[0]], order[1:3]] + [[entry] for entry in order[3:]]


def term_sum(terms, low, high):
    total = terms[0][low:high].astype(F32)
    for array in terms[1:]:
        total = total + array[low:high].astype(F32)
    return total


def sends(terms, count, stage):
    length = count >> len(stage)
    return [
        term_sum(terms, code * length, (code + 1) * length).astype(BF16)
        for code, _ in list(subsets(stage))[::-1]
    ]


def exchange(stage, sent, sizes):
    return [flip(array, flips, sizes) for array, (_, flips) in zip(sent, list(subsets(stage))[::-1])]


def combine_kernel(*refs, terms, pair):
    outs = refs[terms:]
    count, share, modes = refs[0].shape
    each = count // 2 // pair
    for above in range(2):
        for place in range(each):
            rows = pl.ds(above * (count // 2) + place * pair, pair)
            total = refs[0][rows].astype(F32)
            for ref in refs[1:terms]:
                total = total + ref[rows].astype(F32)
            total = total.reshape(pair * share, modes).T
            for swapped in range(2):
                out = outs[2 * above + swapped]
                out[place] = total[swapped * share : (swapped + 1) * share].astype(out.dtype)


def assemble_kernel(own_ref, swapped_ref, above_ref, both_ref, out_ref, *, pair):
    count, share, width = own_ref.shape
    first = lax.axis_index("ma") == 0
    for place in range(count):
        mine = own_ref[place] + above_ref[place].astype(F32)
        theirs = swapped_ref[place].astype(F32) + both_ref[place].astype(F32)
        low = jnp.where(first, mine, theirs)
        high = jnp.where(first, theirs, mine)
        for part in range(pair):
            lanes = slice(part * (width // pair), (part + 1) * (width // pair))
            out_ref[place * pair + part] = jnp.concatenate([low[:, lanes], high[:, lanes]], 1)


def sum_kernel(*refs):
    total = refs[0][...].astype(F32)
    for ref in refs[1:-1]:
        total = total + ref[...].astype(F32)
    refs[-1][...] = total


def summed(terms, count, cost):
    shape = (count, *terms[0].shape[1:])
    whole = pl.BlockSpec(shape, lambda g: (0,) * len(shape))
    return pl.pallas_call(
        sum_kernel,
        grid=(1,),
        out_shape=jax.ShapeDtypeStruct(shape, F32),
        in_specs=[whole] * len(terms),
        out_specs=whole,
        compiler_params=pltpu.CompilerParams(vmem_limit_bytes=16 << 20),
        cost_estimate=pl.CostEstimate(flops=cost, bytes_accessed=1024, transcendentals=0),
    )(*terms)


def finish(terms, count, stage, sizes):
    _, share, modes = terms[0].shape
    pair = 2 if count % 4 == 0 else 1
    places = count // 2 // pair
    shape = (places, share, pair * share)
    whole = lambda shape: pl.BlockSpec(shape, lambda g: (0,) * len(shape))
    parts = pl.pallas_call(
        functools.partial(combine_kernel, terms=len(terms), pair=pair),
        grid=(1,),
        out_shape=[jax.ShapeDtypeStruct(shape, dtype) for dtype in (F32, BF16, BF16, BF16)],
        in_specs=[whole((count, share, modes))] * len(terms),
        out_specs=[whole(shape)] * 4,
        compiler_params=pltpu.CompilerParams(vmem_limit_bytes=16 << 20),
        cost_estimate=pl.CostEstimate(flops=1, bytes_accessed=1024, transcendentals=0),
    )(*terms)
    stage = stage + [("ma", 0)]
    arrived = {code: flip(parts[code], flips, sizes) for code, flips in reversed(list(subsets(stage)))}
    return pl.pallas_call(
        functools.partial(assemble_kernel, pair=pair),
        out_shape=jax.ShapeDtypeStruct((places * pair, share, modes), F32),
        in_specs=[pl.BlockSpec(memory_space=pltpu.VMEM)] * 4,
        out_specs=pl.BlockSpec(memory_space=pltpu.VMEM),
        compiler_params=pltpu.CompilerParams(vmem_limit_bytes=16 << 20),
        cost_estimate=pl.CostEstimate(flops=1, bytes_accessed=1024, transcendentals=0),
    )(parts[0], arrived[1], arrived[2], arrived[3])


def shards(mode_fields, cell_volumes, sizes):
    barrier = lax.optimization_barrier
    own = jnp.transpose(mode_fields, (2, 0, 1, 3))
    row_count, _, share, _ = own.shape
    modes = 2 * share
    quarter = row_count // 4
    all_rows = tuple(range(row_count))
    inner_rows = all_rows[quarter : 3 * quarter]
    outer_rows = all_rows[:quarter] + all_rows[3 * quarter :]
    own_inner = own[quarter : 3 * quarter]
    own_outer = jnp.concatenate([own[:quarter], own[3 * quarter :]], 0)

    other_inner = flip(own_inner, [("ma", 0)], sizes)
    token = flip(own[quarter, 0, :16], [("ma", 0)], sizes)
    edges, token = barrier(((own[:, :, :, -1], own[:, :, :, 0]), token))
    forward, backward = neighbours("gy")
    before = lax.ppermute(edges[0], "gy", forward)
    after = lax.ppermute(edges[1], "gy", backward)
    own_outer_held, before, after = barrier((own_outer, before, after))
    other_outer = flip(own_outer_held, [("ma", 0)], sizes)

    inner = functools.partial(
        partial_tensor, own_inner, other_inner, volumes=cell_volumes, rows=inner_rows, sizes=sizes, blocks=range(BLOCKS)
    )
    so_far = inner(slopes_of(own, inner_rows, (0,)), parts=(0,))
    edges, so_far = barrier(((own[-1:], own[:1]), so_far))
    forward, backward = neighbours("gx")
    above = lax.ppermute(edges[0], "gx", forward)
    below = lax.ppermute(edges[1], "gx", backward)
    before = before.reshape(3 * row_count, share)
    after = after.reshape(3 * row_count, share)
    so_far = inner(slopes_of(own, inner_rows, (1,), before, after, token), parts=(1,), before=so_far)

    slopes_outer = slopes_of(own, outer_rows, (0, 1), before, after, above, below)
    outer = functools.partial(
        partial_tensor, own_outer, other_outer, slopes_outer, rows=outer_rows, sizes=sizes, before=so_far
    )
    stages = stages_of(sizes)
    count = modes // BLOCKS
    cell_count = mode_fields.shape[2] * mode_fields.shape[3]
    sent = outer(cell_volumes, blocks=(5, 6, 7), dtypes=(BF16,))
    cell_volumes, sent = barrier((cell_volumes, sent))
    arrived = flip(sent, stages[0], sizes)
    kept = outer(cell_volumes, blocks=(1, 2, 3))
    sent = [term_sum([kept, arrived], at * count, (at + 1) * count).astype(BF16) for at in range(3)]
    cell_volumes, sent = barrier((cell_volumes, sent))
    received = exchange(stages[1], sent[::-1], sizes)
    sent, kept = outer(cell_volumes, blocks=(4, 0), dtypes=(BF16, F32))
    arrived = flip(sent, stages[0], sizes)
    terms = [summed(received, count, 16 * count * modes * share * cell_count), kept, arrived]
    for stage in stages[2:-1]:
        terms = terms + exchange(stage, sends(terms, count, stage), sizes)
        count = count >> len(stage)
    return finish(terms, count, stages[-1], sizes)


def solution(mesh):
    in_specs = (P(None, "ma", "gx", "gy"), P("gx", "gy"))
    out_specs = P(("gx", "gy"), "ma", None)
    body = functools.partial(shards, sizes=dict(mesh.shape))
    return jax.shard_map(body, mesh=mesh, in_specs=in_specs, out_specs=out_specs, check_vma=False)
```

```python
import functools
import math

import jax
import jax.numpy as jnp
from jax import lax
from jax.experimental import pallas as pl
from jax.experimental.pallas import tpu as pltpu
from jax.sharding import PartitionSpec as P

BF16 = jnp.bfloat16
F32 = jnp.float32
BLOCKS = 8


def bits_of(count):
    return count.bit_length() - 1


def send_order(sizes):
    order = []
    for axis in ("gy", "gx"):
        order += [(axis, bit) for bit in range(bits_of(sizes[axis]))]
    return order


def source_bits(sizes, rows_each):
    row_bits = bits_of(rows_each)
    base = {"gy": row_bits, "gx": row_bits + bits_of(sizes["gy"])}
    found = list(range(row_bits))
    for axis, bit in reversed(send_order(sizes)):
        found.append(base[axis] + bit)
    return found


def slopes_kernel(own_ref, columns_ref, *refs, rows):
    out_ref = refs[-1]
    last = own_ref.shape[0] - 1
    share, cells = own_ref.shape[2:]

    def edge(ref, axis, step):
        at = lax.axis_index(axis) + step
        inside = jnp.logical_and(at >= 0, at < lax.axis_size(axis))
        at = jnp.clip(at, 0, lax.axis_size(axis) - 1)
        values = ref[at, 0 if step < 0 else 1].astype(F32)
        return jnp.where(inside, values, jnp.zeros_like(values))

    before, after = edge(columns_ref, "gy", -1).T, edge(columns_ref, "gy", 1).T
    above = edge(refs[0], "gx", -1) if 0 in rows else None
    below = edge(refs[0], "gx", 1) if last in rows else None
    lane = lax.broadcasted_iota(jnp.int32, (share, cells), 1)
    for place, x in enumerate(rows):
        for a in range(3):
            down = above[a] if x == 0 else own_ref[x - 1, a].astype(F32)
            up = below[a] if x == last else own_ref[x + 1, a].astype(F32)
            out_ref[place, a] = ((up - down) * 0.5).astype(BF16)
            value = own_ref[x, a].astype(F32)
            column = 3 * x + a
            down = jnp.where(lane == 0, before[:, column : column + 1], pltpu.roll(value, 1, 1))
            up = jnp.where(lane == cells - 1, after[:, column : column + 1], pltpu.roll(value, cells - 1, 1))
            out_ref[place, 3 + a] = ((up - down) * 0.5).astype(BF16)


def slopes_of(own, rows, *edges):
    _, _, share, cells = own.shape
    return pl.pallas_call(
        functools.partial(slopes_kernel, rows=rows),
        out_shape=jax.ShapeDtypeStruct((len(rows), 6, share, cells), BF16),
        in_specs=[pl.BlockSpec(memory_space=pltpu.VMEM)] * (1 + len(edges)),
        out_specs=pl.BlockSpec(memory_space=pltpu.VMEM),
        compiler_params=pltpu.CompilerParams(vmem_limit_bytes=16 << 20),
        cost_estimate=pl.CostEstimate(flops=1, bytes_accessed=1024, transcendentals=0),
    )(own, *edges)


def sum_of(left, right):
    return left[0] * right[0] + left[1] * right[1] + left[2] * right[2]


def tensor_kernel(*refs, bits, block, rows_each, first_block, stride, rows, scale, parts, outputs):
    own_ref, other_ref, slope_ref, volume_ref = refs[:4]
    left, right = refs[-2:]
    out_refs = refs[-2 - outputs : -2]
    before_ref = refs[4] if len(refs) == 7 + outputs else None
    row_count, _, share, cells = own_ref.shape
    step = pl.program_id(0)
    top = bits_of(2 * share) - 1

    @pl.when(step == 0)
    def _():
        for x in range(row_count):
            weight = volume_ref[pl.ds(rows[x], 1), :] * scale
            for half, ref in enumerate((own_ref, other_ref)):
                for a in range(3):
                    value = (weight * ref[x, a].astype(F32)).astype(BF16)
                    left[x, a, half * share : (half + 1) * share, :] = value.astype(F32)
                for place, b in enumerate(parts):
                    lanes = len(parts) * x + place
                    right[half * share : (half + 1) * share, lanes * cells : (lanes + 1) * cells] = ref[x, b]

    here = (lax.axis_index("gx") * lax.axis_size("gy") + lax.axis_index("gy")) * rows_each
    start = here ^ (lax.axis_index("ma") << top)
    position = (first_block + stride * step) * block
    for place, bit in enumerate(bits):
        start = start ^ (((position >> place) & 1) << bit)
    columns = []
    for x in range(row_count):
        slopes = [slope_ref[x, n] for n in range(3 * len(parts))]
        sums = [[] for _ in parts]
        for row in range(block):
            offset = 0
            for place, bit in enumerate(bits):
                offset |= ((row >> place) & 1) << bit
            test = [
                jnp.concatenate(
                    [left[x, a, pl.ds(start ^ offset, 16, stride=0), :].astype(BF16)] * (share // 16), 0
                )
                for a in range(3)
            ]
            for place, found in enumerate(sums):
                found.append(sum_of(test, slopes[3 * place : 3 * place + 3]))
        columns += [jnp.concatenate(found, 0) for found in sums]
    sums = jnp.concatenate(columns, 1)
    product = lax.dot_general(sums, right[...], (((1,), (1,)), ((), ())), preferred_element_type=F32)
    product = product.reshape(block, share, 2 * share)
    if before_ref is not None:
        product = product + before_ref[...]
    if outputs == 1:
        out_refs[0][...] = product.astype(out_refs[0].dtype)
    else:
        for place, out_ref in enumerate(out_refs):

            @pl.when(step == place)
            def _(out_ref=out_ref):
                out_ref[...] = product.astype(out_ref.dtype)


def partial_tensor(own, other, slopes, volumes, rows, sizes, blocks, before=None, dtypes=(F32,), parts=(0, 1)):
    row_count, _, share, cells = own.shape
    modes = 2 * share
    block = modes // BLOCKS
    stride = blocks[1] - blocks[0] if len(blocks) > 1 else 1
    outputs = len(dtypes)
    devices = sizes["gx"] * sizes["gy"]
    rows_each = modes // devices
    body = functools.partial(
        tensor_kernel,
        bits=source_bits(sizes, rows_each),
        block=block,
        rows_each=rows_each,
        first_block=blocks[0],
        stride=stride,
        outputs=outputs,
        rows=rows,
        parts=parts,
        scale=1.0 / math.sqrt(volumes.shape[0] * volumes.shape[1] * devices),
    )
    whole = lambda array: pl.BlockSpec(array.shape, lambda g: (0,) * array.ndim, pipeline_mode=pl.Buffered(1))
    shape = (block, share, modes)
    operands = [own, other, slopes, volumes]
    in_specs = [whole(array) for array in operands]
    if before is not None:
        operands.append(before)
        in_specs.append(pl.BlockSpec(shape, lambda g: (blocks[0] + stride * g, 0, 0)))
    if outputs > 1:
        out_shape = [jax.ShapeDtypeStruct(shape, dtype) for dtype in dtypes]
        out_specs = [pl.BlockSpec(shape, lambda g: (0, 0, 0))] * outputs
    else:
        out_shape = (pltpu.VMEM if len(blocks) == BLOCKS else jax.ShapeDtypeStruct)(
            (len(blocks) * block, share, modes), dtypes[0]
        )
        out_specs = pl.BlockSpec(shape, lambda g: (g, 0, 0))
    return pl.pallas_call(
        body,
        grid=(len(blocks),),
        out_shape=out_shape,
        in_specs=in_specs,
        out_specs=out_specs,
        scratch_shapes=[
            pltpu.VMEM((row_count, 3, modes, cells), F32),
            pltpu.VMEM((modes, row_count * len(parts) * cells), BF16),
        ],
        compiler_params=pltpu.CompilerParams(vmem_limit_bytes=20 << 20),
        cost_estimate=pl.CostEstimate(
            flops=4 * len(parts) * len(blocks) * block * share * modes * row_count * cells, bytes_accessed=4 << 20, transcendentals=0
        ),
    )(*operands)


def neighbours(axis):
    count = lax.axis_size(axis)
    forward = [(i, i + 1) for i in range(count - 1)]
    return forward, [(target, source) for source, target in forward]


def flip(array, flips, sizes):
    axes = tuple(sorted({axis for axis, _ in flips}, key=("gx", "gy", "ma").index))
    strides = {}
    count = 1
    for axis in reversed(axes):
        strides[axis] = count
        count *= sizes[axis]
    change = 0
    for axis, bit in flips:
        change |= strides[axis] << bit
    return lax.ppermute(array, axes, [(i, i ^ change) for i in range(count)])


def subsets(stage):
    for code in range(1, 1 << len(stage)):
        yield code, [stage[n] for n in range(len(stage)) if (code >> (len(stage) - 1 - n)) & 1]


def stages_of(sizes):
    order = send_order(sizes)
    return [[order[0]], order[1:3]] + [[entry] for entry in order[3:]]


def term_sum(terms, low, high):
    total = terms[0][low:high].astype(F32)
    for array in terms[1:]:
        total = total + array[low:high].astype(F32)
    return total


def sends(terms, count, stage):
    length = count >> len(stage)
    return [
        term_sum(terms, code * length, (code + 1) * length).astype(BF16)
        for code, _ in list(subsets(stage))[::-1]
    ]


def exchange(stage, sent, sizes):
    return [flip(array, flips, sizes) for array, (_, flips) in zip(sent, list(subsets(stage))[::-1])]


def combine_kernel(*refs, terms, pair):
    outs = refs[terms:]
    count, share, modes = refs[0].shape
    each = count // 2 // pair
    for above in range(2):
        for place in range(each):
            rows = pl.ds(above * (count // 2) + place * pair, pair)
            total = refs[0][rows].astype(F32)
            for ref in refs[1:terms]:
                total = total + ref[rows].astype(F32)
            total = total.reshape(pair * share, modes).T
            for swapped in range(2):
                out = outs[2 * above + swapped]
                out[place] = total[swapped * share : (swapped + 1) * share].astype(out.dtype)


def assemble_kernel(own_ref, swapped_ref, above_ref, both_ref, out_ref, *, pair):
    count, share, width = own_ref.shape
    first = lax.axis_index("ma") == 0
    for place in range(count):
        mine = own_ref[place] + above_ref[place].astype(F32)
        theirs = swapped_ref[place].astype(F32) + both_ref[place].astype(F32)
        low = jnp.where(first, mine, theirs)
        high = jnp.where(first, theirs, mine)
        for part in range(pair):
            lanes = slice(part * (width // pair), (part + 1) * (width // pair))
            out_ref[place * pair + part] = jnp.concatenate([low[:, lanes], high[:, lanes]], 1)


def sum_kernel(*refs):
    total = refs[0][...].astype(F32)
    for ref in refs[1:-1]:
        total = total + ref[...].astype(F32)
    refs[-1][...] = total


def summed(terms, count, cost):
    shape = (count, *terms[0].shape[1:])
    whole = pl.BlockSpec(shape, lambda g: (0,) * len(shape))
    return pl.pallas_call(
        sum_kernel,
        grid=(1,),
        out_shape=jax.ShapeDtypeStruct(shape, F32),
        in_specs=[whole] * len(terms),
        out_specs=whole,
        compiler_params=pltpu.CompilerParams(vmem_limit_bytes=16 << 20),
        cost_estimate=pl.CostEstimate(flops=cost, bytes_accessed=1024, transcendentals=0),
    )(*terms)


def finish(terms, count, stage, sizes):
    _, share, modes = terms[0].shape
    pair = 2 if count % 4 == 0 else 1
    places = count // 2 // pair
    shape = (places, share, pair * share)
    whole = lambda shape: pl.BlockSpec(shape, lambda g: (0,) * len(shape))
    parts = pl.pallas_call(
        functools.partial(combine_kernel, terms=len(terms), pair=pair),
        grid=(1,),
        out_shape=[jax.ShapeDtypeStruct(shape, dtype) for dtype in (F32, BF16, BF16, BF16)],
        in_specs=[whole((count, share, modes))] * len(terms),
        out_specs=[whole(shape)] * 4,
        compiler_params=pltpu.CompilerParams(vmem_limit_bytes=16 << 20),
        cost_estimate=pl.CostEstimate(flops=1, bytes_accessed=1024, transcendentals=0),
    )(*terms)
    stage = stage + [("ma", 0)]
    arrived = {code: flip(parts[code], flips, sizes) for code, flips in reversed(list(subsets(stage)))}
    return pl.pallas_call(
        functools.partial(assemble_kernel, pair=pair),
        out_shape=jax.ShapeDtypeStruct((places * pair, share, modes), F32),
        in_specs=[pl.BlockSpec(memory_space=pltpu.VMEM)] * 4,
        out_specs=pl.BlockSpec(memory_space=pltpu.VMEM),
        compiler_params=pltpu.CompilerParams(vmem_limit_bytes=16 << 20),
        cost_estimate=pl.CostEstimate(flops=1, bytes_accessed=1024, transcendentals=0),
    )(parts[0], arrived[1], arrived[2], arrived[3])


def shards(mode_fields, cell_volumes, sizes):
    barrier = lax.optimization_barrier
    own = jnp.transpose(mode_fields, (2, 0, 1, 3))
    row_count, _, share, _ = own.shape
    modes = 2 * share
    quarter = row_count // 4
    all_rows = tuple(range(row_count))
    inner_rows = all_rows[quarter : 3 * quarter]
    outer_rows = all_rows[:quarter] + all_rows[3 * quarter :]
    own_inner = own[quarter : 3 * quarter]
    own_outer = jnp.concatenate([own[:quarter], own[3 * quarter :]], 0)

    other_inner = flip(own_inner, [("ma", 0)], sizes)
    columns = jnp.stack([own[:, :, :, -1], own[:, :, :, 0]]).reshape(2, 3 * row_count, share)
    columns = lax.all_gather(columns, "gy")
    edge_rows = lax.all_gather(jnp.stack([own[-1], own[0]]), "gx")
    own_outer_held, columns = barrier((own_outer, columns))
    other_outer = flip(own_outer_held, [("ma", 0)], sizes)

    so_far = partial_tensor(
        own_inner,
        other_inner,
        slopes_of(own, inner_rows, columns),
        cell_volumes,
        inner_rows,
        sizes,
        range(BLOCKS),
    )
    edge_rows, so_far = barrier((edge_rows, so_far))
    slopes_outer = slopes_of(own, outer_rows, columns, edge_rows)
    outer = functools.partial(
        partial_tensor, own_outer, other_outer, slopes_outer, rows=outer_rows, sizes=sizes, before=so_far
    )
    stages = stages_of(sizes)
    count = modes // BLOCKS
    cell_count = mode_fields.shape[2] * mode_fields.shape[3]
    sent = outer(cell_volumes, blocks=(4, 5, 6, 7), dtypes=(BF16,))
    cell_volumes, sent = barrier((cell_volumes, sent))
    arrived = flip(sent, stages[0], sizes)
    upper = outer(cell_volumes, blocks=(2, 3))
    upper_terms = [upper, arrived[2 * count :]]
    sent = [term_sum(upper_terms, at * count, (at + 1) * count).astype(BF16) for at in range(2)]
    cell_volumes, sent = barrier((cell_volumes, sent))
    lower = outer(cell_volumes, blocks=(0, 1))
    sent = [term_sum([lower, arrived], count, 2 * count).astype(BF16)] + sent
    received = exchange(stages[1], sent[::-1], sizes)
    cost = 16 * count * modes * share * cell_count
    terms = [summed([lower, arrived] + received[:2], count, cost), received[2]]
    for stage in stages[2:-1]:
        terms = terms + exchange(stage, sends(terms, count, stage), sizes)
        count = count >> len(stage)
    return finish(terms, count, stages[-1], sizes)


def solution(mesh):
    in_specs = (P(None, "ma", "gx", "gy"), P("gx", "gy"))
    out_specs = P(("gx", "gy"), "ma", None)
    body = functools.partial(shards, sizes=dict(mesh.shape))
    return jax.shard_map(body, mesh=mesh, in_specs=in_specs, out_specs=out_specs, check_vma=False)
```

```python
import functools
import math

import jax
import jax.numpy as jnp
from jax import lax
from jax.experimental import pallas as pl
from jax.experimental.pallas import tpu as pltpu
from jax.sharding import PartitionSpec as P

BF16 = jnp.bfloat16
F32 = jnp.float32
BLOCKS = 8


def bits_of(count):
    return count.bit_length() - 1


def send_order(sizes):
    order = []
    for axis in ("gy", "gx"):
        order += [(axis, bit) for bit in range(bits_of(sizes[axis]))]
    return order


def source_bits(sizes, rows_each):
    row_bits = bits_of(rows_each)
    base = {"gy": row_bits, "gx": row_bits + bits_of(sizes["gy"])}
    found = list(range(row_bits))
    for axis, bit in reversed(send_order(sizes)):
        found.append(base[axis] + bit)
    return found


def slopes_kernel(own_ref, columns_ref, *refs, rows):
    out_ref = refs[-1]
    last = own_ref.shape[0] - 1
    share, cells = own_ref.shape[2:]

    def edge(step):
        count = columns_ref.shape[0]
        at = lax.axis_index("gy") + step
        inside = jnp.logical_and(at >= 0, at < count)
        values = columns_ref[jnp.clip(at, 0, count - 1), 0 if step < 0 else 1].astype(F32)
        return jnp.where(inside, values, jnp.zeros_like(values)).T

    before, after = edge(-1), edge(1)
    above_ref, below_ref = refs[:2] if len(refs) > 1 else (None, None)
    lane = lax.broadcasted_iota(jnp.int32, (share, cells), 1)
    for place, x in enumerate(rows):
        for a in range(3):
            down = (above_ref[0, a] if x == 0 else own_ref[x - 1, a]).astype(F32)
            up = (below_ref[0, a] if x == last else own_ref[x + 1, a]).astype(F32)
            out_ref[place, a] = ((up - down) * 0.5).astype(BF16)
            value = own_ref[x, a].astype(F32)
            column = 3 * x + a
            down = jnp.where(lane == 0, before[:, column : column + 1], pltpu.roll(value, 1, 1))
            up = jnp.where(lane == cells - 1, after[:, column : column + 1], pltpu.roll(value, cells - 1, 1))
            out_ref[place, 3 + a] = ((up - down) * 0.5).astype(BF16)


def slopes_of(own, rows, *edges):
    _, _, share, cells = own.shape
    return pl.pallas_call(
        functools.partial(slopes_kernel, rows=rows),
        out_shape=jax.ShapeDtypeStruct((len(rows), 6, share, cells), BF16),
        in_specs=[pl.BlockSpec(memory_space=pltpu.VMEM)] * (1 + len(edges)),
        out_specs=pl.BlockSpec(memory_space=pltpu.VMEM),
        compiler_params=pltpu.CompilerParams(vmem_limit_bytes=16 << 20),
        cost_estimate=pl.CostEstimate(flops=1, bytes_accessed=1024, transcendentals=0),
    )(own, *edges)


def sum_of(left, right):
    return left[0] * right[0] + left[1] * right[1] + left[2] * right[2]


def tensor_kernel(*refs, bits, block, rows_each, first_block, stride, rows, scale, parts, outputs):
    own_ref, other_ref, slope_ref, volume_ref = refs[:4]
    left, right = refs[-2:]
    out_refs = refs[-2 - outputs : -2]
    before_ref = refs[4] if len(refs) == 7 + outputs else None
    row_count, _, share, cells = own_ref.shape
    step = pl.program_id(0)
    top = bits_of(2 * share) - 1

    @pl.when(step == 0)
    def _():
        for x in range(row_count):
            weight = volume_ref[pl.ds(rows[x], 1), :] * scale
            for half, ref in enumerate((own_ref, other_ref)):
                for a in range(3):
                    value = (weight * ref[x, a].astype(F32)).astype(BF16)
                    left[x, a, half * share : (half + 1) * share, :] = value.astype(F32)
                for place, b in enumerate(parts):
                    lanes = len(parts) * x + place
                    right[half * share : (half + 1) * share, lanes * cells : (lanes + 1) * cells] = ref[x, b]

    here = (lax.axis_index("gx") * lax.axis_size("gy") + lax.axis_index("gy")) * rows_each
    start = here ^ (lax.axis_index("ma") << top)
    position = (first_block + stride * step) * block
    for place, bit in enumerate(bits):
        start = start ^ (((position >> place) & 1) << bit)
    columns = []
    for x in range(row_count):
        slopes = [slope_ref[x, n] for n in range(3 * len(parts))]
        sums = [[] for _ in parts]
        for row in range(block):
            offset = 0
            for place, bit in enumerate(bits):
                offset |= ((row >> place) & 1) << bit
            test = [
                jnp.concatenate(
                    [left[x, a, pl.ds(start ^ offset, 16, stride=0), :].astype(BF16)] * (share // 16), 0
                )
                for a in range(3)
            ]
            for place, found in enumerate(sums):
                found.append(sum_of(test, slopes[3 * place : 3 * place + 3]))
        columns += [jnp.concatenate(found, 0) for found in sums]
    sums = jnp.concatenate(columns, 1)
    product = lax.dot_general(sums, right[...], (((1,), (1,)), ((), ())), preferred_element_type=F32)
    product = product.reshape(block, share, 2 * share)
    if before_ref is not None:
        product = product + before_ref[...]
    if outputs == 1:
        out_refs[0][...] = product.astype(out_refs[0].dtype)
    else:
        for place, out_ref in enumerate(out_refs):

            @pl.when(step == place)
            def _(out_ref=out_ref):
                out_ref[...] = product.astype(out_ref.dtype)


def partial_tensor(own, other, slopes, volumes, rows, sizes, blocks, before=None, dtypes=(F32,), parts=(0, 1)):
    row_count, _, share, cells = own.shape
    modes = 2 * share
    block = modes // BLOCKS
    stride = blocks[1] - blocks[0] if len(blocks) > 1 else 1
    outputs = len(dtypes)
    devices = sizes["gx"] * sizes["gy"]
    rows_each = modes // devices
    body = functools.partial(
        tensor_kernel,
        bits=source_bits(sizes, rows_each),
        block=block,
        rows_each=rows_each,
        first_block=blocks[0],
        stride=stride,
        outputs=outputs,
        rows=rows,
        parts=parts,
        scale=1.0 / math.sqrt(volumes.shape[0] * volumes.shape[1] * devices),
    )
    whole = lambda array: pl.BlockSpec(array.shape, lambda g: (0,) * array.ndim, pipeline_mode=pl.Buffered(1))
    shape = (block, share, modes)
    operands = [own, other, slopes, volumes]
    in_specs = [whole(array) for array in operands]
    if before is not None:
        operands.append(before)
        in_specs.append(pl.BlockSpec(shape, lambda g: (blocks[0] + stride * g, 0, 0)))
    if outputs > 1:
        out_shape = [jax.ShapeDtypeStruct(shape, dtype) for dtype in dtypes]
        out_specs = [pl.BlockSpec(shape, lambda g: (0, 0, 0))] * outputs
    else:
        out_shape = (pltpu.VMEM if len(blocks) == BLOCKS else jax.ShapeDtypeStruct)(
            (len(blocks) * block, share, modes), dtypes[0]
        )
        out_specs = pl.BlockSpec(shape, lambda g: (g, 0, 0))
    return pl.pallas_call(
        body,
        grid=(len(blocks),),
        out_shape=out_shape,
        in_specs=in_specs,
        out_specs=out_specs,
        scratch_shapes=[
            pltpu.VMEM((row_count, 3, modes, cells), F32),
            pltpu.VMEM((modes, row_count * len(parts) * cells), BF16),
        ],
        compiler_params=pltpu.CompilerParams(vmem_limit_bytes=20 << 20),
        cost_estimate=pl.CostEstimate(
            flops=4 * len(parts) * len(blocks) * block * share * modes * row_count * cells, bytes_accessed=4 << 20, transcendentals=0
        ),
    )(*operands)


def neighbours(axis):
    count = lax.axis_size(axis)
    forward = [(i, i + 1) for i in range(count - 1)]
    return forward, [(target, source) for source, target in forward]


def flip(array, flips, sizes):
    axes = tuple(sorted({axis for axis, _ in flips}, key=("gx", "gy", "ma").index))
    strides = {}
    count = 1
    for axis in reversed(axes):
        strides[axis] = count
        count *= sizes[axis]
    change = 0
    for axis, bit in flips:
        change |= strides[axis] << bit
    return lax.ppermute(array, axes, [(i, i ^ change) for i in range(count)])


def subsets(stage):
    for code in range(1, 1 << len(stage)):
        yield code, [stage[n] for n in range(len(stage)) if (code >> (len(stage) - 1 - n)) & 1]


def stages_of(sizes):
    order = send_order(sizes)
    return [[order[0]], order[1:3]] + [[entry] for entry in order[3:]]


def term_sum(terms, low, high):
    total = terms[0][low:high].astype(F32)
    for array in terms[1:]:
        total = total + array[low:high].astype(F32)
    return total


def sends(terms, count, stage):
    length = count >> len(stage)
    return [
        term_sum(terms, code * length, (code + 1) * length).astype(BF16)
        for code, _ in list(subsets(stage))[::-1]
    ]


def exchange(stage, sent, sizes):
    return [flip(array, flips, sizes) for array, (_, flips) in zip(sent, list(subsets(stage))[::-1])]


def combine_kernel(*refs, terms, pair):
    outs = refs[terms:]
    count, share, modes = refs[0].shape
    each = count // 2 // pair
    for above in range(2):
        for place in range(each):
            rows = pl.ds(above * (count // 2) + place * pair, pair)
            total = refs[0][rows].astype(F32)
            for ref in refs[1:terms]:
                total = total + ref[rows].astype(F32)
            total = total.reshape(pair * share, modes).T
            for swapped in range(2):
                out = outs[2 * above + swapped]
                out[place] = total[swapped * share : (swapped + 1) * share].astype(out.dtype)


def assemble_kernel(own_ref, swapped_ref, above_ref, both_ref, out_ref, *, pair):
    count, share, width = own_ref.shape
    first = lax.axis_index("ma") == 0
    for place in range(count):
        mine = own_ref[place] + above_ref[place].astype(F32)
        theirs = swapped_ref[place].astype(F32) + both_ref[place].astype(F32)
        low = jnp.where(first, mine, theirs)
        high = jnp.where(first, theirs, mine)
        for part in range(pair):
            lanes = slice(part * (width // pair), (part + 1) * (width // pair))
            out_ref[place * pair + part] = jnp.concatenate([low[:, lanes], high[:, lanes]], 1)


def sum_kernel(*refs):
    total = refs[0][...].astype(F32)
    for ref in refs[1:-1]:
        total = total + ref[...].astype(F32)
    refs[-1][...] = total


def summed(terms, count, cost):
    shape = (count, *terms[0].shape[1:])
    whole = pl.BlockSpec(shape, lambda g: (0,) * len(shape))
    return pl.pallas_call(
        sum_kernel,
        grid=(1,),
        out_shape=jax.ShapeDtypeStruct(shape, F32),
        in_specs=[whole] * len(terms),
        out_specs=whole,
        compiler_params=pltpu.CompilerParams(vmem_limit_bytes=16 << 20),
        cost_estimate=pl.CostEstimate(flops=cost, bytes_accessed=1024, transcendentals=0),
    )(*terms)


def finish(terms, count, stage, sizes):
    _, share, modes = terms[0].shape
    pair = 2 if count % 4 == 0 else 1
    places = count // 2 // pair
    shape = (places, share, pair * share)
    whole = lambda shape: pl.BlockSpec(shape, lambda g: (0,) * len(shape))
    parts = pl.pallas_call(
        functools.partial(combine_kernel, terms=len(terms), pair=pair),
        grid=(1,),
        out_shape=[jax.ShapeDtypeStruct(shape, dtype) for dtype in (F32, BF16, BF16, BF16)],
        in_specs=[whole((count, share, modes))] * len(terms),
        out_specs=[whole(shape)] * 4,
        compiler_params=pltpu.CompilerParams(vmem_limit_bytes=16 << 20),
        cost_estimate=pl.CostEstimate(flops=1, bytes_accessed=1024, transcendentals=0),
    )(*terms)
    stage = stage + [("ma", 0)]
    arrived = {code: flip(parts[code], flips, sizes) for code, flips in reversed(list(subsets(stage)))}
    return pl.pallas_call(
        functools.partial(assemble_kernel, pair=pair),
        out_shape=jax.ShapeDtypeStruct((places * pair, share, modes), F32),
        in_specs=[pl.BlockSpec(memory_space=pltpu.VMEM)] * 4,
        out_specs=pl.BlockSpec(memory_space=pltpu.VMEM),
        compiler_params=pltpu.CompilerParams(vmem_limit_bytes=16 << 20),
        cost_estimate=pl.CostEstimate(flops=1, bytes_accessed=1024, transcendentals=0),
    )(parts[0], arrived[1], arrived[2], arrived[3])


def shards(mode_fields, cell_volumes, sizes):
    barrier = lax.optimization_barrier
    own = jnp.transpose(mode_fields, (2, 0, 1, 3))
    row_count, _, share, _ = own.shape
    modes = 2 * share
    quarter = row_count // 4
    all_rows = tuple(range(row_count))
    inner_rows = all_rows[quarter : 3 * quarter]
    outer_rows = all_rows[:quarter] + all_rows[3 * quarter :]
    own_inner = own[quarter : 3 * quarter]
    own_outer = jnp.concatenate([own[:quarter], own[3 * quarter :]], 0)

    other_inner = flip(own_inner, [("ma", 0)], sizes)
    columns = jnp.stack([own[:, :, :, -1], own[:, :, :, 0]]).reshape(2, 3 * row_count, share)
    columns = lax.all_gather(columns, "gy")
    own_outer_held, edges, columns = barrier((own_outer, (own[-1:], own[:1]), columns))
    forward, backward = neighbours("gx")
    above = lax.ppermute(edges[0], "gx", forward)
    below = lax.ppermute(edges[1], "gx", backward)
    other_outer = flip(own_outer_held, [("ma", 0)], sizes)

    so_far = partial_tensor(
        own_inner,
        other_inner,
        slopes_of(own, inner_rows, columns),
        cell_volumes,
        inner_rows,
        sizes,
        range(BLOCKS),
    )
    columns, so_far = barrier((columns, so_far))
    slopes_outer = slopes_of(own, outer_rows, columns, above, below)
    outer = functools.partial(
        partial_tensor, own_outer, other_outer, slopes_outer, rows=outer_rows, sizes=sizes, before=so_far
    )
    stages = stages_of(sizes)
    count = modes // BLOCKS
    cell_count = mode_fields.shape[2] * mode_fields.shape[3]
    sent = outer(cell_volumes, blocks=(4, 5, 6, 7), dtypes=(BF16,))
    cell_volumes, sent = barrier((cell_volumes, sent))
    arrived = flip(sent, stages[0], sizes)
    upper = outer(cell_volumes, blocks=(2, 3))
    upper_terms = [upper, arrived[2 * count :]]
    sent = [term_sum(upper_terms, at * count, (at + 1) * count).astype(BF16) for at in range(2)]
    cell_volumes, sent = barrier((cell_volumes, sent))
    lower = outer(cell_volumes, blocks=(0, 1))
    sent = [term_sum([lower, arrived], count, 2 * count).astype(BF16)] + sent
    received = exchange(stages[1], sent[::-1], sizes)
    cost = 16 * count * modes * share * cell_count
    terms = [summed([lower, arrived] + received[:2], count, cost), received[2]]
    for stage in stages[2:-1]:
        terms = terms + exchange(stage, sends(terms, count, stage), sizes)
        count = count >> len(stage)
    return finish(terms, count, stages[-1], sizes)


def solution(mesh):
    in_specs = (P(None, "ma", "gx", "gy"), P("gx", "gy"))
    out_specs = P(("gx", "gy"), "ma", None)
    body = functools.partial(shards, sizes=dict(mesh.shape))
    return jax.shard_map(body, mesh=mesh, in_specs=in_specs, out_specs=out_specs, check_vma=False)
```

```python
import functools
import math

import jax
import jax.numpy as jnp
from jax import lax
from jax.experimental import pallas as pl
from jax.experimental.pallas import tpu as pltpu
from jax.sharding import PartitionSpec as P

BF16 = jnp.bfloat16
F32 = jnp.float32
BLOCKS = 8


def bits_of(count):
    return count.bit_length() - 1


def send_order(sizes):
    order = []
    for axis in ("gy", "gx"):
        order += [(axis, bit) for bit in range(bits_of(sizes[axis]))]
    return order


def source_bits(sizes, rows_each):
    row_bits = bits_of(rows_each)
    base = {"gy": row_bits, "gx": row_bits + bits_of(sizes["gy"])}
    found = list(range(row_bits))
    for axis, bit in reversed(send_order(sizes)):
        found.append(base[axis] + bit)
    return found


def slopes_kernel(own_ref, columns_ref, *refs, rows):
    out_ref = refs[-1]
    last = own_ref.shape[0] - 1
    share, cells = own_ref.shape[2:]

    def edge(step):
        count = columns_ref.shape[0]
        at = lax.axis_index("gy") + step
        inside = jnp.logical_and(at >= 0, at < count)
        values = columns_ref[jnp.clip(at, 0, count - 1), 0 if step < 0 else 1].astype(F32)
        return jnp.where(inside, values, jnp.zeros_like(values)).T

    before, after = edge(-1), edge(1)
    here = lax.axis_index("gx")

    def outside(ref, edge_of_grid, a):
        values = ref[0, a].astype(F32)
        return jnp.where(here == edge_of_grid, jnp.zeros_like(values), values)

    lane = lax.broadcasted_iota(jnp.int32, (share, cells), 1)
    for place, x in enumerate(rows):
        for a in range(3):
            down = outside(refs[0], 0, a) if x == 0 else own_ref[x - 1, a].astype(F32)
            up = outside(refs[1], lax.axis_size("gx") - 1, a) if x == last else own_ref[x + 1, a].astype(F32)
            out_ref[place, a] = ((up - down) * 0.5).astype(BF16)
            value = own_ref[x, a].astype(F32)
            column = 3 * x + a
            down = jnp.where(lane == 0, before[:, column : column + 1], pltpu.roll(value, 1, 1))
            up = jnp.where(lane == cells - 1, after[:, column : column + 1], pltpu.roll(value, cells - 1, 1))
            out_ref[place, 3 + a] = ((up - down) * 0.5).astype(BF16)


def slopes_of(own, rows, *edges):
    _, _, share, cells = own.shape
    return pl.pallas_call(
        functools.partial(slopes_kernel, rows=rows),
        out_shape=jax.ShapeDtypeStruct((len(rows), 6, share, cells), BF16),
        in_specs=[pl.BlockSpec(memory_space=pltpu.VMEM)] * (1 + len(edges)),
        out_specs=pl.BlockSpec(memory_space=pltpu.VMEM),
        compiler_params=pltpu.CompilerParams(vmem_limit_bytes=16 << 20),
        cost_estimate=pl.CostEstimate(flops=1, bytes_accessed=1024, transcendentals=0),
    )(own, *edges)


def sum_of(left, right):
    return left[0] * right[0] + left[1] * right[1] + left[2] * right[2]


def tensor_kernel(*refs, bits, block, rows_each, blocks, rows, scale, parts, outputs):
    own_ref, other_ref, slope_ref, volume_ref = refs[:4]
    left, right = refs[-2:]
    out_refs = refs[-2 - outputs : -2]
    before_ref = refs[4] if len(refs) == 7 + outputs else None
    row_count, _, share, cells = own_ref.shape
    step = pl.program_id(0)
    top = bits_of(2 * share) - 1

    @pl.when(step == 0)
    def _():
        for x in range(row_count):
            weight = volume_ref[pl.ds(rows[x], 1), :] * scale
            for half, ref in enumerate((own_ref, other_ref)):
                for a in range(3):
                    value = (weight * ref[x, a].astype(F32)).astype(BF16)
                    left[x, a, half * share : (half + 1) * share, :] = value.astype(F32)
                for place, b in enumerate(parts):
                    lanes = len(parts) * x + place
                    right[half * share : (half + 1) * share, lanes * cells : (lanes + 1) * cells] = ref[x, b]

    here = (lax.axis_index("gx") * lax.axis_size("gy") + lax.axis_index("gy")) * rows_each
    start = here ^ (lax.axis_index("ma") << top)
    position = block_at(blocks, step) * block
    for place, bit in enumerate(bits):
        start = start ^ (((position >> place) & 1) << bit)
    columns = []
    for x in range(row_count):
        slopes = [slope_ref[x, n] for n in range(3 * len(parts))]
        sums = [[] for _ in parts]
        for row in range(block):
            offset = 0
            for place, bit in enumerate(bits):
                offset |= ((row >> place) & 1) << bit
            test = [
                jnp.concatenate(
                    [left[x, a, pl.ds(start ^ offset, 16, stride=0), :].astype(BF16)] * (share // 16), 0
                )
                for a in range(3)
            ]
            for place, found in enumerate(sums):
                found.append(sum_of(test, slopes[3 * place : 3 * place + 3]))
        columns += [jnp.concatenate(found, 0) for found in sums]
    sums = jnp.concatenate(columns, 1)
    product = lax.dot_general(sums, right[...], (((1,), (1,)), ((), ())), preferred_element_type=F32)
    product = product.reshape(block, share, 2 * share)
    if before_ref is not None:
        product = product + before_ref[...]
    if outputs == 1:
        out_refs[0][...] = product.astype(out_refs[0].dtype)
    else:
        for place, out_ref in enumerate(out_refs):

            @pl.when(step == place)
            def _(out_ref=out_ref):
                out_ref[...] = product.astype(out_ref.dtype)


def block_at(blocks, step):
    block = blocks[0] + step
    for n in range(1, len(blocks)):
        jump = blocks[n] - blocks[n - 1] - 1
        if jump:
            block = block + jnp.where(step >= n, jump, 0)
    return block


def partial_tensor(
    own, other, slopes, volumes, rows, sizes, blocks, before=None, first=0, dtypes=(F32,), cost=8
):
    row_count, _, share, cells = own.shape
    modes = 2 * share
    block = modes // BLOCKS
    parts = (0, 1)
    outputs = len(dtypes)
    devices = sizes["gx"] * sizes["gy"]
    rows_each = modes // devices
    body = functools.partial(
        tensor_kernel,
        bits=source_bits(sizes, rows_each),
        block=block,
        rows_each=rows_each,
        blocks=blocks,
        outputs=outputs,
        rows=rows,
        parts=parts,
        scale=1.0 / math.sqrt(volumes.shape[0] * volumes.shape[1] * devices),
    )
    whole = lambda array: pl.BlockSpec(array.shape, lambda g: (0,) * array.ndim, pipeline_mode=pl.Buffered(1))
    shape = (block, share, modes)
    operands = [own, other, slopes, volumes]
    in_specs = [whole(array) for array in operands]
    if before is not None:
        operands.append(before)
        in_specs.append(pl.BlockSpec(shape, lambda g: (first + g, 0, 0)))
    if outputs > 1:
        out_shape = [jax.ShapeDtypeStruct(shape, dtype) for dtype in dtypes]
        out_specs = [pl.BlockSpec(shape, lambda g: (0, 0, 0))] * outputs
    else:
        out_shape = (pltpu.VMEM if before is None else jax.ShapeDtypeStruct)(
            (len(blocks) * block, share, modes), dtypes[0]
        )
        out_specs = pl.BlockSpec(shape, lambda g: (g, 0, 0))
    return pl.pallas_call(
        body,
        grid=(len(blocks),),
        out_shape=out_shape,
        in_specs=in_specs,
        out_specs=out_specs,
        scratch_shapes=[
            pltpu.VMEM((row_count, 3, modes, cells), F32),
            pltpu.VMEM((modes, row_count * len(parts) * cells), BF16),
        ],
        compiler_params=pltpu.CompilerParams(vmem_limit_bytes=20 << 20),
        cost_estimate=pl.CostEstimate(
            flops=cost * len(blocks) * block * share * modes * row_count * cells, bytes_accessed=4 << 20, transcendentals=0
        ),
    )(*operands)


def ring(axis):
    count = lax.axis_size(axis)
    return [(i, (i + 1) % count) for i in range(count)], [((i + 1) % count, i) for i in range(count)]


def flip(array, flips, sizes):
    axes = tuple(sorted({axis for axis, _ in flips}, key=("gx", "gy", "ma").index))
    strides = {}
    count = 1
    for axis in reversed(axes):
        strides[axis] = count
        count *= sizes[axis]
    change = 0
    for axis, bit in flips:
        change |= strides[axis] << bit
    return lax.ppermute(array, axes, [(i, i ^ change) for i in range(count)])


def subsets(stage):
    for code in range(1, 1 << len(stage)):
        yield code, [stage[n] for n in range(len(stage)) if (code >> (len(stage) - 1 - n)) & 1]


def stages_of(sizes):
    order = send_order(sizes)
    return [[order[0]], order[1:3]] + [[entry] for entry in order[3:]]


def term_sum(terms, low, high):
    total = terms[0][low:high].astype(F32)
    for array in terms[1:]:
        total = total + array[low:high].astype(F32)
    return total


def sends(terms, count, stage):
    length = count >> len(stage)
    return [
        term_sum(terms, code * length, (code + 1) * length).astype(BF16)
        for code, _ in list(subsets(stage))[::-1]
    ]


def exchange(stage, sent, sizes):
    return [flip(array, flips, sizes) for array, (_, flips) in zip(sent, list(subsets(stage))[::-1])]


def combine_kernel(*refs, terms, pair):
    outs = refs[terms:]
    count, share, modes = refs[0].shape
    each = count // 2 // pair
    for above in range(2):
        for place in range(each):
            rows = pl.ds(above * (count // 2) + place * pair, pair)
            total = refs[0][rows].astype(F32)
            for ref in refs[1:terms]:
                total = total + ref[rows].astype(F32)
            total = total.reshape(pair * share, modes).T
            for swapped in range(2):
                out = outs[2 * above + swapped]
                out[place] = total[swapped * share : (swapped + 1) * share].astype(out.dtype)


def assemble_kernel(own_ref, swapped_ref, above_ref, both_ref, out_ref, *, pair):
    count, share, width = own_ref.shape
    first = lax.axis_index("ma") == 0
    for place in range(count):
        mine = own_ref[place] + above_ref[place].astype(F32)
        theirs = swapped_ref[place].astype(F32) + both_ref[place].astype(F32)
        low = jnp.where(first, mine, theirs)
        high = jnp.where(first, theirs, mine)
        for part in range(pair):
            lanes = slice(part * (width // pair), (part + 1) * (width // pair))
            out_ref[place * pair + part] = jnp.concatenate([low[:, lanes], high[:, lanes]], 1)


def sum_kernel(*refs):
    total = refs[0][...].astype(F32)
    for ref in refs[1:-1]:
        total = total + ref[...].astype(F32)
    refs[-1][...] = total


def summed(terms, count, cost):
    shape = (count, *terms[0].shape[1:])
    whole = pl.BlockSpec(shape, lambda g: (0,) * len(shape))
    return pl.pallas_call(
        sum_kernel,
        grid=(1,),
        out_shape=jax.ShapeDtypeStruct(shape, F32),
        in_specs=[whole] * len(terms),
        out_specs=whole,
        compiler_params=pltpu.CompilerParams(vmem_limit_bytes=16 << 20),
        cost_estimate=pl.CostEstimate(flops=cost, bytes_accessed=1024, transcendentals=0),
    )(*terms)


def finish(terms, count, stage, sizes):
    _, share, modes = terms[0].shape
    pair = 2 if count % 4 == 0 else 1
    places = count // 2 // pair
    shape = (places, share, pair * share)
    whole = lambda shape: pl.BlockSpec(shape, lambda g: (0,) * len(shape))
    parts = pl.pallas_call(
        functools.partial(combine_kernel, terms=len(terms), pair=pair),
        grid=(1,),
        out_shape=[jax.ShapeDtypeStruct(shape, dtype) for dtype in (F32, BF16, BF16, BF16)],
        in_specs=[whole((count, share, modes))] * len(terms),
        out_specs=[whole(shape)] * 4,
        compiler_params=pltpu.CompilerParams(vmem_limit_bytes=16 << 20),
        cost_estimate=pl.CostEstimate(flops=1, bytes_accessed=1024, transcendentals=0),
    )(*terms)
    stage = stage + [("ma", 0)]
    arrived = {code: flip(parts[code], flips, sizes) for code, flips in reversed(list(subsets(stage)))}
    return pl.pallas_call(
        functools.partial(assemble_kernel, pair=pair),
        out_shape=jax.ShapeDtypeStruct((places * pair, share, modes), F32),
        in_specs=[pl.BlockSpec(memory_space=pltpu.VMEM)] * 4,
        out_specs=pl.BlockSpec(memory_space=pltpu.VMEM),
        compiler_params=pltpu.CompilerParams(vmem_limit_bytes=16 << 20),
        cost_estimate=pl.CostEstimate(flops=1, bytes_accessed=1024, transcendentals=0),
    )(parts[0], arrived[1], arrived[2], arrived[3])


def shards(mode_fields, cell_volumes, sizes):
    barrier = lax.optimization_barrier
    own = jnp.transpose(mode_fields, (2, 0, 1, 3))
    row_count, _, share, _ = own.shape
    modes = 2 * share
    quarter = row_count // 4
    all_rows = tuple(range(row_count))
    inner_rows = all_rows[quarter : 3 * quarter]
    outer_rows = all_rows[:quarter] + all_rows[3 * quarter :]
    own_inner = own[quarter : 3 * quarter]
    own_outer = jnp.concatenate([own[:quarter], own[3 * quarter :]], 0)

    other_inner = flip(own_inner, [("ma", 0)], sizes)
    columns = jnp.stack([own[:, :, :, -1], own[:, :, :, 0]]).reshape(2, 3 * row_count, share)
    columns = lax.all_gather(columns, "gy")
    own_outer_held, edges, columns = barrier((own_outer, (own[-1:], own[:1]), columns))
    forward, backward = ring("gx")
    above = lax.ppermute(edges[0], "gx", forward)
    below = lax.ppermute(edges[1], "gx", backward)
    other_outer = flip(own_outer_held, [("ma", 0)], sizes)

    inner = functools.partial(
        partial_tensor, own_inner, other_inner, slopes_of(own, inner_rows, columns), rows=inner_rows, sizes=sizes
    )
    so_far = inner(cell_volumes, blocks=(1, 2, 3, 5, 6, 7))
    columns, so_far = barrier((columns, so_far))
    slopes_outer = slopes_of(own, outer_rows, columns, above, below)
    outer = functools.partial(
        partial_tensor, own_outer, other_outer, slopes_outer, rows=outer_rows, sizes=sizes
    )
    stages = stages_of(sizes)
    count = modes // BLOCKS
    cell_count = mode_fields.shape[2] * mode_fields.shape[3]
    sent = outer(cell_volumes, blocks=(5, 6, 7), before=so_far, first=3, dtypes=(BF16,))
    cell_volumes, sent = barrier((cell_volumes, sent))
    arrived = flip(sent, stages[0], sizes)
    kept = outer(cell_volumes, blocks=(1, 2, 3), before=so_far)
    sent = [term_sum([kept, arrived], at * count, (at + 1) * count).astype(BF16) for at in range(3)]
    cell_volumes, sent = barrier((cell_volumes, sent))
    received = exchange(stages[1], sent[::-1], sizes)
    so_far = inner(cell_volumes, blocks=(4, 0), cost=1)
    sent, kept = outer(cell_volumes, blocks=(4, 0), before=so_far, dtypes=(BF16, F32), cost=1)
    arrived = flip(sent, stages[0], sizes)
    terms = [summed(received, count, 16 * count * modes * share * cell_count), kept, arrived]
    for stage in stages[2:-1]:
        terms = terms + exchange(stage, sends(terms, count, stage), sizes)
        count = count >> len(stage)
    return finish(terms, count, stages[-1], sizes)


def solution(mesh):
    in_specs = (P(None, "ma", "gx", "gy"), P("gx", "gy"))
    out_specs = P(("gx", "gy"), "ma", None)
    body = functools.partial(shards, sizes=dict(mesh.shape))
    return jax.shard_map(body, mesh=mesh, in_specs=in_specs, out_specs=out_specs, check_vma=False)
```

```python
import functools
import math

import jax
import jax.numpy as jnp
from jax import lax
from jax.experimental import pallas as pl
from jax.experimental.pallas import tpu as pltpu
from jax.sharding import PartitionSpec as P

BF16 = jnp.bfloat16
F32 = jnp.float32
BLOCKS = 8


def bits_of(count):
    return count.bit_length() - 1


def send_order(sizes):
    order = []
    for axis in ("gy", "gx"):
        order += [(axis, bit) for bit in range(bits_of(sizes[axis]))]
    return order


def source_bits(sizes, rows_each):
    row_bits = bits_of(rows_each)
    base = {"gy": row_bits, "gx": row_bits + bits_of(sizes["gy"])}
    found = list(range(row_bits))
    for axis, bit in reversed(send_order(sizes)):
        found.append(base[axis] + bit)
    return found


def slopes_kernel(own_ref, columns_ref, *refs, rows):
    out_ref = refs[-1]
    last = own_ref.shape[0] - 1
    share, cells = own_ref.shape[2:]

    def edge(step):
        count = columns_ref.shape[0]
        at = lax.axis_index("gy") + step
        inside = jnp.logical_and(at >= 0, at < count)
        values = columns_ref[jnp.clip(at, 0, count - 1), 0 if step < 0 else 1].astype(F32)
        return jnp.where(inside, values, jnp.zeros_like(values)).T

    before, after = edge(-1), edge(1)
    here = lax.axis_index("gx")

    def outside(ref, edge_of_grid, a):
        values = ref[0, a].astype(F32)
        return jnp.where(here == edge_of_grid, jnp.zeros_like(values), values)

    lane = lax.broadcasted_iota(jnp.int32, (share, cells), 1)
    for place, x in enumerate(rows):
        for a in range(3):
            down = outside(refs[0], 0, a) if x == 0 else own_ref[x - 1, a].astype(F32)
            up = outside(refs[1], lax.axis_size("gx") - 1, a) if x == last else own_ref[x + 1, a].astype(F32)
            out_ref[place, a] = ((up - down) * 0.5).astype(BF16)
            value = own_ref[x, a].astype(F32)
            column = 3 * x + a
            down = jnp.where(lane == 0, before[:, column : column + 1], pltpu.roll(value, 1, 1))
            up = jnp.where(lane == cells - 1, after[:, column : column + 1], pltpu.roll(value, cells - 1, 1))
            out_ref[place, 3 + a] = ((up - down) * 0.5).astype(BF16)


def slopes_of(own, rows, *edges):
    _, _, share, cells = own.shape
    return pl.pallas_call(
        functools.partial(slopes_kernel, rows=rows),
        out_shape=jax.ShapeDtypeStruct((len(rows), 6, share, cells), BF16),
        in_specs=[pl.BlockSpec(memory_space=pltpu.VMEM)] * (1 + len(edges)),
        out_specs=pl.BlockSpec(memory_space=pltpu.VMEM),
        compiler_params=pltpu.CompilerParams(vmem_limit_bytes=16 << 20),
        cost_estimate=pl.CostEstimate(flops=1, bytes_accessed=1024, transcendentals=0),
    )(own, *edges)


def sum_of(left, right):
    return left[0] * right[0] + left[1] * right[1] + left[2] * right[2]


def tensor_kernel(*refs, bits, block, rows_each, blocks, rows, scale, parts, outputs):
    own_ref, other_ref, slope_ref, volume_ref = refs[:4]
    left, right = refs[-2:]
    out_refs = refs[-2 - outputs : -2]
    before_ref = refs[4] if len(refs) == 7 + outputs else None
    row_count, _, share, cells = own_ref.shape
    step = pl.program_id(0)
    top = bits_of(2 * share) - 1

    @pl.when(step == 0)
    def _():
        for x in range(row_count):
            weight = volume_ref[pl.ds(rows[x], 1), :] * scale
            for half, ref in enumerate((own_ref, other_ref)):
                for a in range(3):
                    value = (weight * ref[x, a].astype(F32)).astype(BF16)
                    left[x, a, half * share : (half + 1) * share, :] = value.astype(F32)
                for place, b in enumerate(parts):
                    lanes = len(parts) * x + place
                    right[half * share : (half + 1) * share, lanes * cells : (lanes + 1) * cells] = ref[x, b]

    here = (lax.axis_index("gx") * lax.axis_size("gy") + lax.axis_index("gy")) * rows_each
    start = here ^ (lax.axis_index("ma") << top)
    position = block_at(blocks, step) * block
    for place, bit in enumerate(bits):
        start = start ^ (((position >> place) & 1) << bit)
    columns = []
    for x in range(row_count):
        slopes = [slope_ref[x, n] for n in range(3 * len(parts))]
        sums = [[] for _ in parts]
        for row in range(block):
            offset = 0
            for place, bit in enumerate(bits):
                offset |= ((row >> place) & 1) << bit
            test = [
                jnp.concatenate(
                    [left[x, a, pl.ds(start ^ offset, 16, stride=0), :].astype(BF16)] * (share // 16), 0
                )
                for a in range(3)
            ]
            for place, found in enumerate(sums):
                found.append(sum_of(test, slopes[3 * place : 3 * place + 3]))
        columns += [jnp.concatenate(found, 0) for found in sums]
    sums = jnp.concatenate(columns, 1)
    product = lax.dot_general(sums, right[...], (((1,), (1,)), ((), ())), preferred_element_type=F32)
    product = product.reshape(block, share, 2 * share)
    if before_ref is not None:
        product = product + before_ref[...]
    if outputs == 1:
        out_refs[0][...] = product.astype(out_refs[0].dtype)
    else:
        for place, out_ref in enumerate(out_refs):

            @pl.when(step == place)
            def _(out_ref=out_ref):
                out_ref[...] = product.astype(out_ref.dtype)


def block_at(blocks, step):
    block = blocks[0] + step
    for n in range(1, len(blocks)):
        jump = blocks[n] - blocks[n - 1] - 1
        if jump:
            block = block + jnp.where(step >= n, jump, 0)
    return block


def partial_tensor(
    own, other, slopes, volumes, rows, sizes, blocks, before=None, first=0, dtypes=(F32,), cost=8
):
    row_count, _, share, cells = own.shape
    modes = 2 * share
    block = modes // BLOCKS
    parts = (0, 1)
    outputs = len(dtypes)
    devices = sizes["gx"] * sizes["gy"]
    rows_each = modes // devices
    body = functools.partial(
        tensor_kernel,
        bits=source_bits(sizes, rows_each),
        block=block,
        rows_each=rows_each,
        blocks=blocks,
        outputs=outputs,
        rows=rows,
        parts=parts,
        scale=1.0 / math.sqrt(volumes.shape[0] * volumes.shape[1] * devices),
    )
    whole = lambda array: pl.BlockSpec(array.shape, lambda g: (0,) * array.ndim, pipeline_mode=pl.Buffered(1))
    shape = (block, share, modes)
    operands = [own, other, slopes, volumes]
    in_specs = [whole(array) for array in operands]
    if before is not None:
        operands.append(before)
        in_specs.append(pl.BlockSpec(shape, lambda g: (first + g, 0, 0)))
    if outputs > 1:
        out_shape = [jax.ShapeDtypeStruct(shape, dtype) for dtype in dtypes]
        out_specs = [pl.BlockSpec(shape, lambda g: (0, 0, 0))] * outputs
    else:
        out_shape = (pltpu.VMEM if before is None else jax.ShapeDtypeStruct)(
            (len(blocks) * block, share, modes), dtypes[0]
        )
        out_specs = pl.BlockSpec(shape, lambda g: (g, 0, 0))
    return pl.pallas_call(
        body,
        grid=(len(blocks),),
        out_shape=out_shape,
        in_specs=in_specs,
        out_specs=out_specs,
        scratch_shapes=[
            pltpu.VMEM((row_count, 3, modes, cells), F32),
            pltpu.VMEM((modes, row_count * len(parts) * cells), BF16),
        ],
        compiler_params=pltpu.CompilerParams(vmem_limit_bytes=20 << 20),
        cost_estimate=pl.CostEstimate(
            flops=cost * len(blocks) * block * share * modes * row_count * cells, bytes_accessed=4 << 20, transcendentals=0
        ),
    )(*operands)


def ring(axis):
    count = lax.axis_size(axis)
    return [(i, (i + 1) % count) for i in range(count)], [((i + 1) % count, i) for i in range(count)]


def flip(array, flips, sizes):
    axes = tuple(sorted({axis for axis, _ in flips}, key=("gx", "gy", "ma").index))
    strides = {}
    count = 1
    for axis in reversed(axes):
        strides[axis] = count
        count *= sizes[axis]
    change = 0
    for axis, bit in flips:
        change |= strides[axis] << bit
    return lax.ppermute(array, axes, [(i, i ^ change) for i in range(count)])


def subsets(stage):
    for code in range(1, 1 << len(stage)):
        yield code, [stage[n] for n in range(len(stage)) if (code >> (len(stage) - 1 - n)) & 1]


def stages_of(sizes):
    order = send_order(sizes)
    return [[order[0]], order[1:3]] + [[entry] for entry in order[3:]]


def term_sum(terms, low, high):
    total = terms[0][low:high].astype(F32)
    for array in terms[1:]:
        total = total + array[low:high].astype(F32)
    return total


def sends(terms, count, stage):
    length = count >> len(stage)
    return [
        term_sum(terms, code * length, (code + 1) * length).astype(BF16)
        for code, _ in list(subsets(stage))[::-1]
    ]


def exchange(stage, sent, sizes):
    return [flip(array, flips, sizes) for array, (_, flips) in zip(sent, list(subsets(stage))[::-1])]


def combine_kernel(*refs, terms, pair):
    outs = refs[terms:]
    count, share, modes = refs[0].shape
    each = count // 2 // pair
    for above in range(2):
        for place in range(each):
            rows = pl.ds(above * (count // 2) + place * pair, pair)
            total = refs[0][rows].astype(F32)
            for ref in refs[1:terms]:
                total = total + ref[rows].astype(F32)
            total = total.reshape(pair * share, modes).T
            for swapped in range(2):
                out = outs[2 * above + swapped]
                out[place] = total[swapped * share : (swapped + 1) * share].astype(out.dtype)


def assemble_kernel(own_ref, above_ref, both_ref, swapped_ref, out_ref, *, pair):
    count, share, width = own_ref.shape
    first = lax.axis_index("ma") == 0
    for place in range(count):
        mine = own_ref[place] + above_ref[place].astype(F32)
        theirs = swapped_ref[place].astype(F32) + both_ref[place].astype(F32)
        low = jnp.where(first, mine, theirs)
        high = jnp.where(first, theirs, mine)
        for part in range(pair):
            lanes = slice(part * (width // pair), (part + 1) * (width // pair))
            out_ref[place * pair + part] = jnp.concatenate([low[:, lanes], high[:, lanes]], 1)


def sum_kernel(*refs):
    total = refs[0][...].astype(F32)
    for ref in refs[1:-1]:
        total = total + ref[...].astype(F32)
    refs[-1][...] = total


def summed(terms, count, cost):
    shape = (count, *terms[0].shape[1:])
    whole = pl.BlockSpec(shape, lambda g: (0,) * len(shape))
    return pl.pallas_call(
        sum_kernel,
        grid=(1,),
        out_shape=jax.ShapeDtypeStruct(shape, F32),
        in_specs=[whole] * len(terms),
        out_specs=whole,
        compiler_params=pltpu.CompilerParams(vmem_limit_bytes=16 << 20),
        cost_estimate=pl.CostEstimate(flops=cost, bytes_accessed=1024, transcendentals=0),
    )(*terms)


def finish(terms, count, stage, sizes):
    _, share, modes = terms[0].shape
    pair = 2 if count % 4 == 0 else 1
    places = count // 2 // pair
    shape = (places, share, pair * share)
    whole = lambda shape: pl.BlockSpec(shape, lambda g: (0,) * len(shape))
    parts = pl.pallas_call(
        functools.partial(combine_kernel, terms=len(terms), pair=pair),
        grid=(1,),
        out_shape=[jax.ShapeDtypeStruct(shape, dtype) for dtype in (F32, BF16, BF16, BF16)],
        in_specs=[whole((count, share, modes))] * len(terms),
        out_specs=[whole(shape)] * 4,
        compiler_params=pltpu.CompilerParams(vmem_limit_bytes=16 << 20),
        cost_estimate=pl.CostEstimate(flops=1, bytes_accessed=1024, transcendentals=0),
    )(*terms)
    stage = stage + [("ma", 0)]
    arrived = {code: flip(parts[code], flips, sizes) for code, flips in reversed(list(subsets(stage)))}
    return pl.pallas_call(
        functools.partial(assemble_kernel, pair=pair),
        out_shape=jax.ShapeDtypeStruct((places * pair, share, modes), F32),
        in_specs=[pl.BlockSpec(memory_space=pltpu.VMEM)] * 4,
        out_specs=pl.BlockSpec(memory_space=pltpu.VMEM),
        compiler_params=pltpu.CompilerParams(vmem_limit_bytes=16 << 20),
        cost_estimate=pl.CostEstimate(flops=1, bytes_accessed=1024, transcendentals=0),
    )(parts[0], arrived[2], arrived[3], arrived[1])


def shards(mode_fields, cell_volumes, sizes):
    barrier = lax.optimization_barrier
    own = jnp.transpose(mode_fields, (2, 0, 1, 3))
    row_count, _, share, _ = own.shape
    modes = 2 * share
    quarter = row_count // 4
    all_rows = tuple(range(row_count))
    inner_rows = all_rows[quarter : 3 * quarter]
    outer_rows = all_rows[:quarter] + all_rows[3 * quarter :]
    own_inner = own[quarter : 3 * quarter]
    own_outer = jnp.concatenate([own[:quarter], own[3 * quarter :]], 0)

    other_inner = flip(own_inner, [("ma", 0)], sizes)
    columns = jnp.stack([own[:, :, :, -1], own[:, :, :, 0]]).reshape(2, 3 * row_count, share)
    columns = lax.all_gather(columns, "gy")
    own_outer_held, edges, columns = barrier((own_outer, (own[-1:], own[:1]), columns))
    forward, backward = ring("gx")
    above = lax.ppermute(edges[0], "gx", forward)
    below = lax.ppermute(edges[1], "gx", backward)
    other_outer = flip(own_outer_held, [("ma", 0)], sizes)

    inner = functools.partial(
        partial_tensor, own_inner, other_inner, slopes_of(own, inner_rows, columns), rows=inner_rows, sizes=sizes
    )
    so_far = inner(cell_volumes, blocks=(1, 2, 3, 5, 6, 7))
    columns, so_far = barrier((columns, so_far))
    slopes_outer = slopes_of(own, outer_rows, columns, above, below)
    outer = functools.partial(
        partial_tensor, own_outer, other_outer, slopes_outer, rows=outer_rows, sizes=sizes
    )
    stages = stages_of(sizes)
    count = modes // BLOCKS
    cell_count = mode_fields.shape[2] * mode_fields.shape[3]
    flips = dict(subsets(stages[1]))
    sent = outer(cell_volumes, blocks=(7,), before=so_far, first=5, dtypes=(BF16,))
    cell_volumes, sent = barrier((cell_volumes, sent))
    arrived = flip(sent, stages[0], sizes)
    kept = outer(cell_volumes, blocks=(3,), before=so_far, first=2)
    sent = term_sum([kept, arrived], 0, count).astype(BF16)
    cell_volumes, sent = barrier((cell_volumes, sent))
    both = flip(sent, flips[3], sizes)

    sent = outer(cell_volumes, blocks=(5, 6), before=so_far, first=3, dtypes=(BF16,), cost=1)
    cell_volumes, sent = barrier((cell_volumes, sent))
    arrived = flip(sent, stages[0], sizes)
    kept = outer(cell_volumes, blocks=(1, 2), before=so_far, cost=1)
    sent = [term_sum([kept, arrived], at * count, (at + 1) * count).astype(BF16) for at in range(2)]
    cell_volumes, sent = barrier((cell_volumes, sent))
    cell_volumes, both = barrier((cell_volumes, both))
    received = [flip(sent[1], flips[2], sizes), flip(sent[0], flips[1], sizes), both]

    so_far = inner(cell_volumes, blocks=(4, 0), cost=1)
    sent, kept = outer(cell_volumes, blocks=(4, 0), before=so_far, dtypes=(BF16, F32), cost=1)
    arrived = flip(sent, stages[0], sizes)
    terms = [summed(received, count, 16 * count * modes * share * cell_count), kept, arrived]
    for stage in stages[2:-1]:
        terms = terms + exchange(stage, sends(terms, count, stage), sizes)
        count = count >> len(stage)
    return finish(terms, count, stages[-1], sizes)


def solution(mesh):
    in_specs = (P(None, "ma", "gx", "gy"), P("gx", "gy"))
    out_specs = P(("gx", "gy"), "ma", None)
    body = functools.partial(shards, sizes=dict(mesh.shape))
    return jax.shard_map(body, mesh=mesh, in_specs=in_specs, out_specs=out_specs, check_vma=False)
```

```python
import functools
import math

import jax
import jax.numpy as jnp
from jax import lax
from jax.experimental import pallas as pl
from jax.experimental.pallas import tpu as pltpu
from jax.sharding import PartitionSpec as P

BF16 = jnp.bfloat16
F32 = jnp.float32
BLOCKS = 8


def bits_of(count):
    return count.bit_length() - 1


def send_order(sizes):
    order = []
    for axis in ("gy", "gx"):
        order += [(axis, bit) for bit in range(bits_of(sizes[axis]))]
    return order


def source_bits(sizes, rows_each):
    row_bits = bits_of(rows_each)
    base = {"gy": row_bits, "gx": row_bits + bits_of(sizes["gy"])}
    found = list(range(row_bits))
    for axis, bit in reversed(send_order(sizes)):
        found.append(base[axis] + bit)
    return found


def slopes_kernel(own_ref, columns_ref, *refs, rows):
    out_ref = refs[-1]
    last = own_ref.shape[0] - 1
    share, cells = own_ref.shape[2:]

    def edge(step):
        count = columns_ref.shape[0]
        at = lax.axis_index("gy") + step
        inside = jnp.logical_and(at >= 0, at < count)
        values = columns_ref[jnp.clip(at, 0, count - 1), 0 if step < 0 else 1].astype(F32)
        return jnp.where(inside, values, jnp.zeros_like(values)).T

    before, after = edge(-1), edge(1)
    here = lax.axis_index("gx")

    def outside(ref, edge_of_grid, a):
        values = ref[0, a].astype(F32)
        return jnp.where(here == edge_of_grid, jnp.zeros_like(values), values)

    lane = lax.broadcasted_iota(jnp.int32, (share, cells), 1)
    for place, x in enumerate(rows):
        for a in range(3):
            down = outside(refs[0], 0, a) if x == 0 else own_ref[x - 1, a].astype(F32)
            up = outside(refs[1], lax.axis_size("gx") - 1, a) if x == last else own_ref[x + 1, a].astype(F32)
            out_ref[place, a] = ((up - down) * 0.5).astype(BF16)
            value = own_ref[x, a].astype(F32)
            column = 3 * x + a
            down = jnp.where(lane == 0, before[:, column : column + 1], pltpu.roll(value, 1, 1))
            up = jnp.where(lane == cells - 1, after[:, column : column + 1], pltpu.roll(value, cells - 1, 1))
            out_ref[place, 3 + a] = ((up - down) * 0.5).astype(BF16)


def slopes_of(own, rows, *edges):
    _, _, share, cells = own.shape
    return pl.pallas_call(
        functools.partial(slopes_kernel, rows=rows),
        out_shape=jax.ShapeDtypeStruct((len(rows), 6, share, cells), BF16),
        in_specs=[pl.BlockSpec(memory_space=pltpu.VMEM)] * (1 + len(edges)),
        out_specs=pl.BlockSpec(memory_space=pltpu.VMEM),
        compiler_params=pltpu.CompilerParams(vmem_limit_bytes=16 << 20),
        cost_estimate=pl.CostEstimate(flops=1, bytes_accessed=1024, transcendentals=0),
    )(own, *edges)


def sum_of(left, right):
    return left[0] * right[0] + left[1] * right[1] + left[2] * right[2]


def tensor_kernel(*refs, bits, block, rows_each, blocks, rows, scale, parts, outputs):
    own_ref, other_ref, slope_ref, volume_ref = refs[:4]
    left, right = refs[-2:]
    out_refs = refs[-2 - outputs : -2]
    before_ref = refs[4] if len(refs) == 7 + outputs else None
    row_count, _, share, cells = own_ref.shape
    step = pl.program_id(0)
    top = bits_of(2 * share) - 1

    @pl.when(step == 0)
    def _():
        for x in range(row_count):
            weight = volume_ref[pl.ds(rows[x], 1), :] * scale
            for half, ref in enumerate((own_ref, other_ref)):
                for a in range(3):
                    value = (weight * ref[x, a].astype(F32)).astype(BF16)
                    left[x, a, half * share : (half + 1) * share, :] = value.astype(F32)
                for place, b in enumerate(parts):
                    lanes = len(parts) * x + place
                    right[half * share : (half + 1) * share, lanes * cells : (lanes + 1) * cells] = ref[x, b]

    here = (lax.axis_index("gx") * lax.axis_size("gy") + lax.axis_index("gy")) * rows_each
    start = here ^ (lax.axis_index("ma") << top)
    position = block_at(blocks, step) * block
    for place, bit in enumerate(bits):
        start = start ^ (((position >> place) & 1) << bit)
    columns = []
    for x in range(row_count):
        slopes = [slope_ref[x, n] for n in range(3 * len(parts))]
        sums = [[] for _ in parts]
        for row in range(block):
            offset = 0
            for place, bit in enumerate(bits):
                offset |= ((row >> place) & 1) << bit
            test = [
                jnp.concatenate(
                    [left[x, a, pl.ds(start ^ offset, 16, stride=0), :].astype(BF16)] * (share // 16), 0
                )
                for a in range(3)
            ]
            for place, found in enumerate(sums):
                found.append(sum_of(test, slopes[3 * place : 3 * place + 3]))
        columns += [jnp.concatenate(found, 0) for found in sums]
    sums = jnp.concatenate(columns, 1)
    product = lax.dot_general(sums, right[...], (((1,), (1,)), ((), ())), preferred_element_type=F32)
    product = product.reshape(block, share, 2 * share)
    if before_ref is not None:
        product = product + before_ref[...]
    if outputs == 1:
        out_refs[0][...] = product.astype(out_refs[0].dtype)
    else:
        for place, out_ref in enumerate(out_refs):

            @pl.when(step == place)
            def _(out_ref=out_ref):
                out_ref[...] = product.astype(out_ref.dtype)


def block_at(blocks, step):
    block = blocks[0] + step
    for n in range(1, len(blocks)):
        jump = blocks[n] - blocks[n - 1] - 1
        if jump:
            block = block + jnp.where(step >= n, jump, 0)
    return block


def partial_tensor(
    own, other, slopes, volumes, rows, sizes, blocks, before=None, first=0, dtypes=(F32,), cost=8
):
    row_count, _, share, cells = own.shape
    modes = 2 * share
    block = modes // BLOCKS
    parts = (0, 1)
    outputs = len(dtypes)
    devices = sizes["gx"] * sizes["gy"]
    rows_each = modes // devices
    body = functools.partial(
        tensor_kernel,
        bits=source_bits(sizes, rows_each),
        block=block,
        rows_each=rows_each,
        blocks=blocks,
        outputs=outputs,
        rows=rows,
        parts=parts,
        scale=1.0 / math.sqrt(volumes.shape[0] * volumes.shape[1] * devices),
    )
    whole = lambda array: pl.BlockSpec(array.shape, lambda g: (0,) * array.ndim, pipeline_mode=pl.Buffered(1))
    shape = (block, share, modes)
    operands = [own, other, slopes, volumes]
    in_specs = [whole(array) for array in operands]
    if before is not None:
        operands.append(before)
        in_specs.append(pl.BlockSpec(shape, lambda g: (first + g, 0, 0)))
    if outputs > 1:
        out_shape = [jax.ShapeDtypeStruct(shape, dtype) for dtype in dtypes]
        out_specs = [pl.BlockSpec(shape, lambda g: (0, 0, 0))] * outputs
    else:
        out_shape = (pltpu.VMEM if before is None else jax.ShapeDtypeStruct)(
            (len(blocks) * block, share, modes), dtypes[0]
        )
        out_specs = pl.BlockSpec(shape, lambda g: (g, 0, 0))
    return pl.pallas_call(
        body,
        grid=(len(blocks),),
        out_shape=out_shape,
        in_specs=in_specs,
        out_specs=out_specs,
        scratch_shapes=[
            pltpu.VMEM((row_count, 3, modes, cells), F32),
            pltpu.VMEM((modes, row_count * len(parts) * cells), BF16),
        ],
        compiler_params=pltpu.CompilerParams(vmem_limit_bytes=20 << 20),
        cost_estimate=pl.CostEstimate(
            flops=cost * len(blocks) * block * share * modes * row_count * cells, bytes_accessed=4 << 20, transcendentals=0
        ),
    )(*operands)


def ring(axis):
    count = lax.axis_size(axis)
    return [(i, (i + 1) % count) for i in range(count)], [((i + 1) % count, i) for i in range(count)]


def flip(array, flips, sizes):
    axes = tuple(sorted({axis for axis, _ in flips}, key=("gx", "gy", "ma").index))
    strides = {}
    count = 1
    for axis in reversed(axes):
        strides[axis] = count
        count *= sizes[axis]
    change = 0
    for axis, bit in flips:
        change |= strides[axis] << bit
    return lax.ppermute(array, axes, [(i, i ^ change) for i in range(count)])


def subsets(stage):
    for code in range(1, 1 << len(stage)):
        yield code, [stage[n] for n in range(len(stage)) if (code >> (len(stage) - 1 - n)) & 1]


def stages_of(sizes):
    order = send_order(sizes)
    return [[order[0]], order[1:3]] + [[entry] for entry in order[3:]]


def term_sum(terms, low, high):
    total = terms[0][low:high].astype(F32)
    for array in terms[1:]:
        total = total + array[low:high].astype(F32)
    return total


def sends(terms, count, stage):
    length = count >> len(stage)
    return [
        term_sum(terms, code * length, (code + 1) * length).astype(BF16)
        for code, _ in list(subsets(stage))[::-1]
    ]


def exchange(stage, sent, sizes):
    return [flip(array, flips, sizes) for array, (_, flips) in zip(sent, list(subsets(stage))[::-1])]


def combine_kernel(*refs, terms, pair):
    outs = refs[terms:]
    count, share, modes = refs[0].shape
    each = count // 2 // pair
    for above in range(2):
        for place in range(each):
            rows = pl.ds(above * (count // 2) + place * pair, pair)
            total = refs[0][rows].astype(F32)
            for ref in refs[1:terms]:
                total = total + ref[rows].astype(F32)
            total = total.reshape(pair * share, modes).T
            for swapped in range(2):
                out = outs[2 * above + swapped]
                out[place] = total[swapped * share : (swapped + 1) * share].astype(out.dtype)


def assemble_kernel(own_ref, above_ref, both_ref, swapped_ref, out_ref, *, pair):
    count, share, width = own_ref.shape
    first = lax.axis_index("ma") == 0
    for place in range(count):
        mine = own_ref[place] + above_ref[place].astype(F32)
        theirs = swapped_ref[place].astype(F32) + both_ref[place].astype(F32)
        low = jnp.where(first, mine, theirs)
        high = jnp.where(first, theirs, mine)
        for part in range(pair):
            lanes = slice(part * (width // pair), (part + 1) * (width // pair))
            out_ref[place * pair + part] = jnp.concatenate([low[:, lanes], high[:, lanes]], 1)


def sum_kernel(*refs):
    total = refs[0][...].astype(F32)
    for ref in refs[1:-1]:
        total = total + ref[...].astype(F32)
    refs[-1][...] = total


def summed(terms, count, cost):
    shape = (count, *terms[0].shape[1:])
    whole = pl.BlockSpec(shape, lambda g: (0,) * len(shape))
    return pl.pallas_call(
        sum_kernel,
        grid=(1,),
        out_shape=jax.ShapeDtypeStruct(shape, F32),
        in_specs=[whole] * len(terms),
        out_specs=whole,
        compiler_params=pltpu.CompilerParams(vmem_limit_bytes=16 << 20),
        cost_estimate=pl.CostEstimate(flops=cost, bytes_accessed=1024, transcendentals=0),
    )(*terms)


def finish(terms, count, stage, sizes):
    _, share, modes = terms[0].shape
    pair = 2 if count % 4 == 0 else 1
    places = count // 2 // pair
    shape = (places, share, pair * share)
    whole = lambda shape: pl.BlockSpec(shape, lambda g: (0,) * len(shape))
    parts = pl.pallas_call(
        functools.partial(combine_kernel, terms=len(terms), pair=pair),
        grid=(1,),
        out_shape=[jax.ShapeDtypeStruct(shape, dtype) for dtype in (F32, BF16, BF16, BF16)],
        in_specs=[whole((count, share, modes))] * len(terms),
        out_specs=[whole(shape)] * 4,
        compiler_params=pltpu.CompilerParams(vmem_limit_bytes=16 << 20),
        cost_estimate=pl.CostEstimate(flops=1, bytes_accessed=1024, transcendentals=0),
    )(*terms)
    stage = stage + [("ma", 0)]
    arrived = {code: flip(parts[code], flips, sizes) for code, flips in reversed(list(subsets(stage)))}
    return pl.pallas_call(
        functools.partial(assemble_kernel, pair=pair),
        out_shape=jax.ShapeDtypeStruct((places * pair, share, modes), F32),
        in_specs=[pl.BlockSpec(memory_space=pltpu.VMEM)] * 4,
        out_specs=pl.BlockSpec(memory_space=pltpu.VMEM),
        compiler_params=pltpu.CompilerParams(vmem_limit_bytes=16 << 20),
        cost_estimate=pl.CostEstimate(flops=1, bytes_accessed=1024, transcendentals=0),
    )(parts[0], arrived[2], arrived[3], arrived[1])


def shards(mode_fields, cell_volumes, sizes):
    barrier = lax.optimization_barrier
    own = jnp.transpose(mode_fields, (2, 0, 1, 3))
    row_count, _, share, _ = own.shape
    modes = 2 * share
    quarter = row_count // 4
    all_rows = tuple(range(row_count))
    inner_rows = all_rows[quarter : 3 * quarter]
    outer_rows = all_rows[:quarter] + all_rows[3 * quarter :]
    own_inner = own[quarter : 3 * quarter]
    own_outer = jnp.concatenate([own[:quarter], own[3 * quarter :]], 0)

    other_inner = flip(own_inner, [("ma", 0)], sizes)
    columns = jnp.stack([own[:, :, :, -1], own[:, :, :, 0]]).reshape(2, 3 * row_count, share)
    columns = lax.all_gather(columns, "gy")
    own_outer_held, edges, columns = barrier((own_outer, (own[-1:], own[:1]), columns))
    forward, backward = ring("gx")
    above = lax.ppermute(edges[0], "gx", forward)
    below = lax.ppermute(edges[1], "gx", backward)
    other_outer = flip(own_outer_held, [("ma", 0)], sizes)

    inner = functools.partial(
        partial_tensor, own_inner, other_inner, slopes_of(own, inner_rows, columns), rows=inner_rows, sizes=sizes
    )
    so_far = inner(cell_volumes, blocks=(1, 2, 3, 5, 6, 7))
    columns, so_far = barrier((columns, so_far))
    slopes_outer = slopes_of(own, outer_rows, columns, above, below)
    outer = functools.partial(
        partial_tensor, own_outer, other_outer, slopes_outer, rows=outer_rows, sizes=sizes
    )
    stages = stages_of(sizes)
    count = modes // BLOCKS
    cell_count = mode_fields.shape[2] * mode_fields.shape[3]
    flips = dict(subsets(stages[1]))
    sent = outer(cell_volumes, blocks=(7,), before=so_far, first=5, dtypes=(BF16,))
    cell_volumes, sent = barrier((cell_volumes, sent))
    arrived = flip(sent, stages[0], sizes)
    kept = outer(cell_volumes, blocks=(3,), before=so_far, first=2)
    sent = term_sum([kept, arrived], 0, count).astype(BF16)
    cell_volumes, sent = barrier((cell_volumes, sent))
    both = flip(sent, flips[3], sizes)

    sent = outer(cell_volumes, blocks=(5, 6), before=so_far, first=3, dtypes=(BF16,), cost=1)
    cell_volumes, sent = barrier((cell_volumes, sent))
    arrived = flip(sent, stages[0], sizes)
    kept = outer(cell_volumes, blocks=(1, 2), before=so_far, cost=1)
    sent = [term_sum([kept, arrived], at * count, (at + 1) * count).astype(BF16) for at in range(2)]
    cell_volumes, sent = barrier((cell_volumes, sent))
    received = [flip(sent[1], flips[2], sizes), flip(sent[0], flips[1], sizes)]

    so_far = inner(cell_volumes, blocks=(4, 0), cost=1)
    sent = outer(cell_volumes, blocks=(4,), before=so_far, dtypes=(BF16,), cost=1)
    cell_volumes, sent, both = barrier((cell_volumes, sent, both))
    arrived = flip(sent, stages[0], sizes)
    kept = outer(cell_volumes, blocks=(0,), before=so_far, first=1, cost=1)
    received.append(both)
    terms = [summed(received, count, 16 * count * modes * share * cell_count), kept, arrived]
    for stage in stages[2:-1]:
        terms = terms + exchange(stage, sends(terms, count, stage), sizes)
        count = count >> len(stage)
    return finish(terms, count, stages[-1], sizes)


def solution(mesh):
    in_specs = (P(None, "ma", "gx", "gy"), P("gx", "gy"))
    out_specs = P(("gx", "gy"), "ma", None)
    body = functools.partial(shards, sizes=dict(mesh.shape))
    return jax.shard_map(body, mesh=mesh, in_specs=in_specs, out_specs=out_specs, check_vma=False)
```

```python
import functools
import math

import jax
import jax.numpy as jnp
from jax import lax
from jax.experimental import pallas as pl
from jax.experimental.pallas import tpu as pltpu
from jax.sharding import PartitionSpec as P

BF16 = jnp.bfloat16
F32 = jnp.float32
BLOCKS = 8


def bits_of(count):
    return count.bit_length() - 1


def send_order(sizes):
    order = []
    for axis in ("gy", "gx"):
        order += [(axis, bit) for bit in range(bits_of(sizes[axis]))]
    return order


def source_bits(sizes, rows_each):
    row_bits = bits_of(rows_each)
    base = {"gy": row_bits, "gx": row_bits + bits_of(sizes["gy"])}
    found = list(range(row_bits))
    for axis, bit in reversed(send_order(sizes)):
        found.append(base[axis] + bit)
    return found


def slopes_kernel(own_ref, columns_ref, *refs, rows):
    out_ref = refs[-1]
    last = own_ref.shape[0] - 1
    share, cells = own_ref.shape[2:]

    def edge(step):
        count = columns_ref.shape[0]
        at = lax.axis_index("gy") + step
        inside = jnp.logical_and(at >= 0, at < count)
        values = columns_ref[jnp.clip(at, 0, count - 1), 0 if step < 0 else 1].astype(F32)
        return jnp.where(inside, values, jnp.zeros_like(values)).T

    before, after = edge(-1), edge(1)
    here = lax.axis_index("gx")

    def outside(ref, edge_of_grid, a):
        values = ref[0, a].astype(F32)
        return jnp.where(here == edge_of_grid, jnp.zeros_like(values), values)

    lane = lax.broadcasted_iota(jnp.int32, (share, cells), 1)
    for place, x in enumerate(rows):
        for a in range(3):
            down = outside(refs[0], 0, a) if x == 0 else own_ref[x - 1, a].astype(F32)
            up = outside(refs[1], lax.axis_size("gx") - 1, a) if x == last else own_ref[x + 1, a].astype(F32)
            out_ref[place, a] = ((up - down) * 0.5).astype(BF16)
            value = own_ref[x, a].astype(F32)
            column = 3 * x + a
            down = jnp.where(lane == 0, before[:, column : column + 1], pltpu.roll(value, 1, 1))
            up = jnp.where(lane == cells - 1, after[:, column : column + 1], pltpu.roll(value, cells - 1, 1))
            out_ref[place, 3 + a] = ((up - down) * 0.5).astype(BF16)


def slopes_of(own, rows, *edges):
    _, _, share, cells = own.shape
    return pl.pallas_call(
        functools.partial(slopes_kernel, rows=rows),
        out_shape=jax.ShapeDtypeStruct((len(rows), 6, share, cells), BF16),
        in_specs=[pl.BlockSpec(memory_space=pltpu.VMEM)] * (1 + len(edges)),
        out_specs=pl.BlockSpec(memory_space=pltpu.VMEM),
        compiler_params=pltpu.CompilerParams(vmem_limit_bytes=16 << 20),
        cost_estimate=pl.CostEstimate(flops=1, bytes_accessed=1024, transcendentals=0),
    )(own, *edges)


def sum_of(left, right):
    return left[0] * right[0] + left[1] * right[1] + left[2] * right[2]


def tensor_kernel(*refs, bits, block, group, rows_each, blocks, rows, scale, has_before):
    left, right, out_ref = refs[-2], refs[-1], refs[-3]
    before_ref = refs[-4] if has_before else None
    volume_ref = refs[0]
    sets = [refs[1 + 3 * n : 4 + 3 * n] for n in range(len(rows))]
    _, _, share, cells = sets[0][0].shape
    places = [(n, x) for n in range(len(rows)) for x in range(len(rows[n]))]
    step = pl.program_id(0)
    top = bits_of(2 * share) - 1

    @pl.when(step == 0)
    def _():
        for place, (n, x) in enumerate(places):
            weight = volume_ref[pl.ds(rows[n][x], 1), :] * scale
            for half, ref in enumerate(sets[n][:2]):
                for a in range(3):
                    value = (weight * ref[x, a].astype(F32)).astype(BF16)
                    left[place, a, half * share : (half + 1) * share, :] = value.astype(F32)
                for b in range(2):
                    lanes = 2 * place + b
                    right[half * share : (half + 1) * share, lanes * cells : (lanes + 1) * cells] = ref[x, b]

    here = (lax.axis_index("gx") * lax.axis_size("gy") + lax.axis_index("gy")) * rows_each
    here = here ^ (lax.axis_index("ma") << top)
    tests = []
    for part in range(group):
        start = here
        position = block_at(blocks, step * group + part) * block
        for place, bit in enumerate(bits):
            start = start ^ (((position >> place) & 1) << bit)
        for row in range(block):
            offset = 0
            for place, bit in enumerate(bits):
                offset |= ((row >> place) & 1) << bit
            tests.append((start, offset))
    columns = []
    for place, (n, x) in enumerate(places):
        slopes = [sets[n][2][x, m] for m in range(6)]
        sums = [[], []]
        for start, offset in tests:
            test = [
                jnp.concatenate(
                    [left[place, a, pl.ds(start ^ offset, 16, stride=0), :].astype(BF16)] * (share // 16), 0
                )
                for a in range(3)
            ]
            for b, found in enumerate(sums):
                found.append(sum_of(test, slopes[3 * b : 3 * b + 3]))
        columns += [jnp.concatenate(found, 0) for found in sums]
    sums = jnp.concatenate(columns, 1)
    product = lax.dot_general(sums, right[...], (((1,), (1,)), ((), ())), preferred_element_type=F32)
    product = product.reshape(out_ref.shape)
    if before_ref is not None:
        product = product + before_ref[...]
    out_ref[...] = product.astype(out_ref.dtype)


def block_at(blocks, step):
    block = blocks[0] + step
    for n in range(1, len(blocks)):
        jump = blocks[n] - blocks[n - 1] - 1
        if jump:
            block = block + jnp.where(step >= n, jump, 0)
    return block


def partial_tensor(volumes, sets, sizes, blocks, before=None, first=0, dtype=F32, cost=8):
    _, _, share, cells = sets[0][0].shape
    modes = 2 * share
    block = modes // BLOCKS
    group = 2 if len(blocks) % 2 == 0 else 1
    devices = sizes["gx"] * sizes["gy"]
    rows_each = modes // devices
    row_count = sum(len(rows) for *_, rows in sets)
    body = functools.partial(
        tensor_kernel,
        bits=source_bits(sizes, rows_each),
        block=block,
        group=group,
        rows_each=rows_each,
        blocks=blocks,
        rows=[rows for *_, rows in sets],
        scale=1.0 / math.sqrt(volumes.shape[0] * volumes.shape[1] * devices),
        has_before=before is not None,
    )
    whole = lambda array: pl.BlockSpec(array.shape, lambda g: (0,) * array.ndim, pipeline_mode=pl.Buffered(1))
    shape = (group * block, share, modes)
    operands = [volumes] + [array for own, other, slopes, _ in sets for array in (own, other, slopes)]
    in_specs = [whole(array) for array in operands]
    if before is not None:
        operands.append(before)
        in_specs.append(pl.BlockSpec(shape, lambda g: (first // group + g, 0, 0)))
    result = pltpu.VMEM if len(blocks) > 2 else jax.ShapeDtypeStruct
    return pl.pallas_call(
        body,
        grid=(len(blocks) // group,),
        out_shape=result((len(blocks) * block, share, modes), dtype),
        in_specs=in_specs,
        out_specs=pl.BlockSpec(shape, lambda g: (g, 0, 0)),
        scratch_shapes=[
            pltpu.VMEM((row_count, 3, modes, cells), F32),
            pltpu.VMEM((modes, row_count * 2 * cells), BF16),
        ],
        compiler_params=pltpu.CompilerParams(vmem_limit_bytes=24 << 20),
        cost_estimate=pl.CostEstimate(
            flops=cost * len(blocks) * block * share * modes * row_count * cells,
            bytes_accessed=4 << 20,
            transcendentals=0,
        ),
    )(*operands)


def ring(axis):
    count = lax.axis_size(axis)
    return [(i, (i + 1) % count) for i in range(count)], [((i + 1) % count, i) for i in range(count)]


def flip(array, flips, sizes):
    axes = tuple(sorted({axis for axis, _ in flips}, key=("gx", "gy", "ma").index))
    strides = {}
    count = 1
    for axis in reversed(axes):
        strides[axis] = count
        count *= sizes[axis]
    change = 0
    for axis, bit in flips:
        change |= strides[axis] << bit
    return lax.ppermute(array, axes, [(i, i ^ change) for i in range(count)])


def subsets(stage):
    for code in range(1, 1 << len(stage)):
        yield code, [stage[n] for n in range(len(stage)) if (code >> (len(stage) - 1 - n)) & 1]


def stages_of(sizes):
    order = send_order(sizes)
    return [[order[0]], order[1:3]] + [[entry] for entry in order[3:]]


def term_sum(terms, low, high):
    total = terms[0][low:high].astype(F32)
    for array in terms[1:]:
        total = total + array[low:high].astype(F32)
    return total


def sends(terms, count, stage):
    length = count >> len(stage)
    return [
        term_sum(terms, code * length, (code + 1) * length).astype(BF16)
        for code, _ in list(subsets(stage))[::-1]
    ]


def exchange(stage, sent, sizes):
    return [flip(array, flips, sizes) for array, (_, flips) in zip(sent, list(subsets(stage))[::-1])]


def combine_kernel(*refs, terms, pair):
    outs = refs[terms:]
    count, share, modes = refs[0].shape
    each = count // 2 // pair
    for above in range(2):
        for place in range(each):
            rows = pl.ds(above * (count // 2) + place * pair, pair)
            total = refs[0][rows].astype(F32)
            for ref in refs[1:terms]:
                total = total + ref[rows].astype(F32)
            total = total.reshape(pair * share, modes).T
            for swapped in range(2):
                out = outs[2 * above + swapped]
                out[place] = total[swapped * share : (swapped + 1) * share].astype(out.dtype)


def assemble_kernel(own_ref, above_ref, both_ref, swapped_ref, out_ref, *, pair):
    count, share, width = own_ref.shape
    first = lax.axis_index("ma") == 0
    for place in range(count):
        mine = own_ref[place] + above_ref[place].astype(F32)
        theirs = swapped_ref[place].astype(F32) + both_ref[place].astype(F32)
        low = jnp.where(first, mine, theirs)
        high = jnp.where(first, theirs, mine)
        for part in range(pair):
            lanes = slice(part * (width // pair), (part + 1) * (width // pair))
            out_ref[place * pair + part] = jnp.concatenate([low[:, lanes], high[:, lanes]], 1)


def sum_kernel(*refs):
    total = refs[0][...].astype(F32)
    for ref in refs[1:-1]:
        total = total + ref[...].astype(F32)
    refs[-1][...] = total


def summed(terms, count, cost):
    shape = (count, *terms[0].shape[1:])
    whole = pl.BlockSpec(shape, lambda g: (0,) * len(shape))
    return pl.pallas_call(
        sum_kernel,
        grid=(1,),
        out_shape=jax.ShapeDtypeStruct(shape, F32),
        in_specs=[whole] * len(terms),
        out_specs=whole,
        compiler_params=pltpu.CompilerParams(vmem_limit_bytes=16 << 20),
        cost_estimate=pl.CostEstimate(flops=cost, bytes_accessed=1024, transcendentals=0),
    )(*terms)


def finish(terms, count, stage, sizes):
    _, share, modes = terms[0].shape
    pair = 2 if count % 4 == 0 else 1
    places = count // 2 // pair
    shape = (places, share, pair * share)
    whole = lambda shape: pl.BlockSpec(shape, lambda g: (0,) * len(shape))
    parts = pl.pallas_call(
        functools.partial(combine_kernel, terms=len(terms), pair=pair),
        grid=(1,),
        out_shape=[jax.ShapeDtypeStruct(shape, dtype) for dtype in (F32, BF16, BF16, BF16)],
        in_specs=[whole((count, share, modes))] * len(terms),
        out_specs=[whole(shape)] * 4,
        compiler_params=pltpu.CompilerParams(vmem_limit_bytes=16 << 20),
        cost_estimate=pl.CostEstimate(flops=1, bytes_accessed=1024, transcendentals=0),
    )(*terms)
    stage = stage + [("ma", 0)]
    arrived = {code: flip(parts[code], flips, sizes) for code, flips in reversed(list(subsets(stage)))}
    return pl.pallas_call(
        functools.partial(assemble_kernel, pair=pair),
        out_shape=jax.ShapeDtypeStruct((places * pair, share, modes), F32),
        in_specs=[pl.BlockSpec(memory_space=pltpu.VMEM)] * 4,
        out_specs=pl.BlockSpec(memory_space=pltpu.VMEM),
        compiler_params=pltpu.CompilerParams(vmem_limit_bytes=16 << 20),
        cost_estimate=pl.CostEstimate(flops=1, bytes_accessed=1024, transcendentals=0),
    )(parts[0], arrived[2], arrived[3], arrived[1])


def shards(mode_fields, cell_volumes, sizes):
    barrier = lax.optimization_barrier
    own = jnp.transpose(mode_fields, (2, 0, 1, 3))
    row_count, _, share, _ = own.shape
    modes = 2 * share
    quarter = row_count // 4
    all_rows = tuple(range(row_count))
    inner_rows = all_rows[quarter : 3 * quarter]
    outer_rows = all_rows[:quarter] + all_rows[3 * quarter :]
    own_inner = own[quarter : 3 * quarter]
    own_outer = jnp.concatenate([own[:quarter], own[3 * quarter :]], 0)

    other_inner = flip(own_inner, [("ma", 0)], sizes)
    columns = jnp.stack([own[:, :, :, -1], own[:, :, :, 0]]).reshape(2, 3 * row_count, share)
    columns = lax.all_gather(columns, "gy")
    own_outer_held, edges, columns = barrier((own_outer, (own[-1:], own[:1]), columns))
    forward, backward = ring("gx")
    above = lax.ppermute(edges[0], "gx", forward)
    below = lax.ppermute(edges[1], "gx", backward)
    other_outer = flip(own_outer_held, [("ma", 0)], sizes)

    inner = [(own_inner, other_inner, slopes_of(own, inner_rows, columns), inner_rows)]
    so_far = partial_tensor(cell_volumes, inner, sizes, (1, 2, 5, 6, 3, 7))
    columns, so_far = barrier((columns, so_far))
    outer = [(own_outer, other_outer, slopes_of(own, outer_rows, columns, above, below), outer_rows)]
    stages = stages_of(sizes)
    count = modes // BLOCKS
    cell_count = mode_fields.shape[2] * mode_fields.shape[3]
    flips = dict(subsets(stages[1]))
    sent = partial_tensor(cell_volumes, outer, sizes, (7,), so_far, 5, BF16)
    cell_volumes, sent = barrier((cell_volumes, sent))
    arrived = flip(sent, stages[0], sizes)
    kept = partial_tensor(cell_volumes, outer, sizes, (3,), so_far, 4)
    sent = term_sum([kept, arrived], 0, count).astype(BF16)
    cell_volumes, sent = barrier((cell_volumes, sent))
    both = flip(sent, flips[3], sizes)

    sent = partial_tensor(cell_volumes, outer, sizes, (5, 6), so_far, 2, BF16, cost=1)
    cell_volumes, sent = barrier((cell_volumes, sent))
    arrived = flip(sent, stages[0], sizes)
    kept = partial_tensor(cell_volumes, outer, sizes, (1, 2), so_far, 0, cost=1)
    sent = [term_sum([kept, arrived], at * count, (at + 1) * count).astype(BF16) for at in range(2)]
    cell_volumes, sent = barrier((cell_volumes, sent))
    received = [flip(sent[1], flips[2], sizes), flip(sent[0], flips[1], sizes)]

    sent = partial_tensor(cell_volumes, inner + outer, sizes, (4,), dtype=BF16, cost=1)
    cell_volumes, sent, both = barrier((cell_volumes, sent, both))
    arrived = flip(sent, stages[0], sizes)
    kept = partial_tensor(cell_volumes, inner + outer, sizes, (0,), cost=1)
    received.append(both)
    terms = [summed(received, count, 16 * count * modes * share * cell_count), kept, arrived]
    for stage in stages[2:-1]:
        terms = terms + exchange(stage, sends(terms, count, stage), sizes)
        count = count >> len(stage)
    return finish(terms, count, stages[-1], sizes)


def solution(mesh):
    in_specs = (P(None, "ma", "gx", "gy"), P("gx", "gy"))
    out_specs = P(("gx", "gy"), "ma", None)
    body = functools.partial(shards, sizes=dict(mesh.shape))
    return jax.shard_map(body, mesh=mesh, in_specs=in_specs, out_specs=out_specs, check_vma=False)
```

```python
import functools
import math

import jax
import jax.numpy as jnp
from jax import lax
from jax.experimental import pallas as pl
from jax.experimental.pallas import tpu as pltpu
from jax.sharding import PartitionSpec as P

BF16 = jnp.bfloat16
F32 = jnp.float32
BLOCKS = 8


def bits_of(count):
    return count.bit_length() - 1


def send_order(sizes):
    order = []
    for axis in ("gy", "gx"):
        order += [(axis, bit) for bit in range(bits_of(sizes[axis]))]
    return order


def source_bits(sizes, rows_each):
    row_bits = bits_of(rows_each)
    base = {"gy": row_bits, "gx": row_bits + bits_of(sizes["gy"])}
    found = list(range(row_bits))
    for axis, bit in reversed(send_order(sizes)):
        found.append(base[axis] + bit)
    return found


def slopes_kernel(own_ref, columns_ref, *refs, rows):
    out_ref = refs[-1]
    last = own_ref.shape[0] - 1
    share, cells = own_ref.shape[2:]

    def edge(step):
        count = columns_ref.shape[0]
        at = lax.axis_index("gy") + step
        inside = jnp.logical_and(at >= 0, at < count)
        values = columns_ref[jnp.clip(at, 0, count - 1), 0 if step < 0 else 1].astype(F32)
        return jnp.where(inside, values, jnp.zeros_like(values)).T

    before, after = edge(-1), edge(1)
    here = lax.axis_index("gx")

    def outside(ref, edge_of_grid, a):
        values = ref[0, a].astype(F32)
        return jnp.where(here == edge_of_grid, jnp.zeros_like(values), values)

    lane = lax.broadcasted_iota(jnp.int32, (share, cells), 1)
    for place, x in enumerate(rows):
        for a in range(3):
            down = outside(refs[0], 0, a) if x == 0 else own_ref[x - 1, a].astype(F32)
            up = outside(refs[1], lax.axis_size("gx") - 1, a) if x == last else own_ref[x + 1, a].astype(F32)
            out_ref[place, a] = ((up - down) * 0.5).astype(BF16)
            value = own_ref[x, a].astype(F32)
            column = 3 * x + a
            down = jnp.where(lane == 0, before[:, column : column + 1], pltpu.roll(value, 1, 1))
            up = jnp.where(lane == cells - 1, after[:, column : column + 1], pltpu.roll(value, cells - 1, 1))
            out_ref[place, 3 + a] = ((up - down) * 0.5).astype(BF16)


def slopes_of(own, rows, *edges):
    _, _, share, cells = own.shape
    return pl.pallas_call(
        functools.partial(slopes_kernel, rows=rows),
        out_shape=jax.ShapeDtypeStruct((len(rows), 6, share, cells), BF16),
        in_specs=[pl.BlockSpec(memory_space=pltpu.VMEM)] * (1 + len(edges)),
        out_specs=pl.BlockSpec(memory_space=pltpu.VMEM),
        compiler_params=pltpu.CompilerParams(vmem_limit_bytes=16 << 20),
        cost_estimate=pl.CostEstimate(flops=1, bytes_accessed=1024, transcendentals=0),
    )(own, *edges)


def sum_of(left, right):
    return left[0] * right[0] + left[1] * right[1] + left[2] * right[2]


def tensor_kernel(*refs, bits, block, group, rows_each, blocks, rows, scale, has_before):
    left, right, out_ref = refs[-2], refs[-1], refs[-3]
    before_ref = refs[-4] if has_before else None
    volume_ref = refs[0]
    sets = [refs[1 + 3 * n : 4 + 3 * n] for n in range(len(rows))]
    _, _, share, cells = sets[0][0].shape
    places = [(n, x) for n in range(len(rows)) for x in range(len(rows[n]))]
    step = pl.program_id(0)
    top = bits_of(2 * share) - 1

    @pl.when(step == 0)
    def _():
        for place, (n, x) in enumerate(places):
            weight = volume_ref[pl.ds(rows[n][x], 1), :] * scale
            for half, ref in enumerate(sets[n][:2]):
                for a in range(3):
                    value = (weight * ref[x, a].astype(F32)).astype(BF16)
                    left[place, a, half * share : (half + 1) * share, :] = value.astype(F32)
                for b in range(2):
                    lanes = 2 * place + b
                    right[half * share : (half + 1) * share, lanes * cells : (lanes + 1) * cells] = ref[x, b]

    here = (lax.axis_index("gx") * lax.axis_size("gy") + lax.axis_index("gy")) * rows_each
    here = here ^ (lax.axis_index("ma") << top)
    tests = []
    for part in range(group):
        start = here
        position = block_at(blocks, step * group + part) * block
        for place, bit in enumerate(bits):
            start = start ^ (((position >> place) & 1) << bit)
        for row in range(block):
            offset = 0
            for place, bit in enumerate(bits):
                offset |= ((row >> place) & 1) << bit
            tests.append((start, offset))
    columns = []
    for place, (n, x) in enumerate(places):
        slopes = [sets[n][2][x, m] for m in range(6)]
        sums = [[], []]
        for start, offset in tests:
            test = [
                jnp.concatenate(
                    [left[place, a, pl.ds(start ^ offset, 16, stride=0), :].astype(BF16)] * (share // 16), 0
                )
                for a in range(3)
            ]
            for b, found in enumerate(sums):
                found.append(sum_of(test, slopes[3 * b : 3 * b + 3]))
        columns += [jnp.concatenate(found, 0) for found in sums]
    sums = jnp.concatenate(columns, 1)
    product = lax.dot_general(sums, right[...], (((1,), (1,)), ((), ())), preferred_element_type=F32)
    product = product.reshape(out_ref.shape)
    if before_ref is not None:
        product = product + before_ref[...]
    out_ref[...] = product.astype(out_ref.dtype)


def block_at(blocks, step):
    block = blocks[0] + step
    for n in range(1, len(blocks)):
        jump = blocks[n] - blocks[n - 1] - 1
        if jump:
            block = block + jnp.where(step >= n, jump, 0)
    return block


def partial_tensor(volumes, sets, sizes, blocks, before=None, first=0, dtype=F32, cost=8):
    _, _, share, cells = sets[0][0].shape
    modes = 2 * share
    block = modes // BLOCKS
    group = 2 if len(blocks) % 2 == 0 else 1
    devices = sizes["gx"] * sizes["gy"]
    rows_each = modes // devices
    row_count = sum(len(rows) for *_, rows in sets)
    body = functools.partial(
        tensor_kernel,
        bits=source_bits(sizes, rows_each),
        block=block,
        group=group,
        rows_each=rows_each,
        blocks=blocks,
        rows=[rows for *_, rows in sets],
        scale=1.0 / math.sqrt(volumes.shape[0] * volumes.shape[1] * devices),
        has_before=before is not None,
    )
    whole = lambda array: pl.BlockSpec(array.shape, lambda g: (0,) * array.ndim, pipeline_mode=pl.Buffered(1))
    shape = (group * block, share, modes)
    operands = [volumes] + [array for own, other, slopes, _ in sets for array in (own, other, slopes)]
    in_specs = [whole(array) for array in operands]
    if before is not None:
        operands.append(before)
        in_specs.append(pl.BlockSpec(shape, lambda g: (first // group + g, 0, 0)))
    result = pltpu.VMEM if len(blocks) > 2 else jax.ShapeDtypeStruct
    return pl.pallas_call(
        body,
        grid=(len(blocks) // group,),
        out_shape=result((len(blocks) * block, share, modes), dtype),
        in_specs=in_specs,
        out_specs=pl.BlockSpec(shape, lambda g: (g, 0, 0)),
        scratch_shapes=[
            pltpu.VMEM((row_count, 3, modes, cells), F32),
            pltpu.VMEM((modes, row_count * 2 * cells), BF16),
        ],
        compiler_params=pltpu.CompilerParams(vmem_limit_bytes=24 << 20),
        cost_estimate=pl.CostEstimate(
            flops=cost * len(blocks) * block * share * modes * row_count * cells,
            bytes_accessed=4 << 20,
            transcendentals=0,
        ),
    )(*operands)


def ring(axis):
    count = lax.axis_size(axis)
    return [(i, (i + 1) % count) for i in range(count)], [((i + 1) % count, i) for i in range(count)]


def flip(array, flips, sizes):
    axes = tuple(sorted({axis for axis, _ in flips}, key=("gx", "gy", "ma").index))
    strides = {}
    count = 1
    for axis in reversed(axes):
        strides[axis] = count
        count *= sizes[axis]
    change = 0
    for axis, bit in flips:
        change |= strides[axis] << bit
    return lax.ppermute(array, axes, [(i, i ^ change) for i in range(count)])


def subsets(stage):
    for code in range(1, 1 << len(stage)):
        yield code, [stage[n] for n in range(len(stage)) if (code >> (len(stage) - 1 - n)) & 1]


def stages_of(sizes):
    order = send_order(sizes)
    return [[order[0]], order[1:3]] + [[entry] for entry in order[3:]]


def term_sum(terms, low, high):
    total = terms[0][low:high].astype(F32)
    for array in terms[1:]:
        total = total + array[low:high].astype(F32)
    return total


def sends(terms, count, stage):
    length = count >> len(stage)
    return [
        term_sum(terms, code * length, (code + 1) * length).astype(BF16)
        for code, _ in list(subsets(stage))[::-1]
    ]


def exchange(stage, sent, sizes):
    return [flip(array, flips, sizes) for array, (_, flips) in zip(sent, list(subsets(stage))[::-1])]


def combine_kernel(*refs, terms, pair):
    outs = refs[terms:]
    count, share, modes = refs[0].shape
    each = count // 2 // pair
    for above in range(2):
        for place in range(each):
            rows = pl.ds(above * (count // 2) + place * pair, pair)
            total = refs[0][rows].astype(F32)
            for ref in refs[1:terms]:
                total = total + ref[rows].astype(F32)
            total = total.reshape(pair * share, modes).T
            for swapped in range(2):
                out = outs[2 * above + swapped]
                out[place] = total[swapped * share : (swapped + 1) * share].astype(out.dtype)


def assemble_kernel(own_ref, above_ref, both_ref, swapped_ref, out_ref, *, pair):
    count, share, width = own_ref.shape
    first = lax.axis_index("ma") == 0
    for place in range(count):
        mine = own_ref[place] + above_ref[place].astype(F32)
        theirs = swapped_ref[place].astype(F32) + both_ref[place].astype(F32)
        low = jnp.where(first, mine, theirs)
        high = jnp.where(first, theirs, mine)
        for part in range(pair):
            lanes = slice(part * (width // pair), (part + 1) * (width // pair))
            out_ref[place * pair + part] = jnp.concatenate([low[:, lanes], high[:, lanes]], 1)


def sum_kernel(*refs):
    total = refs[0][...].astype(F32)
    for ref in refs[1:-1]:
        total = total + ref[...].astype(F32)
    refs[-1][...] = total


def summed(terms, count, cost):
    shape = (count, *terms[0].shape[1:])
    whole = pl.BlockSpec(shape, lambda g: (0,) * len(shape))
    return pl.pallas_call(
        sum_kernel,
        grid=(1,),
        out_shape=jax.ShapeDtypeStruct(shape, F32),
        in_specs=[whole] * len(terms),
        out_specs=whole,
        compiler_params=pltpu.CompilerParams(vmem_limit_bytes=16 << 20),
        cost_estimate=pl.CostEstimate(flops=cost, bytes_accessed=1024, transcendentals=0),
    )(*terms)


def finish(terms, count, stage, sizes):
    _, share, modes = terms[0].shape
    pair = 2 if count % 4 == 0 else 1
    places = count // 2 // pair
    shape = (places, share, pair * share)
    whole = lambda shape: pl.BlockSpec(shape, lambda g: (0,) * len(shape))
    parts = pl.pallas_call(
        functools.partial(combine_kernel, terms=len(terms), pair=pair),
        grid=(1,),
        out_shape=[jax.ShapeDtypeStruct(shape, dtype) for dtype in (F32, BF16, BF16, BF16)],
        in_specs=[whole((count, share, modes))] * len(terms),
        out_specs=[whole(shape)] * 4,
        compiler_params=pltpu.CompilerParams(vmem_limit_bytes=16 << 20),
        cost_estimate=pl.CostEstimate(flops=1, bytes_accessed=1024, transcendentals=0),
    )(*terms)
    stage = stage + [("ma", 0)]
    arrived = {code: flip(parts[code], flips, sizes) for code, flips in reversed(list(subsets(stage)))}
    return pl.pallas_call(
        functools.partial(assemble_kernel, pair=pair),
        out_shape=jax.ShapeDtypeStruct((places * pair, share, modes), F32),
        in_specs=[pl.BlockSpec(memory_space=pltpu.VMEM)] * 4,
        out_specs=pl.BlockSpec(memory_space=pltpu.VMEM),
        compiler_params=pltpu.CompilerParams(vmem_limit_bytes=16 << 20),
        cost_estimate=pl.CostEstimate(flops=1, bytes_accessed=1024, transcendentals=0),
    )(parts[0], arrived[2], arrived[3], arrived[1])


def shards(mode_fields, cell_volumes, sizes):
    barrier = lax.optimization_barrier
    own = jnp.transpose(mode_fields, (2, 0, 1, 3))
    row_count, _, share, _ = own.shape
    modes = 2 * share
    quarter = row_count // 4
    all_rows = tuple(range(row_count))
    inner_rows = all_rows[quarter : 3 * quarter]
    outer_rows = all_rows[:quarter] + all_rows[3 * quarter :]
    own_inner = own[quarter : 3 * quarter]
    own_outer = jnp.concatenate([own[:quarter], own[3 * quarter :]], 0)

    other_inner = flip(own_inner, [("ma", 0)], sizes)
    columns = jnp.stack([own[:, :, :, -1], own[:, :, :, 0]]).reshape(2, 3 * row_count, share)
    columns = lax.all_gather(columns, "gy")
    own_outer_held, columns = barrier((own_outer, columns))
    slopes_inner = slopes_of(own, inner_rows, columns)
    edges, slopes_inner = barrier(((own[-1:], own[:1]), slopes_inner))
    forward, backward = ring("gx")
    above = lax.ppermute(edges[0], "gx", forward)
    below = lax.ppermute(edges[1], "gx", backward)
    other_outer = flip(own_outer_held, [("ma", 0)], sizes)

    inner = [(own_inner, other_inner, slopes_inner, inner_rows)]
    so_far = partial_tensor(cell_volumes, inner, sizes, (1, 2, 5, 6, 3, 7))
    columns, so_far = barrier((columns, so_far))
    outer = [(own_outer, other_outer, slopes_of(own, outer_rows, columns, above, below), outer_rows)]
    stages = stages_of(sizes)
    count = modes // BLOCKS
    cell_count = mode_fields.shape[2] * mode_fields.shape[3]
    flips = dict(subsets(stages[1]))
    sent = partial_tensor(cell_volumes, outer, sizes, (7,), so_far, 5, BF16)
    cell_volumes, sent = barrier((cell_volumes, sent))
    arrived = flip(sent, stages[0], sizes)
    kept = partial_tensor(cell_volumes, outer, sizes, (3,), so_far, 4)
    sent = term_sum([kept, arrived], 0, count).astype(BF16)
    cell_volumes, sent = barrier((cell_volumes, sent))
    both = flip(sent, flips[3], sizes)

    sent = partial_tensor(cell_volumes, outer, sizes, (5, 6), so_far, 2, BF16, cost=1)
    cell_volumes, sent = barrier((cell_volumes, sent))
    arrived = flip(sent, stages[0], sizes)
    kept = partial_tensor(cell_volumes, outer, sizes, (1, 2), so_far, 0, cost=1)
    sent = [term_sum([kept, arrived], at * count, (at + 1) * count).astype(BF16) for at in range(2)]
    cell_volumes, sent = barrier((cell_volumes, sent))
    received = [flip(sent[1], flips[2], sizes), flip(sent[0], flips[1], sizes)]

    sent = partial_tensor(cell_volumes, inner + outer, sizes, (4,), dtype=BF16, cost=1)
    cell_volumes, sent, both = barrier((cell_volumes, sent, both))
    arrived = flip(sent, stages[0], sizes)
    kept = partial_tensor(cell_volumes, inner + outer, sizes, (0,), cost=1)
    received.append(both)
    terms = [summed(received, count, 16 * count * modes * share * cell_count), kept, arrived]
    for stage in stages[2:-1]:
        terms = terms + exchange(stage, sends(terms, count, stage), sizes)
        count = count >> len(stage)
    return finish(terms, count, stages[-1], sizes)


def solution(mesh):
    in_specs = (P(None, "ma", "gx", "gy"), P("gx", "gy"))
    out_specs = P(("gx", "gy"), "ma", None)
    body = functools.partial(shards, sizes=dict(mesh.shape))
    return jax.shard_map(body, mesh=mesh, in_specs=in_specs, out_specs=out_specs, check_vma=False)
```

```python
import functools
import math

import jax
import jax.numpy as jnp
from jax import lax
from jax.experimental import pallas as pl
from jax.experimental.pallas import tpu as pltpu
from jax.sharding import PartitionSpec as P

BF16 = jnp.bfloat16
F32 = jnp.float32
BLOCKS = 8


def bits_of(count):
    return count.bit_length() - 1


def send_order(sizes):
    order = []
    for axis in ("gy", "gx"):
        order += [(axis, bit) for bit in range(bits_of(sizes[axis]))]
    return order


def source_bits(sizes, rows_each):
    row_bits = bits_of(rows_each)
    base = {"gy": row_bits, "gx": row_bits + bits_of(sizes["gy"])}
    found = list(range(row_bits))
    for axis, bit in reversed(send_order(sizes)):
        found.append(base[axis] + bit)
    return found


def slopes_kernel(own_ref, columns_ref, *refs, rows):
    out_ref = refs[-1]
    last = own_ref.shape[0] - 1
    share, cells = own_ref.shape[2:]

    def edge(step):
        count = columns_ref.shape[0]
        at = lax.axis_index("gy") + step
        inside = jnp.logical_and(at >= 0, at < count)
        values = columns_ref[jnp.clip(at, 0, count - 1), 0 if step < 0 else 1].astype(F32)
        return jnp.where(inside, values, jnp.zeros_like(values)).T

    before, after = edge(-1), edge(1)
    here = lax.axis_index("gx")

    def outside(ref, edge_of_grid, a):
        values = ref[0, a].astype(F32)
        return jnp.where(here == edge_of_grid, jnp.zeros_like(values), values)

    lane = lax.broadcasted_iota(jnp.int32, (share, cells), 1)
    for place, x in enumerate(rows):
        for a in range(3):
            down = outside(refs[0], 0, a) if x == 0 else own_ref[x - 1, a].astype(F32)
            up = outside(refs[1], lax.axis_size("gx") - 1, a) if x == last else own_ref[x + 1, a].astype(F32)
            out_ref[place, a] = ((up - down) * 0.5).astype(BF16)
            value = own_ref[x, a].astype(F32)
            column = 3 * x + a
            down = jnp.where(lane == 0, before[:, column : column + 1], pltpu.roll(value, 1, 1))
            up = jnp.where(lane == cells - 1, after[:, column : column + 1], pltpu.roll(value, cells - 1, 1))
            out_ref[place, 3 + a] = ((up - down) * 0.5).astype(BF16)


def slopes_of(own, rows, *edges):
    _, _, share, cells = own.shape
    return pl.pallas_call(
        functools.partial(slopes_kernel, rows=rows),
        out_shape=jax.ShapeDtypeStruct((len(rows), 6, share, cells), BF16),
        in_specs=[pl.BlockSpec(memory_space=pltpu.VMEM)] * (1 + len(edges)),
        out_specs=pl.BlockSpec(memory_space=pltpu.VMEM),
        compiler_params=pltpu.CompilerParams(vmem_limit_bytes=16 << 20),
        cost_estimate=pl.CostEstimate(flops=1, bytes_accessed=1024, transcendentals=0),
    )(own, *edges)


def sum_of(left, right):
    return left[0] * right[0] + left[1] * right[1] + left[2] * right[2]


def tensor_kernel(*refs, bits, block, group, rows_each, blocks, rows, scale, has_before):
    left, right, out_ref = refs[-2], refs[-1], refs[-3]
    before_ref = refs[-4] if has_before else None
    volume_ref = refs[0]
    sets = [refs[1 + 3 * n : 4 + 3 * n] for n in range(len(rows))]
    _, _, share, cells = sets[0][0].shape
    places = [(n, x) for n in range(len(rows)) for x in range(len(rows[n]))]
    step = pl.program_id(0)
    top = bits_of(2 * share) - 1

    @pl.when(step == 0)
    def _():
        for place, (n, x) in enumerate(places):
            weight = volume_ref[pl.ds(rows[n][x], 1), :] * scale
            for half, ref in enumerate(sets[n][:2]):
                for a in range(3):
                    value = (weight * ref[x, a].astype(F32)).astype(BF16)
                    left[place, a, half * share : (half + 1) * share, :] = value.astype(F32)
                for b in range(2):
                    lanes = 2 * place + b
                    right[half * share : (half + 1) * share, lanes * cells : (lanes + 1) * cells] = ref[x, b]

    here = (lax.axis_index("gx") * lax.axis_size("gy") + lax.axis_index("gy")) * rows_each
    here = here ^ (lax.axis_index("ma") << top)
    tests = []
    for part in range(group):
        start = here
        position = block_at(blocks, step * group + part) * block
        for place, bit in enumerate(bits):
            start = start ^ (((position >> place) & 1) << bit)
        for row in range(block):
            offset = 0
            for place, bit in enumerate(bits):
                offset |= ((row >> place) & 1) << bit
            tests.append((start, offset))
    columns = []
    for place, (n, x) in enumerate(places):
        slopes = [sets[n][2][x, m] for m in range(6)]
        sums = [[], []]
        for start, offset in tests:
            test = [
                jnp.concatenate(
                    [left[place, a, pl.ds(start ^ offset, 16, stride=0), :].astype(BF16)] * (share // 16), 0
                )
                for a in range(3)
            ]
            for b, found in enumerate(sums):
                found.append(sum_of(test, slopes[3 * b : 3 * b + 3]))
        columns += [jnp.concatenate(found, 0) for found in sums]
    sums = jnp.concatenate(columns, 1)
    product = lax.dot_general(sums, right[...], (((1,), (1,)), ((), ())), preferred_element_type=F32)
    product = product.reshape(out_ref.shape)
    if before_ref is not None:
        product = product + before_ref[...]
    out_ref[...] = product.astype(out_ref.dtype)


def block_at(blocks, step):
    block = blocks[0] + step
    for n in range(1, len(blocks)):
        jump = blocks[n] - blocks[n - 1] - 1
        if jump:
            block = block + jnp.where(step >= n, jump, 0)
    return block


def partial_tensor(volumes, sets, sizes, blocks, before=None, first=0, dtype=F32, cost=8):
    _, _, share, cells = sets[0][0].shape
    modes = 2 * share
    block = modes // BLOCKS
    group = 2 if len(blocks) % 2 == 0 else 1
    devices = sizes["gx"] * sizes["gy"]
    rows_each = modes // devices
    row_count = sum(len(rows) for *_, rows in sets)
    body = functools.partial(
        tensor_kernel,
        bits=source_bits(sizes, rows_each),
        block=block,
        group=group,
        rows_each=rows_each,
        blocks=blocks,
        rows=[rows for *_, rows in sets],
        scale=1.0 / math.sqrt(volumes.shape[0] * volumes.shape[1] * devices),
        has_before=before is not None,
    )
    whole = lambda array: pl.BlockSpec(array.shape, lambda g: (0,) * array.ndim, pipeline_mode=pl.Buffered(1))
    shape = (group * block, share, modes)
    operands = [volumes] + [array for own, other, slopes, _ in sets for array in (own, other, slopes)]
    in_specs = [whole(array) for array in operands]
    if before is not None:
        operands.append(before)
        in_specs.append(pl.BlockSpec(shape, lambda g: (first // group + g, 0, 0)))
    result = pltpu.VMEM if len(blocks) > 2 else jax.ShapeDtypeStruct
    return pl.pallas_call(
        body,
        grid=(len(blocks) // group,),
        out_shape=result((len(blocks) * block, share, modes), dtype),
        in_specs=in_specs,
        out_specs=pl.BlockSpec(shape, lambda g: (g, 0, 0)),
        scratch_shapes=[
            pltpu.VMEM((row_count, 3, modes + 16, cells), F32),
            pltpu.VMEM((modes, row_count * 2 * cells), BF16),
        ],
        compiler_params=pltpu.CompilerParams(vmem_limit_bytes=24 << 20),
        cost_estimate=pl.CostEstimate(
            flops=cost * len(blocks) * block * share * modes * row_count * cells,
            bytes_accessed=4 << 20,
            transcendentals=0,
        ),
    )(*operands)


def ring(axis):
    count = lax.axis_size(axis)
    return [(i, (i + 1) % count) for i in range(count)], [((i + 1) % count, i) for i in range(count)]


def flip(array, flips, sizes):
    axes = tuple(sorted({axis for axis, _ in flips}, key=("gx", "gy", "ma").index))
    strides = {}
    count = 1
    for axis in reversed(axes):
        strides[axis] = count
        count *= sizes[axis]
    change = 0
    for axis, bit in flips:
        change |= strides[axis] << bit
    return lax.ppermute(array, axes, [(i, i ^ change) for i in range(count)])


def subsets(stage):
    for code in range(1, 1 << len(stage)):
        yield code, [stage[n] for n in range(len(stage)) if (code >> (len(stage) - 1 - n)) & 1]


def stages_of(sizes):
    order = send_order(sizes)
    return [[order[0]], order[1:3]] + [[entry] for entry in order[3:]]


def term_sum(terms, low, high):
    total = terms[0][low:high].astype(F32)
    for array in terms[1:]:
        total = total + array[low:high].astype(F32)
    return total


def sends(terms, count, stage):
    length = count >> len(stage)
    return [
        term_sum(terms, code * length, (code + 1) * length).astype(BF16)
        for code, _ in list(subsets(stage))[::-1]
    ]


def exchange(stage, sent, sizes):
    return [flip(array, flips, sizes) for array, (_, flips) in zip(sent, list(subsets(stage))[::-1])]


def combine_kernel(*refs, terms, pair):
    outs = refs[terms:]
    count, share, modes = refs[0].shape
    each = count // 2 // pair
    for above in range(2):
        for place in range(each):
            rows = pl.ds(above * (count // 2) + place * pair, pair)
            total = refs[0][rows].astype(F32)
            for ref in refs[1:terms]:
                total = total + ref[rows].astype(F32)
            total = total.reshape(pair * share, modes).T
            for swapped in range(2):
                out = outs[2 * above + swapped]
                out[place] = total[swapped * share : (swapped + 1) * share].astype(out.dtype)


def assemble_kernel(own_ref, above_ref, both_ref, swapped_ref, out_ref, *, pair):
    count, share, width = own_ref.shape
    first = lax.axis_index("ma") == 0
    for place in range(count):
        mine = own_ref[place] + above_ref[place].astype(F32)
        theirs = swapped_ref[place].astype(F32) + both_ref[place].astype(F32)
        low = jnp.where(first, mine, theirs)
        high = jnp.where(first, theirs, mine)
        for part in range(pair):
            lanes = slice(part * (width // pair), (part + 1) * (width // pair))
            out_ref[place * pair + part] = jnp.concatenate([low[:, lanes], high[:, lanes]], 1)


def sum_kernel(*refs):
    total = refs[0][...].astype(F32)
    for ref in refs[1:-1]:
        total = total + ref[...].astype(F32)
    refs[-1][...] = total


def summed(terms, count, cost):
    shape = (count, *terms[0].shape[1:])
    whole = pl.BlockSpec(shape, lambda g: (0,) * len(shape))
    return pl.pallas_call(
        sum_kernel,
        grid=(1,),
        out_shape=jax.ShapeDtypeStruct(shape, F32),
        in_specs=[whole] * len(terms),
        out_specs=whole,
        compiler_params=pltpu.CompilerParams(vmem_limit_bytes=16 << 20),
        cost_estimate=pl.CostEstimate(flops=cost, bytes_accessed=1024, transcendentals=0),
    )(*terms)


def finish(terms, count, stage, sizes):
    _, share, modes = terms[0].shape
    pair = 2 if count % 4 == 0 else 1
    places = count // 2 // pair
    shape = (places, share, pair * share)
    whole = lambda shape: pl.BlockSpec(shape, lambda g: (0,) * len(shape))
    parts = pl.pallas_call(
        functools.partial(combine_kernel, terms=len(terms), pair=pair),
        grid=(1,),
        out_shape=[jax.ShapeDtypeStruct(shape, dtype) for dtype in (F32, BF16, BF16, BF16)],
        in_specs=[whole((count, share, modes))] * len(terms),
        out_specs=[whole(shape)] * 4,
        compiler_params=pltpu.CompilerParams(vmem_limit_bytes=16 << 20),
        cost_estimate=pl.CostEstimate(flops=1, bytes_accessed=1024, transcendentals=0),
    )(*terms)
    stage = stage + [("ma", 0)]
    arrived = {code: flip(parts[code], flips, sizes) for code, flips in reversed(list(subsets(stage)))}
    return pl.pallas_call(
        functools.partial(assemble_kernel, pair=pair),
        out_shape=jax.ShapeDtypeStruct((places * pair, share, modes), F32),
        in_specs=[pl.BlockSpec(memory_space=pltpu.VMEM)] * 4,
        out_specs=pl.BlockSpec(memory_space=pltpu.VMEM),
        compiler_params=pltpu.CompilerParams(vmem_limit_bytes=16 << 20),
        cost_estimate=pl.CostEstimate(flops=1, bytes_accessed=1024, transcendentals=0),
    )(parts[0], arrived[2], arrived[3], arrived[1])


def shards(mode_fields, cell_volumes, sizes):
    barrier = lax.optimization_barrier
    own = jnp.transpose(mode_fields, (2, 0, 1, 3))
    row_count, _, share, _ = own.shape
    modes = 2 * share
    quarter = row_count // 4
    all_rows = tuple(range(row_count))
    inner_rows = all_rows[quarter : 3 * quarter]
    outer_rows = all_rows[:quarter] + all_rows[3 * quarter :]
    own_inner = own[quarter : 3 * quarter]
    own_outer = jnp.concatenate([own[:quarter], own[3 * quarter :]], 0)

    other_inner = flip(own_inner, [("ma", 0)], sizes)
    columns = jnp.stack([own[:, :, :, -1], own[:, :, :, 0]]).reshape(2, 3 * row_count, share)
    columns = lax.all_gather(columns, "gy")
    own_outer_held, columns = barrier((own_outer, columns))
    slopes_inner = slopes_of(own, inner_rows, columns)
    edges, slopes_inner = barrier(((own[-1:], own[:1]), slopes_inner))
    forward, backward = ring("gx")
    above = lax.ppermute(edges[0], "gx", forward)
    below = lax.ppermute(edges[1], "gx", backward)
    other_outer = flip(own_outer_held, [("ma", 0)], sizes)

    inner = [(own_inner, other_inner, slopes_inner, inner_rows)]
    so_far = partial_tensor(cell_volumes, inner, sizes, (1, 2, 5, 6, 3, 7))
    columns, so_far = barrier((columns, so_far))
    outer = [(own_outer, other_outer, slopes_of(own, outer_rows, columns, above, below), outer_rows)]
    stages = stages_of(sizes)
    count = modes // BLOCKS
    cell_count = mode_fields.shape[2] * mode_fields.shape[3]
    flips = dict(subsets(stages[1]))
    sent = partial_tensor(cell_volumes, outer, sizes, (7,), so_far, 5, BF16)
    cell_volumes, sent = barrier((cell_volumes, sent))
    arrived = flip(sent, stages[0], sizes)
    kept = partial_tensor(cell_volumes, outer, sizes, (3,), so_far, 4)
    sent = term_sum([kept, arrived], 0, count).astype(BF16)
    cell_volumes, sent = barrier((cell_volumes, sent))
    both = flip(sent, flips[3], sizes)

    sent = partial_tensor(cell_volumes, outer, sizes, (5, 6), so_far, 2, BF16, cost=1)
    cell_volumes, sent = barrier((cell_volumes, sent))
    arrived = flip(sent, stages[0], sizes)
    kept = partial_tensor(cell_volumes, outer, sizes, (1, 2), so_far, 0, cost=1)
    sent = [term_sum([kept, arrived], at * count, (at + 1) * count).astype(BF16) for at in range(2)]
    cell_volumes, sent = barrier((cell_volumes, sent))
    received = [flip(sent[1], flips[2], sizes), flip(sent[0], flips[1], sizes)]

    sent = partial_tensor(cell_volumes, inner + outer, sizes, (4,), dtype=BF16, cost=1)
    cell_volumes, sent, both = barrier((cell_volumes, sent, both))
    arrived = flip(sent, stages[0], sizes)
    kept = partial_tensor(cell_volumes, inner + outer, sizes, (0,), cost=1)
    received.append(both)
    terms = [summed(received, count, 16 * count * modes * share * cell_count), kept, arrived]
    for stage in stages[2:-1]:
        terms = terms + exchange(stage, sends(terms, count, stage), sizes)
        count = count >> len(stage)
    return finish(terms, count, stages[-1], sizes)


def solution(mesh):
    in_specs = (P(None, "ma", "gx", "gy"), P("gx", "gy"))
    out_specs = P(("gx", "gy"), "ma", None)
    body = functools.partial(shards, sizes=dict(mesh.shape))
    return jax.shard_map(body, mesh=mesh, in_specs=in_specs, out_specs=out_specs, check_vma=False)
```

```python
import functools
import math

import jax
import jax.numpy as jnp
from jax import lax
from jax.experimental import pallas as pl
from jax.experimental.pallas import tpu as pltpu
from jax.sharding import PartitionSpec as P

BF16 = jnp.bfloat16
F32 = jnp.float32
BLOCKS = 8


def bits_of(count):
    return count.bit_length() - 1


def send_order(sizes):
    order = []
    for axis in ("gy", "gx"):
        order += [(axis, bit) for bit in range(bits_of(sizes[axis]))]
    return order


def source_bits(sizes, rows_each):
    row_bits = bits_of(rows_each)
    base = {"gy": row_bits, "gx": row_bits + bits_of(sizes["gy"])}
    found = list(range(row_bits))
    for axis, bit in reversed(send_order(sizes)):
        found.append(base[axis] + bit)
    return found


def slopes_kernel(own_ref, columns_ref, *refs, rows):
    out_ref = refs[-1]
    last = own_ref.shape[0] - 1
    share, cells = own_ref.shape[2:]

    def edge(step):
        count = columns_ref.shape[0]
        at = lax.axis_index("gy") + step
        inside = jnp.logical_and(at >= 0, at < count)
        values = columns_ref[jnp.clip(at, 0, count - 1), 0 if step < 0 else 1].astype(F32)
        return jnp.where(inside, values, jnp.zeros_like(values)).T

    before, after = edge(-1), edge(1)
    here = lax.axis_index("gx")

    def outside(ref, edge_of_grid, a):
        values = ref[0, a].astype(F32)
        return jnp.where(here == edge_of_grid, jnp.zeros_like(values), values)

    lane = lax.broadcasted_iota(jnp.int32, (share, cells), 1)
    for place, x in enumerate(rows):
        for a in range(3):
            down = outside(refs[0], 0, a) if x == 0 else own_ref[x - 1, a].astype(F32)
            up = outside(refs[1], lax.axis_size("gx") - 1, a) if x == last else own_ref[x + 1, a].astype(F32)
            out_ref[place, a] = ((up - down) * 0.5).astype(BF16)
            value = own_ref[x, a].astype(F32)
            column = 3 * x + a
            down = jnp.where(lane == 0, before[:, column : column + 1], pltpu.roll(value, 1, 1))
            up = jnp.where(lane == cells - 1, after[:, column : column + 1], pltpu.roll(value, cells - 1, 1))
            out_ref[place, 3 + a] = ((up - down) * 0.5).astype(BF16)


def slopes_of(own, rows, *edges):
    _, _, share, cells = own.shape
    return pl.pallas_call(
        functools.partial(slopes_kernel, rows=rows),
        out_shape=jax.ShapeDtypeStruct((len(rows), 6, share, cells), BF16),
        in_specs=[pl.BlockSpec(memory_space=pltpu.VMEM)] * (1 + len(edges)),
        out_specs=pl.BlockSpec(memory_space=pltpu.VMEM),
        compiler_params=pltpu.CompilerParams(vmem_limit_bytes=16 << 20),
        cost_estimate=pl.CostEstimate(flops=1, bytes_accessed=1024, transcendentals=0),
    )(own, *edges)


def sum_of(left, right):
    return left[0] * right[0] + left[1] * right[1] + left[2] * right[2]


def tensor_kernel(*refs, bits, block, group, rows_each, blocks, rows, scale, has_before):
    left, right, out_ref = refs[-2], refs[-1], refs[-3]
    before_ref = refs[-4] if has_before else None
    volume_ref = refs[0]
    sets = [refs[1 + 3 * n : 4 + 3 * n] for n in range(len(rows))]
    _, _, share, cells = sets[0][0].shape
    places = [(n, x) for n in range(len(rows)) for x in range(len(rows[n]))]
    step = pl.program_id(0)
    top = bits_of(2 * share) - 1

    @pl.when(step == 0)
    def _():
        for place, (n, x) in enumerate(places):
            weight = volume_ref[pl.ds(rows[n][x], 1), :] * scale
            for half, ref in enumerate(sets[n][:2]):
                for a in range(3):
                    value = (weight * ref[x, a].astype(F32)).astype(BF16)
                    left[place, a, half * share : (half + 1) * share, :] = value.astype(F32)
                for b in range(2):
                    lanes = 2 * place + b
                    right[half * share : (half + 1) * share, lanes * cells : (lanes + 1) * cells] = ref[x, b]

    here = (lax.axis_index("gx") * lax.axis_size("gy") + lax.axis_index("gy")) * rows_each
    here = here ^ (lax.axis_index("ma") << top)
    tests = []
    for part in range(group):
        start = here
        position = block_at(blocks, step * group + part) * block
        for place, bit in enumerate(bits):
            start = start ^ (((position >> place) & 1) << bit)
        for row in range(block):
            offset = 0
            for place, bit in enumerate(bits):
                offset |= ((row >> place) & 1) << bit
            tests.append((start, offset))
    columns = []
    for place, (n, x) in enumerate(places):
        slopes = [sets[n][2][x, m] for m in range(6)]
        sums = [[], []]
        for start, offset in tests:
            test = [
                jnp.concatenate(
                    [left[place, a, pl.ds(start ^ offset, 16, stride=0), :].astype(BF16)] * (share // 16), 0
                )
                for a in range(3)
            ]
            for b, found in enumerate(sums):
                found.append(sum_of(test, slopes[3 * b : 3 * b + 3]))
        columns += [jnp.concatenate(found, 0) for found in sums]
    sums = jnp.concatenate(columns, 1)
    product = lax.dot_general(sums, right[...], (((1,), (1,)), ((), ())), preferred_element_type=F32)
    product = product.reshape(out_ref.shape)
    if before_ref is not None:
        product = product + before_ref[...]
    out_ref[...] = product.astype(out_ref.dtype)


def block_at(blocks, step):
    block = blocks[0] + step
    for n in range(1, len(blocks)):
        jump = blocks[n] - blocks[n - 1] - 1
        if jump:
            block = block + jnp.where(step >= n, jump, 0)
    return block


def partial_tensor(volumes, sets, sizes, blocks, before=None, first=0, dtype=F32, cost=8):
    _, _, share, cells = sets[0][0].shape
    modes = 2 * share
    block = modes // BLOCKS
    group = 2 if len(blocks) % 2 == 0 else 1
    devices = sizes["gx"] * sizes["gy"]
    rows_each = modes // devices
    row_count = sum(len(rows) for *_, rows in sets)
    body = functools.partial(
        tensor_kernel,
        bits=source_bits(sizes, rows_each),
        block=block,
        group=group,
        rows_each=rows_each,
        blocks=blocks,
        rows=[rows for *_, rows in sets],
        scale=1.0 / math.sqrt(volumes.shape[0] * volumes.shape[1] * devices),
        has_before=before is not None,
    )
    whole = lambda array: pl.BlockSpec(array.shape, lambda g: (0,) * array.ndim, pipeline_mode=pl.Buffered(1))
    shape = (group * block, share, modes)
    operands = [volumes] + [array for own, other, slopes, _ in sets for array in (own, other, slopes)]
    in_specs = [whole(array) for array in operands]
    if before is not None:
        operands.append(before)
        in_specs.append(pl.BlockSpec(shape, lambda g: (first // group + g, 0, 0)))
    result = pltpu.VMEM if len(blocks) > 2 else jax.ShapeDtypeStruct
    return pl.pallas_call(
        body,
        grid=(len(blocks) // group,),
        out_shape=result((len(blocks) * block, share, modes), dtype),
        in_specs=in_specs,
        out_specs=pl.BlockSpec(shape, lambda g: (g, 0, 0)),
        scratch_shapes=[
            pltpu.VMEM((row_count, 3, modes + 16, cells), F32),
            pltpu.VMEM((modes, row_count * 2 * cells), BF16),
        ],
        compiler_params=pltpu.CompilerParams(vmem_limit_bytes=24 << 20),
        cost_estimate=pl.CostEstimate(
            flops=cost * len(blocks) * block * share * modes * row_count * cells,
            bytes_accessed=4 << 20,
            transcendentals=0,
        ),
    )(*operands)


def ring(axis):
    count = lax.axis_size(axis)
    return [(i, (i + 1) % count) for i in range(count)], [((i + 1) % count, i) for i in range(count)]


def flip(array, flips, sizes):
    axes = tuple(sorted({axis for axis, _ in flips}, key=("gx", "gy", "ma").index))
    strides = {}
    count = 1
    for axis in reversed(axes):
        strides[axis] = count
        count *= sizes[axis]
    change = 0
    for axis, bit in flips:
        change |= strides[axis] << bit
    return lax.ppermute(array, axes, [(i, i ^ change) for i in range(count)])


def subsets(stage):
    for code in range(1, 1 << len(stage)):
        yield code, [stage[n] for n in range(len(stage)) if (code >> (len(stage) - 1 - n)) & 1]


def stages_of(sizes):
    order = send_order(sizes)
    return [[order[0]], order[1:3]] + [[entry] for entry in order[3:]]


def term_sum(terms, low, high):
    total = terms[0][low:high].astype(F32)
    for array in terms[1:]:
        total = total + array[low:high].astype(F32)
    return total


def sends(terms, count, stage):
    length = count >> len(stage)
    return [
        term_sum(terms, code * length, (code + 1) * length).astype(BF16)
        for code, _ in list(subsets(stage))[::-1]
    ]


def exchange(stage, sent, sizes):
    return [flip(array, flips, sizes) for array, (_, flips) in zip(sent, list(subsets(stage))[::-1])]


def combine_kernel(*refs, terms, pair):
    outs = refs[terms:]
    count, share, modes = refs[0].shape
    each = count // 2 // pair
    for above in range(2):
        for place in range(each):
            rows = pl.ds(above * (count // 2) + place * pair, pair)
            total = refs[0][rows].astype(F32)
            for ref in refs[1:terms]:
                total = total + ref[rows].astype(F32)
            total = total.reshape(pair * share, modes).T
            for swapped in range(2):
                out = outs[2 * above + swapped]
                out[place] = total[swapped * share : (swapped + 1) * share].astype(out.dtype)


def assemble_kernel(own_ref, both_ref, above_ref, swapped_ref, out_ref, *, pair):
    count, share, width = own_ref.shape
    first = lax.axis_index("ma") == 0
    for place in range(count):
        mine = own_ref[place] + above_ref[place].astype(F32)
        theirs = swapped_ref[place].astype(F32) + both_ref[place].astype(F32)
        low = jnp.where(first, mine, theirs)
        high = jnp.where(first, theirs, mine)
        for part in range(pair):
            lanes = slice(part * (width // pair), (part + 1) * (width // pair))
            out_ref[place * pair + part] = jnp.concatenate([low[:, lanes], high[:, lanes]], 1)


def sum_kernel(*refs):
    total = refs[0][...].astype(F32)
    for ref in refs[1:-1]:
        total = total + ref[...].astype(F32)
    refs[-1][...] = total


def summed(terms, count, cost):
    shape = (count, *terms[0].shape[1:])
    whole = pl.BlockSpec(shape, lambda g: (0,) * len(shape))
    return pl.pallas_call(
        sum_kernel,
        grid=(1,),
        out_shape=jax.ShapeDtypeStruct(shape, F32),
        in_specs=[whole] * len(terms),
        out_specs=whole,
        compiler_params=pltpu.CompilerParams(vmem_limit_bytes=16 << 20),
        cost_estimate=pl.CostEstimate(flops=cost, bytes_accessed=1024, transcendentals=0),
    )(*terms)


def finish(terms, count, stage, sizes):
    _, share, modes = terms[0].shape
    pair = 2 if count % 4 == 0 else 1
    places = count // 2 // pair
    shape = (places, share, pair * share)
    whole = lambda shape: pl.BlockSpec(shape, lambda g: (0,) * len(shape))
    parts = pl.pallas_call(
        functools.partial(combine_kernel, terms=len(terms), pair=pair),
        grid=(1,),
        out_shape=[jax.ShapeDtypeStruct(shape, dtype) for dtype in (F32, BF16, BF16, BF16)],
        in_specs=[whole((count, share, modes))] * len(terms),
        out_specs=[whole(shape)] * 4,
        compiler_params=pltpu.CompilerParams(vmem_limit_bytes=16 << 20),
        cost_estimate=pl.CostEstimate(flops=1, bytes_accessed=1024, transcendentals=0),
    )(*terms)
    stage = stage + [("ma", 0)]
    arrived = {code: flip(parts[code], flips, sizes) for code, flips in reversed(list(subsets(stage)))}
    return pl.pallas_call(
        functools.partial(assemble_kernel, pair=pair),
        out_shape=jax.ShapeDtypeStruct((places * pair, share, modes), F32),
        in_specs=[pl.BlockSpec(memory_space=pltpu.VMEM)] * 4,
        out_specs=pl.BlockSpec(memory_space=pltpu.VMEM),
        compiler_params=pltpu.CompilerParams(vmem_limit_bytes=16 << 20),
        cost_estimate=pl.CostEstimate(flops=1, bytes_accessed=1024, transcendentals=0),
    )(parts[0], arrived[3], arrived[2], arrived[1])


def shards(mode_fields, cell_volumes, sizes):
    barrier = lax.optimization_barrier
    own = jnp.transpose(mode_fields, (2, 0, 1, 3))
    row_count, _, share, _ = own.shape
    modes = 2 * share
    quarter = row_count // 4
    all_rows = tuple(range(row_count))
    inner_rows = all_rows[quarter : 3 * quarter]
    outer_rows = all_rows[:quarter] + all_rows[3 * quarter :]
    own_inner = own[quarter : 3 * quarter]
    own_outer = jnp.concatenate([own[:quarter], own[3 * quarter :]], 0)

    other_inner = flip(own_inner, [("ma", 0)], sizes)
    columns = jnp.stack([own[:, :, :, -1], own[:, :, :, 0]]).reshape(2, 3 * row_count, share)
    columns = lax.all_gather(columns, "gy")
    own_outer_held, columns = barrier((own_outer, columns))
    slopes_inner = slopes_of(own, inner_rows, columns)
    edges, slopes_inner = barrier(((own[-1:], own[:1]), slopes_inner))
    forward, backward = ring("gx")
    above = lax.ppermute(edges[0], "gx", forward)
    below = lax.ppermute(edges[1], "gx", backward)
    other_outer = flip(own_outer_held, [("ma", 0)], sizes)

    inner = [(own_inner, other_inner, slopes_inner, inner_rows)]
    so_far = partial_tensor(cell_volumes, inner, sizes, (1, 2, 5, 6, 3, 7))
    columns, so_far = barrier((columns, so_far))
    outer = [(own_outer, other_outer, slopes_of(own, outer_rows, columns, above, below), outer_rows)]
    stages = stages_of(sizes)
    count = modes // BLOCKS
    cell_count = mode_fields.shape[2] * mode_fields.shape[3]
    flips = dict(subsets(stages[1]))
    sent = partial_tensor(cell_volumes, outer, sizes, (7,), so_far, 5, BF16)
    cell_volumes, sent = barrier((cell_volumes, sent))
    arrived = flip(sent, stages[0], sizes)
    kept = partial_tensor(cell_volumes, outer, sizes, (3,), so_far, 4)
    sent = term_sum([kept, arrived], 0, count).astype(BF16)
    cell_volumes, sent = barrier((cell_volumes, sent))
    both = flip(sent, flips[3], sizes)

    sent = partial_tensor(cell_volumes, outer, sizes, (5, 6), so_far, 2, BF16, cost=1)
    cell_volumes, sent = barrier((cell_volumes, sent))
    arrived = flip(sent, stages[0], sizes)
    kept = partial_tensor(cell_volumes, outer, sizes, (1, 2), so_far, 0, cost=1)
    sent = [term_sum([kept, arrived], at * count, (at + 1) * count).astype(BF16) for at in range(2)]
    cell_volumes, sent = barrier((cell_volumes, sent))
    received = [flip(sent[1], flips[2], sizes), flip(sent[0], flips[1], sizes)]

    sent = partial_tensor(cell_volumes, inner + outer, sizes, (4,), dtype=BF16, cost=1)
    cell_volumes, sent, both = barrier((cell_volumes, sent, both))
    arrived = flip(sent, stages[0], sizes)
    kept = partial_tensor(cell_volumes, inner + outer, sizes, (0,), cost=1)
    received.append(both)
    terms = [summed(received, count, 16 * count * modes * share * cell_count), kept, arrived]
    for stage in stages[2:-1]:
        terms = terms + exchange(stage, sends(terms, count, stage), sizes)
        count = count >> len(stage)
    return finish(terms, count, stages[-1], sizes)


def solution(mesh):
    in_specs = (P(None, "ma", "gx", "gy"), P("gx", "gy"))
    out_specs = P(("gx", "gy"), "ma", None)
    body = functools.partial(shards, sizes=dict(mesh.shape))
    return jax.shard_map(body, mesh=mesh, in_specs=in_specs, out_specs=out_specs, check_vma=False)
```
